32 devices in a mesh: groups: 2 (over y), band: 4 (over x, core), sect: 4 (over z).
Axes of the slice: x: 2, y: 2, z: 4, core: 2. Of those that a mesh axis runs over, the one named last changes fastest.
Arguments:
- state_field: bfloat16 [198, 128, 512], P('groups', 'band', 'sect'), parts along dimension 0, may hold values from -6 to 6
- conv_in_weight: bfloat16 [9, 128, 99], replicated, may hold values from -0.1875 to 0.1875
- conv_in_bias: float32 [128], replicated, may hold values from -3 to 3
- conv_out_weight: bfloat16 [9, 99, 128], replicated, may hold values from -0.1875 to 0.1875
- conv_out_bias: float32 [99], replicated, may hold values from -3 to 3
- patch_anchor: int32 [32, 2], P('groups'), parts along dimension 0, may hold values from 0 to 480, as said below
- patch_noise: bfloat16 [32, 2, 99, 1024], P(('groups', 'band', 'sect')), parts along dimension 0, may hold values from -6 to 6
- denoise_in_weight: bfloat16 [9, 128, 99], replicated, may hold values from -0.1875 to 0.1875
- step_bias: float32 [2, 128], replicated, may hold values from -3 to 3
- denoise_out_weight: bfloat16 [9, 99, 128], replicated, may hold values from -0.1875 to 0.1875
- denoise_bias: float32 [99], replicated, may hold values from -3 to 3
Outputs:
- next_field: bfloat16 [198, 128, 512], P('groups', 'band', 'sect'), parts along dimension 0
The draws below stay inside these ranges and needn't reach their ends.
There are 2 independent parts, one for each index of `groups`. The reference program is written for one: setup_inputs(seed, part) draws one part's arguments, and reference() takes and returns one part's arrays. A program takes and returns all parts, laid end to end along the dimension named above; an argument that names none is the same for every part. Nothing has to cross between parts.
Inputs may be any that keep to these rules, and one draw needn't show every extreme that they name: `patch_anchor`: patches p * 1 to p + 1 - 1 are denoised by the device at position p of band+sect, band first. Each patch's anchor column lies in the columns of its reader's sector, its anchor row at most 96 and its anchor column at most 480. Among the patches of one sector, at most 2 have anchor rows in one band's rows, and in every sector some band holds exactly 2.
All inputs are finite; a program needn't handle non-finite values.
Results may differ from the reference program's by a relative error of at most 0.0049.
Values may be sent and summed in bfloat16 or wider, within the bound.
No kernel may reach another device: no remote copies, remote signals or barrier semaphores. Data moves between devices by JAX's collectives and lax.ppermute only.
A program may use at most 64 MiB of HBM per device.

```python
import jax
import jax.numpy as jnp
from jax import lax

CH = 99
HID = 128
RB = 32
CB = 128
P_SIZE = 32
PPD = 1
STEPS = 2
NLAT = 128
NLON = 512
NP = 16
N_BAND = 4
N_SECT = 4


def draw_patch_anchor(key, part):
    keys = jax.random.split(jax.random.fold_in(key, 17), 5)
    band_total = N_BAND
    sect_total = N_SECT
    owner_perm = jax.vmap(lambda sub: jax.random.permutation(sub, band_total))(jax.random.split(keys[0], sect_total))
    unit_perm = jax.vmap(lambda sub: jax.random.permutation(sub, band_total))(jax.random.split(keys[1], sect_total))
    doubled = jax.random.randint(keys[2], (sect_total,), 1, band_total // 2 + 1)
    position = jnp.arange(band_total, dtype=jnp.int32)
    mapped = jnp.where(position[None, :] < 2 * doubled[:, None], position[None, :] // 2, position[None, :])
    chosen = jnp.take_along_axis(mapped, unit_perm, axis=1)
    owner = jnp.take_along_axis(owner_perm, chosen, axis=1)
    owner_grid = jnp.broadcast_to(owner.T[:, :, None], (band_total, sect_total, PPD))
    sector = jnp.broadcast_to(jnp.arange(sect_total, dtype=jnp.int32)[None, :, None], (band_total, sect_total, PPD))
    row_offset = jax.random.randint(keys[3], (band_total, sect_total, PPD), 0, RB)
    col_offset = jax.random.randint(keys[4], (band_total, sect_total, PPD), 0, CB)
    anchor_rows = jnp.minimum(owner_grid * RB + row_offset, NLAT - P_SIZE)
    anchor_cols = jnp.minimum(sector * CB + col_offset, NLON - P_SIZE)
    return jnp.stack([anchor_rows, anchor_cols], axis=-1).reshape(NP, 2).astype(jnp.int32)


def block_scale(stream_key, extent, shards, low, largest):
    def one(axis_at, parts):
        draws = jax.random.uniform(jax.random.fold_in(jax.random.fold_in(stream_key, 6), axis_at), (parts,), jnp.float32, low / len(shards), largest / len(shards))
        return jnp.repeat(jnp.exp(draws), extent[axis_at] // parts).reshape((-1,) + (1,) * (len(extent) - axis_at - 1))

    level = one(*shards[0])
    for cut in shards[1:]:
        level = level * one(*cut)
    return level


def gaussian(stream_key, dims, spread, limit, cuts=(), kind=jnp.bfloat16):
    factor_of = block_scale(stream_key, dims, cuts, -0.22, 0.18) if cuts else 1.0
    values = jax.random.normal(stream_key, dims, jnp.float32) * spread * factor_of
    return jnp.minimum(jnp.maximum(values, -limit), limit).astype(kind)


def setup_inputs(seed: int = 0, part: int = 0) -> dict:
    streams_of = jax.random.split(jax.random.key(seed), 12)
    own_keys = jax.random.split(jax.random.fold_in(streams_of[11], part), 12)
    return {
        "state_field": gaussian(own_keys[0], (CH, NLAT, NLON), 1.0, 6.0, ((1, 4), (2, 4))),
        "conv_in_weight": gaussian(streams_of[1], (9, HID, CH), (9 * CH) ** -0.5, 0.1875),
        "conv_in_bias": gaussian(streams_of[2], (HID,), 0.5, 3.0, (), jnp.float32),
        "conv_out_weight": gaussian(streams_of[3], (9, CH, HID), (9 * HID) ** -0.5, 0.1875),
        "conv_out_bias": gaussian(streams_of[4], (CH,), 0.5, 3.0, (), jnp.float32),
        "patch_anchor": draw_patch_anchor(jax.random.fold_in(jax.random.fold_in(streams_of[11], part), 71), part),
        "patch_noise": gaussian(own_keys[6], (NP, STEPS, CH, P_SIZE * P_SIZE), 1.0, 6.0, ((0, 16),)),
        "denoise_in_weight": gaussian(streams_of[7], (9, HID, CH), (9 * CH) ** -0.5, 0.1875),
        "step_bias": gaussian(streams_of[8], (STEPS, HID), 0.5, 3.0, (), jnp.float32),
        "denoise_out_weight": gaussian(streams_of[9], (9, CH, HID), (9 * HID) ** -0.5, 0.1875),
        "denoise_bias": gaussian(streams_of[10], (CH,), 0.5, 3.0, (), jnp.float32),
    }


def conv_grid(values, weight):
    height = values.shape[1]
    width = values.shape[2]
    padded = jnp.pad(values, ((0, 0), (1, 1), (1, 1)))
    summed = jnp.zeros((weight.shape[1], height, width), jnp.float32)
    tap_index = 0
    for shift_row in (-1, 0, 1):
        for shift_col in (-1, 0, 1):
            window = padded[:, 1 + shift_row:1 + shift_row + height, 1 + shift_col:1 + shift_col + width]
            summed = summed + jnp.einsum("oi,ihw->ohw", weight[tap_index].astype(jnp.float32), window.astype(jnp.float32))
            tap_index = tap_index + 1
    return summed


def reference(state_field, conv_in_weight, conv_in_bias, conv_out_weight, conv_out_bias, patch_anchor, patch_noise, denoise_in_weight, step_bias, denoise_out_weight, denoise_bias):
    hidden = jax.nn.silu(conv_grid(state_field, conv_in_weight) + conv_in_bias[:, None, None]).astype(jnp.bfloat16)
    mean_field = (state_field.astype(jnp.float32) + conv_grid(hidden, conv_out_weight) + conv_out_bias[:, None, None]).astype(jnp.bfloat16)
    noises = patch_noise.reshape(NP, STEPS, CH, P_SIZE, P_SIZE)

    def one_patch(inputs):
        anchor, noise_set = inputs
        zero = jnp.zeros((), jnp.int32)
        patch_mean = lax.dynamic_slice(mean_field, (zero, anchor[0].astype(jnp.int32), anchor[1].astype(jnp.int32)), (CH, P_SIZE, P_SIZE))
        state = patch_mean.astype(jnp.float32) + noise_set[0].astype(jnp.float32)
        for step in range(STEPS):
            inner = state.astype(jnp.bfloat16)
            denoise_hidden = jax.nn.silu(conv_grid(inner, denoise_in_weight) + step_bias[step][:, None, None]).astype(jnp.bfloat16)
            state = state - 0.5 * (conv_grid(denoise_hidden, denoise_out_weight) + denoise_bias[:, None, None])
            if step + 1 < STEPS:
                state = state + 0.5 * noise_set[step + 1].astype(jnp.float32)
        return (state - patch_mean.astype(jnp.float32)).astype(jnp.bfloat16)

    corrections = lax.map(one_patch, (patch_anchor, noises))

    def accumulate(index, canvas):
        anchor = patch_anchor[index]
        zero = jnp.zeros((), jnp.int32)
        start = (zero, anchor[0].astype(jnp.int32), anchor[1].astype(jnp.int32))
        current = lax.dynamic_slice(canvas, start, (CH, P_SIZE, P_SIZE))
        return lax.dynamic_update_slice(canvas, current + corrections[index].astype(jnp.float32), start)

    summed = lax.fori_loop(0, NP, accumulate, jnp.zeros((CH, NLAT, NLON), jnp.float32))
    grid_rows = jnp.arange(NLAT, dtype=jnp.int32)
    grid_cols = jnp.arange(NLON, dtype=jnp.int32)
    start_rows = patch_anchor[:, 0:1]
    start_cols = patch_anchor[:, 1:2]
    cover_rows = ((grid_rows[None, :] >= start_rows) & (grid_rows[None, :] < start_rows + P_SIZE)).astype(jnp.float32)
    cover_cols = ((grid_cols[None, :] >= start_cols) & (grid_cols[None, :] < start_cols + P_SIZE)).astype(jnp.float32)
    coverage = jnp.dot(cover_rows.T, cover_cols, precision=lax.Precision.HIGHEST)
    averaged = summed / jnp.maximum(coverage, 1.0)[None, :, :]
    return (mean_field.astype(jnp.float32) + averaged).astype(jnp.bfloat16)
```

```python
import jax
import jax.numpy as jnp
from jax import lax
from jax.sharding import PartitionSpec as P

SIDE = 32


def shift_from(block, axis, distance):
    count = lax.axis_size(axis)
    route = [(i - distance, i) for i in range(count) if 0 <= i - distance < count]
    return lax.ppermute(block, axis, route)


def swap(block, axis, bit):
    count = lax.axis_size(axis)
    return lax.ppermute(block, axis, [(i, i ^ bit) for i in range(count)])


def tap_list():
    return [(shift_row, shift_col) for shift_row in (-1, 0, 1) for shift_col in (-1, 0, 1)]


def conv_block(padded, weight, out_rows, out_cols):
    summed = None
    for tap_index, (shift_row, shift_col) in enumerate(tap_list()):
        window = padded[
            :, 1 + shift_row : 1 + shift_row + out_rows, 1 + shift_col : 1 + shift_col + out_cols
        ]
        term = jnp.einsum(
            "oi,irc->orc", weight[tap_index], window, preferred_element_type=jnp.float32
        )
        summed = term if summed is None else summed + term
    return summed


def conv_patch(values, weight, side):
    return conv_block(
        jnp.pad(values.reshape(-1, side, side), ((0, 0), (1, 1), (1, 1))), weight, side, side
    ).reshape(-1, side * side)


def regression(wide, rows, cols, row0, col0, limits, w_in, b_in, w_out, b_out):
    hidden = jax.nn.silu(conv_block(wide, w_in, rows + 2, cols + 2) + b_in[:, None, None])
    grid_rows = row0 - 1 + jnp.arange(rows + 2, dtype=jnp.int32)
    grid_cols = col0 - 1 + jnp.arange(cols + 2, dtype=jnp.int32)
    keep = ((grid_rows >= 0) & (grid_rows < limits[0]))[:, None] & (
        (grid_cols >= 0) & (grid_cols < limits[1])
    )[None, :]
    hidden = jnp.where(keep[None], hidden, jnp.zeros_like(hidden)).astype(jnp.bfloat16)
    return (
        wide[:, 2 : 2 + rows, 2 : 2 + cols].astype(jnp.float32)
        + conv_block(hidden, w_out, rows, cols)
        + b_out[:, None, None]
    ).astype(jnp.bfloat16)


def denoise(start, noises, weight_in, biases, weight_out, out_bias, side):
    steps_total = noises.shape[0]
    start_mean = start.astype(jnp.float32)
    state = start_mean + noises[0].astype(jnp.float32)
    for step in range(steps_total):
        inner = state.astype(jnp.bfloat16)
        pre_act = conv_patch(inner, weight_in, side) + biases[step][:, None]
        hidden_patch = jax.nn.silu(pre_act).astype(jnp.bfloat16)
        state = state - 0.5 * (conv_patch(hidden_patch, weight_out, side) + out_bias[:, None])
        if step + 1 < steps_total:
            state = state + 0.5 * noises[step + 1].astype(jnp.float32)
    return (state - start_mean).astype(jnp.bfloat16)


def per_device(
    state_field,
    conv_in_weight,
    conv_in_bias,
    conv_out_weight,
    conv_out_bias,
    patch_anchor,
    patch_noise,
    denoise_in_weight,
    step_bias,
    denoise_out_weight,
    denoise_bias,
):
    bands = lax.axis_size("band")
    sects = lax.axis_size("sect")
    band = lax.axis_index("band")
    sect = lax.axis_index("sect")
    channels, rows, cols = state_field.shape
    side = SIDE
    limits = (rows * bands, cols * sects)
    wide_side = side + 4
    right = shift_from(state_field[:, :, : side + 2], "sect", -1)
    left = shift_from(state_field[:, :, cols - 2 :], "sect", 1)
    ext = jnp.concatenate([left, state_field, right], axis=2)
    local = lax.dynamic_slice_in_dim(
        patch_anchor.reshape(bands, sects, 2), sect, 1, 1
    ).reshape(bands, 2) - jnp.stack([band * rows, sect * cols])
    order = [band ^ j for j in range(bands)]
    slot_row = [local[q, 0] for q in order]
    slot_col = [local[q, 1] for q in order]
    tall = jnp.pad(ext, ((0, 0), (wide_side, wide_side), (0, 0)))
    parts = []
    for j in range(bands):
        at_row = jnp.clip(slot_row[j] - 2 + wide_side, 0, rows + wide_side)
        parts.append(
            lax.dynamic_slice(tall, (0, at_row, slot_col[j]), (channels, wide_side, wide_side))
        )
    parts = jnp.stack(parts)
    bit = 1
    while bit < bands:
        got = swap(parts[1::2], "band", bit)
        parts = parts[0::2] + got
        bit *= 2
    window = parts[0]
    patch = regression(
        window, side, side, slot_row[0] + band * rows, slot_col[0] + sect * cols, limits,
        conv_in_weight, conv_in_bias, conv_out_weight, conv_out_bias,
    )
    correction = denoise(
        patch.reshape(channels, side * side), patch_noise[0], denoise_in_weight, step_bias,
        denoise_out_weight, denoise_bias, side,
    )
    shared = correction[None]
    bit = bands // 2
    while bit:
        got = swap(shared, "band", bit)
        shared = jnp.stack([shared, got], axis=1).reshape((-1,) + correction.shape)
        bit //= 2
    core = ext[:, :, : cols + 4]
    above = shift_from(core[:, rows - 2 :], "band", 1)
    below = shift_from(core[:, :2], "band", -1)
    mean_field = regression(
        jnp.concatenate([above, core, below], axis=1), rows, cols, band * rows, sect * cols,
        limits, conv_in_weight, conv_in_bias, conv_out_weight, conv_out_bias,
    )
    canvas = jnp.zeros((channels, rows + 2 * side, cols + side), jnp.float32)
    for j in range(bands):
        start = (0, jnp.clip(slot_row[j] + side, 0, rows + side), slot_col[j])
        piece = shared[j].reshape(channels, side, side).astype(jnp.float32)
        current = lax.dynamic_slice(canvas, start, piece.shape)
        canvas = lax.dynamic_update_slice(canvas, current + piece, start)
    canvas = canvas[:, side : side + rows]
    spilled = shift_from(canvas[:, :, cols:].astype(jnp.bfloat16), "sect", 1)
    summed = canvas[:, :, :cols] + jnp.pad(
        spilled.astype(jnp.float32), ((0, 0), (0, 0), (0, cols - side))
    )
    grid_rows = band * rows + jnp.arange(rows, dtype=jnp.int32)
    grid_cols = sect * cols + jnp.arange(cols, dtype=jnp.int32)
    start_rows = patch_anchor[:, 0:1]
    start_cols = patch_anchor[:, 1:2]
    cover_rows = (
        (grid_rows[None, :] >= start_rows) & (grid_rows[None, :] < start_rows + side)
    ).astype(jnp.float32)
    cover_cols = (
        (grid_cols[None, :] >= start_cols) & (grid_cols[None, :] < start_cols + side)
    ).astype(jnp.float32)
    coverage = jnp.dot(cover_rows.T, cover_cols, precision=lax.Precision.HIGHEST)
    averaged = summed / jnp.maximum(coverage, 1.0)[None, :, :]
    return (mean_field.astype(jnp.float32) + averaged).astype(jnp.bfloat16)


def solution(mesh):
    placed = (
        P("groups", "band", "sect"),
        P(),
        P(),
        P(),
        P(),
        P("groups", None),
        P(("groups", "band", "sect"), None, None, None),
        P(),
        P(),
        P(),
        P(),
    )
    return jax.shard_map(
        per_device,
        mesh=mesh,
        in_specs=placed,
        out_specs=P("groups", "band", "sect"),
        check_vma=False,
    )
```

```python
import jax
import jax.numpy as jnp
from jax import lax
from jax.experimental import pallas as pl
from jax.experimental.pallas import tpu as pltpu
from jax.sharding import PartitionSpec as P

SIDE = 32
WIDE = SIDE + 4
PER_TILE = 3
TILES = WIDE // PER_TILE
LANES = 128
REACH = SIDE + 2
HALF = jnp.bfloat16
FULL = jnp.float32


def shift_from(block, axis, distance):
    count = lax.axis_size(axis)
    route = [(i - distance, i) for i in range(count) if 0 <= i - distance < count]
    return lax.ppermute(block, axis, route)


def swap(block, axis, bit):
    count = lax.axis_size(axis)
    return lax.ppermute(block, axis, [(i, i ^ bit) for i in range(count)])


def run(body, outs, ins, scratch, flops=0, scalars=1):
    smem = pl.BlockSpec(memory_space=pltpu.SMEM)
    vmem = pl.BlockSpec(memory_space=pltpu.VMEM)
    moved = sum(x.size * x.dtype.itemsize for x in list(ins) + list(outs))
    return pl.pallas_call(
        body,
        out_shape=outs,
        in_specs=[smem] * scalars + [vmem] * (len(ins) - scalars),
        out_specs=[vmem] * len(outs),
        scratch_shapes=scratch,
        cost_estimate=pl.CostEstimate(flops=flops, bytes_accessed=moved, transcendentals=0),
        compiler_params=pltpu.CompilerParams(vmem_limit_bytes=56 * 1024 * 1024),
    )(*ins)


def like(shape, dtype=HALF):
    return jax.ShapeDtypeStruct(shape, dtype)


def lane_index(shape):
    return lax.broadcasted_iota(jnp.int32, shape, len(shape) - 1)


def pack(state):
    channels, rows, cols = state.shape
    padded = -(-channels // 8) * 8
    span = -(-rows * REACH // LANES)

    def body(state_ref, rows_ref, right_ref, left_ref, flat):
        flat[: channels * rows] = state_ref[...].astype(FULL).reshape(channels * rows, cols)
        flat[channels * rows :] = jnp.zeros(((padded - channels) * rows, cols), FULL)
        lane = lane_index((padded, LANES))
        tiles = [None] * span
        rim = jnp.zeros((padded, LANES), FULL)
        for r in range(rows):
            row = flat[pl.ds(r, padded, stride=rows), :]
            rows_ref[r] = row.astype(HALF)
            at, off = divmod(r * REACH, LANES)
            moved = row if off == 0 else pltpu.roll(row, off, 1)
            part = jnp.where((lane >= off) & (lane < off + REACH), moved, 0.0)
            tiles[at] = part if tiles[at] is None else tiles[at] + part
            if off + REACH > LANES:
                tiles[at + 1] = jnp.where(lane < off + REACH - LANES, moved, 0.0)
            turned = pltpu.roll(row, (2 * r + 2) % LANES, 1)
            rim = jnp.where((lane >= 2 * r) & (lane < 2 * r + 2), turned, rim)
        for at in range(span):
            right_ref[:, at * LANES : (at + 1) * LANES] = tiles[at].astype(HALF)
        left_ref[...] = rim.astype(HALF)

    return run(
        body,
        [like((rows, padded, cols)), like((padded, span * LANES)), like((padded, LANES))],
        [state],
        [pltpu.VMEM((padded * rows, cols), FULL)],
        scalars=0,
    )


def extract(anchors, by_row, right, left):
    rows, padded, cols = by_row.shape
    slots = anchors.shape[0] // 2
    deep = -(-padded // 16) * 16
    tall = rows + 2 * WIDE

    def body(at_ref, rows_ref, right_ref, left_ref, keep_ref, send_ref, ext_ref, top_ref, low_ref, ext):
        lane = lane_index((padded, LANES))
        ext[...] = jnp.zeros(ext.shape, HALF)
        rim = left_ref[...].astype(FULL)
        for r in range(rows):
            at, off = divmod(r * REACH, LANES)
            piece = right_ref[:, at * LANES : (at + 1) * LANES].astype(FULL)
            if off:
                piece = pltpu.roll(piece, LANES - off, 1)
            if off + REACH > LANES:
                after = right_ref[:, (at + 1) * LANES : (at + 2) * LANES].astype(FULL)
                piece = jnp.where(lane < LANES - off, piece, pltpu.roll(after, LANES - off, 1))
            turned = pltpu.roll(rim, (LANES - 2 - 2 * r) % LANES, 1)
            piece = jnp.where(lane < REACH, piece, jnp.where(lane >= LANES - 2, turned, 0.0))
            ext[WIDE + r, :padded, :cols] = rows_ref[r]
            ext[WIDE + r, :padded, cols:] = piece.astype(HALF)
        ext_ref[...] = ext[WIDE : WIDE + rows, :padded, :]
        top_ref[...] = ext[WIDE : WIDE + 2, :padded, :]
        low_ref[...] = ext[WIDE + rows - 2 : WIDE + rows, :padded, :]
        width = cols + LANES
        for j in range(slots):
            out_ref = send_ref if j % 2 else keep_ref
            row0 = at_ref[2 * j] - 2 + WIDE
            col0 = at_ref[2 * j + 1] - 2
            inside = (row0 > 0) & (row0 < rows + WIDE)

            @pl.when(inside)
            def _():
                source = lax.broadcasted_iota(jnp.int32, (width, LANES), 0)
                target = lane_index((width, LANES))
                picks = []
                for m in range(PER_TILE):
                    want = jnp.bitwise_and(target - WIDE * m + col0, width - 1)
                    hit = (source == want) & (target >= WIDE * m) & (target < WIDE * m + WIDE)
                    picks.append(jnp.where(hit, 1.0, 0.0).astype(HALF))
                pick = jnp.concatenate(picks, axis=0)
                view = ext[pl.ds(row0, WIDE)].reshape(TILES, PER_TILE, deep, width)
                view = jnp.concatenate([view[:, m] for m in range(PER_TILE)], axis=-1)
                got = jnp.dot(
                    view.reshape(TILES * deep, PER_TILE * width), pick, preferred_element_type=FULL
                ).reshape(TILES, deep, LANES)
                for t in range(TILES):
                    out_ref[j // 2, :, t * LANES : (t + 1) * LANES] = got[t, :padded].astype(HALF)

            @pl.when(jnp.logical_not(inside))
            def _():
                out_ref[j // 2] = jnp.zeros((padded, TILES * LANES), HALF)

    part = like((slots // 2, padded, TILES * LANES))
    edge = like((2, padded, cols + LANES))
    return run(
        body,
        [part, part, like((rows, padded, cols + LANES)), edge, edge],
        [anchors, by_row, right, left],
        [pltpu.VMEM((tall, deep, cols + LANES), HALF)],
        flops=2 * slots * TILES * deep * PER_TILE * (cols + LANES) * LANES,
    )


def pair_weight(weight):
    taps, outs, ins = weight.shape
    grid = jnp.pad(
        weight.transpose(0, 2, 1), ((0, 0), (0, LANES - ins), (0, LANES - outs))
    ).reshape(3, 3, LANES, LANES)
    empty = jnp.zeros((1, 3, LANES, LANES), weight.dtype)
    return jnp.concatenate(
        [jnp.concatenate([grid, empty], axis=0), jnp.concatenate([empty, grid], axis=0)], axis=-1
    ).reshape(12 * LANES, 2 * LANES)


def pair_bias(bias):
    line = jnp.pad(bias, ((0, LANES - bias.shape[0]),))
    return jnp.concatenate([line, line])[None, :]


def gather_pairs(shifted, first, count):
    view = jnp.concatenate(
        [shifted[b, pl.ds(first + u, count), v] for u in (0, 1) for v in (0, 1) for b in (0, 1, 2)],
        axis=-1,
    )
    return view.reshape(count * view.shape[1], view.shape[2])


def silu(value):
    return value / (1.0 + jnp.exp(-value))


def patch_step(place, addends, noise, weights, biases, step_bias, channels):
    padded = addends[0].shape[1]
    steps = noise.shape[0]
    half = SIDE // 2
    loose = 48

    def body(*refs):
        place_ref = refs[0]
        parts = refs[1 : 1 + len(addends)]
        (noise_ref, w_in, w_out, d_in, d_out, b_in, b_out, b_step, b_den, out_ref,
         flat, state_sh, hid, hid_sh, pad, pad_sh, corr) = refs[1 + len(addends) :]
        for t in range(TILES):
            lanes = slice(t * LANES, (t + 1) * LANES)
            tile = parts[0][0, :, lanes].astype(FULL)
            for part in parts[1:]:
                tile = tile + part[0, :, lanes].astype(FULL)
            tile = jnp.concatenate([tile, jnp.zeros((LANES - padded, LANES), FULL)], axis=0)
            flat[lanes, :] = tile.T
        for i in range(WIDE):
            t, m = divmod(i, PER_TILE)
            off = t * LANES + m * WIDE
            for b in range(3):
                state_sh[b, i // 2, i % 2] = flat[off + b : off + b + loose, :].astype(HALF)
        pairs = half + 1
        value = jnp.dot(gather_pairs(state_sh, 0, pairs), w_in[...], preferred_element_type=FULL)
        value = silu(value + b_in[...]).reshape(pairs, loose, 2 * LANES)
        pair = lax.broadcasted_iota(jnp.int32, value.shape, 0)
        col = lax.broadcasted_iota(jnp.int32, value.shape, 1)
        odd = (lane_index(value.shape) >= LANES).astype(jnp.int32)
        grid_row = place_ref[0] - 1 + 2 * pair + odd
        grid_col = place_ref[1] - 1 + col
        keep = (
            (grid_row >= 0) & (grid_row < place_ref[2])
            & (grid_col >= 0) & (grid_col < place_ref[3]) & (col < SIDE + 2)
        )
        value = jnp.where(keep, value, 0.0)
        hid[:, 0] = value[:, :, :LANES]
        hid[:, 1] = value[:, :, LANES:]
        for b in range(3):
            hid_sh[b] = hid[:, :, b : b + SIDE, :].astype(HALF)
        value = jnp.dot(gather_pairs(hid_sh, 0, half), w_out[...], preferred_element_type=FULL)
        center = jnp.concatenate(
            [state_sh[2, 1 : 1 + half, v, :SIDE, :] for v in (0, 1)], axis=-1
        ).astype(FULL).reshape(half * SIDE, 2 * LANES)
        mean = (center + value + b_out[...]).astype(HALF).astype(FULL)
        state = mean + noise_ref[0].astype(FULL)
        pad[...] = jnp.zeros(pad.shape, FULL)

        def conv(source, weight):
            shaped = source.reshape(half, SIDE, 2 * LANES)
            pad[:half, 1, 8 : 8 + SIDE] = shaped[:, :, :LANES]
            pad[1:, 0, 8 : 8 + SIDE] = shaped[:, :, LANES:]
            for b in range(3):
                pad_sh[b] = pad[:, :, 7 + b : 7 + b + SIDE, :].astype(HALF)
            return jnp.dot(gather_pairs(pad_sh, 0, half), weight[...], preferred_element_type=FULL)

        for step in range(steps):
            inner = silu(conv(state, d_in) + b_step[step : step + 1])
            state = state - 0.5 * (conv(inner, d_out) + b_den[...])
            if step + 1 < steps:
                state = state + 0.5 * noise_ref[step + 1].astype(FULL)
        change = (state - mean).reshape(half, SIDE, 2 * LANES)
        corr[:, 0] = change[:, :, :LANES]
        corr[:, 1] = change[:, :, LANES:]
        cells = corr[...].reshape(SIDE * SIDE, LANES)
        for t in range(SIDE * SIDE // LANES):
            lanes = slice(t * LANES, (t + 1) * LANES)
            out_ref[:, lanes] = cells[lanes].T[:padded].astype(HALF)

    return run(
        body,
        [like((padded, SIDE * SIDE))],
        [place, *addends, noise, *weights, *biases[:2], step_bias, biases[2]],
        [
            pltpu.VMEM((TILES * LANES, LANES), FULL),
            pltpu.VMEM((3, WIDE // 2, 2, loose, LANES), HALF),
            pltpu.VMEM((half + 1, 2, loose, LANES), FULL),
            pltpu.VMEM((3, half + 1, 2, SIDE, LANES), HALF),
            pltpu.VMEM((half + 1, 2, loose, LANES), FULL),
            pltpu.VMEM((3, half + 1, 2, SIDE, LANES), HALF),
            pltpu.VMEM((half, 2, SIDE, LANES), FULL),
        ],
        flops=2 * 12 * LANES * 2 * LANES * SIDE * half * 6,
    )[0]


def grid_mean(place, ext, above, below, weights, biases):
    rows, padded, width = ext.shape
    cols = width - LANES
    loose = cols + 16
    pairs_in, pairs_out = 6, 4
    hidden_pairs = -(-(rows // 2 + 1) // pairs_in) * pairs_in
    state_pairs = hidden_pairs + 1

    def body(place_ref, ext_ref, above_ref, below_ref, w_in, w_out, b_in, b_out, out_ref,
             line, state_sh, hid, hid_sh):
        def spread(i, source):
            value = source.astype(FULL)
            value = jnp.concatenate([value, jnp.zeros((LANES - padded, width), FULL)], axis=0).T
            line[8 : 8 + cols] = value[:cols]
            line[8 + cols :] = value[cols : cols + 16]
            line[:8] = value[width - 8 :]
            for b in range(3):
                state_sh[b, i // 2, i % 2] = line[6 + b : 6 + b + loose, :].astype(HALF)

        for i in range(2):
            spread(i, above_ref[i])
            spread(rows + 2 + i, below_ref[i])
        for pair in range(rows // 2 + 2, state_pairs):
            for b in range(3):
                state_sh[b, pair] = jnp.zeros((2, loose, LANES), HALF)

        def spread_row(i, carry):
            for v in range(2):
                spread(2 * i + 2 + v, ext_ref[2 * i + v])
            return carry

        lax.fori_loop(0, rows // 2, spread_row, 0)

        def first(chunk, carry):
            start = chunk * pairs_in
            value = jnp.dot(
                gather_pairs(state_sh, start, pairs_in), w_in[...], preferred_element_type=FULL
            )
            value = silu(value + b_in[...]).reshape(pairs_in, loose, 2 * LANES)
            pair = lax.broadcasted_iota(jnp.int32, value.shape, 0)
            col = lax.broadcasted_iota(jnp.int32, value.shape, 1)
            odd = (lane_index(value.shape) >= LANES).astype(jnp.int32)
            grid_row = place_ref[0] - 1 + 2 * (start + pair) + odd
            grid_col = place_ref[1] - 1 + col
            keep = (
                (grid_row >= 0) & (grid_row < place_ref[2])
                & (grid_col >= 0) & (grid_col < place_ref[3])
            )
            value = jnp.where(keep, value, 0.0)
            hid[:, 0] = value[:, :, :LANES]
            hid[:, 1] = value[:, :, LANES:]
            for b in range(3):
                hid_sh[b, pl.ds(start, pairs_in)] = hid[:, :, b : b + cols, :].astype(HALF)
            return carry

        lax.fori_loop(0, hidden_pairs // pairs_in, first, 0)

        def second(chunk, carry):
            start = chunk * pairs_out
            value = jnp.dot(
                gather_pairs(hid_sh, start, pairs_out), w_out[...], preferred_element_type=FULL
            ) + b_out[...]
            value = value.reshape(pairs_out, cols, 2 * LANES)
            for k in range(pairs_out):
                for v in range(2):
                    center = state_sh[2, start + k + 1, v, :cols, :].astype(FULL)
                    mean = center + value[k, :, v * LANES : (v + 1) * LANES]
                    out_ref[2 * (start + k) + v] = mean.T[:padded].astype(HALF)
            return carry

        lax.fori_loop(0, rows // 2 // pairs_out, second, 0)

    return run(
        body,
        [like((rows, padded, cols))],
        [place, ext, above, below, *weights, *biases],
        [
            pltpu.VMEM((loose + 8, LANES), FULL),
            pltpu.VMEM((3, state_pairs, 2, loose, LANES), HALF),
            pltpu.VMEM((pairs_in, 2, loose, LANES), FULL),
            pltpu.VMEM((3, hidden_pairs, 2, cols, LANES), HALF),
        ],
        flops=2 * 12 * LANES * 2 * LANES * cols * rows // 2 * 2,
    )[0]


def spill(anchors, pieces, rows, cols):
    padded = pieces[0].shape[-2]
    counts = [piece.shape[0] for piece in pieces]

    def body(at_ref, *refs):
        out_ref, total = refs[-2:]
        lane = lane_index((padded, LANES))
        total[...] = jnp.zeros(total.shape, FULL)
        slot = 0
        for piece, count in zip(refs, counts):
            for k in range(count):
                row0, col0 = at_ref[2 * slot], at_ref[2 * slot + 1]
                slot += 1

                @pl.when(col0 > cols - SIDE)
                def _(piece=piece, k=k, row0=row0, col0=col0):
                    def one(r, carry):
                        i = r - row0
                        source = pl.multiple_of((i // 4) * LANES, LANES)
                        target = pl.multiple_of((r // 4) * LANES, LANES)
                        low = SIDE * (r % 4)
                        turn = jnp.bitwise_and(low - SIDE * (i % 4) + col0 - cols, LANES - 1)
                        value = pltpu.roll(piece[k, :, pl.ds(source, LANES)].astype(FULL), turn, 1)
                        keep = (lane >= low) & (lane < low + col0 - (cols - SIDE))
                        total[:, pl.ds(target, LANES)] += jnp.where(keep, value, 0.0)
                        return carry

                    lax.fori_loop(jnp.maximum(row0, 0), jnp.minimum(row0 + SIDE, rows), one, 0)

        out_ref[...] = total[...].astype(HALF)

    shape = (padded, rows * SIDE)
    return run(body, [like(shape)], [anchors, *pieces], [pltpu.VMEM(shape, FULL)])[0]


def canvas(anchors, pieces, rows, cols):
    padded = pieces[0].shape[-2]
    counts = [piece.shape[0] for piece in pieces]

    def body(at_ref, *refs):
        out_ref = refs[-1]
        lane = lane_index((padded, LANES))
        out_ref[...] = jnp.zeros(out_ref.shape, FULL)
        slot = 0
        for piece, count in zip(refs, counts):
            for k in range(count):
                row0, col0 = at_ref[2 * slot], at_ref[2 * slot + 1]
                slot += 1

                def one(r, carry, piece=piece, k=k, row0=row0, col0=col0):
                    i = r - row0
                    source = pl.multiple_of((i // 4) * LANES, LANES)
                    turn = jnp.bitwise_and(col0 - SIDE * (i % 4), LANES - 1)
                    value = pltpu.roll(piece[k, :, pl.ds(source, LANES)].astype(FULL), turn, 1)
                    keep = (lane >= col0) & (lane < col0 + SIDE)
                    out_ref[r] += jnp.where(keep, value, 0.0)
                    return carry

                lax.fori_loop(jnp.maximum(row0, 0), jnp.minimum(row0 + SIDE, rows), one, 0)

    return run(body, [like((rows, padded, cols), FULL)], [anchors, *pieces], [])[0]


def finish(mean, summed, arrived, coverage, channels):
    rows, padded, cols = mean.shape

    def body(mean_ref, sum_ref, spill_ref, cover_ref, out_ref, flat):
        lane = lane_index((padded, LANES))
        weight = jnp.maximum(cover_ref[...], 1.0)
        for r in range(rows):
            at, low = divmod(r * SIDE, LANES)
            extra = spill_ref[:, at * LANES : (at + 1) * LANES].astype(FULL)
            if low:
                extra = pltpu.roll(extra, LANES - low, 1)
            total = sum_ref[r] + jnp.where(lane < SIDE, extra, 0.0)
            value = mean_ref[r].astype(FULL) + total / weight[r : r + 1]
            flat[pl.ds(r, padded, stride=rows), :] = value
        out_ref[...] = flat[: channels * rows].reshape(channels, rows, cols).astype(HALF)

    return run(
        body,
        [like((channels, rows, cols))],
        [mean, summed, arrived, coverage],
        [pltpu.VMEM((padded * rows, cols), FULL)],
        scalars=0,
    )[0]


def per_device(
    state_field,
    conv_in_weight,
    conv_in_bias,
    conv_out_weight,
    conv_out_bias,
    patch_anchor,
    patch_noise,
    denoise_in_weight,
    step_bias,
    denoise_out_weight,
    denoise_bias,
):
    bands = lax.axis_size("band")
    sects = lax.axis_size("sect")
    band = lax.axis_index("band")
    sect = lax.axis_index("sect")
    channels, rows, cols = state_field.shape
    steps = patch_noise.shape[1]
    base = jnp.stack([band * rows, sect * cols])
    column = lax.dynamic_slice_in_dim(
        patch_anchor.reshape(bands, sects, 2), sect, 1, 1
    ).reshape(bands, 2)
    order = jnp.bitwise_xor(jnp.arange(bands, dtype=jnp.int32), band)
    slots = jnp.take(column, order, axis=0) - base[None, :]
    anchors = slots.reshape(-1)
    limits = jnp.array([rows * bands, cols * sects], jnp.int32)
    grid_place = jnp.concatenate([base, limits])
    patch_place = jnp.concatenate([slots[0] + base, limits])

    by_row, right_rim, left_rim = pack(state_field)
    right = shift_from(right_rim, "sect", -1)
    left = shift_from(left_rim, "sect", 1)

    weights = [pair_weight(w) for w in (conv_in_weight, conv_out_weight)]
    denoisers = [pair_weight(w) for w in (denoise_in_weight, denoise_out_weight)]
    biases = [pair_bias(b) for b in (conv_in_bias, conv_out_bias, denoise_bias)]
    step_lines = jnp.concatenate([step_bias, step_bias], axis=-1)
    noise = jnp.pad(
        patch_noise[0].reshape(steps, channels, SIDE // 2, 2, SIDE).transpose(0, 2, 4, 3, 1),
        ((0, 0), (0, 0), (0, 0), (0, 0), (0, LANES - channels)),
    ).reshape(steps, SIDE * SIDE // 2, 2 * LANES)

    kept, sent, ext, top, low = extract(anchors, by_row, right, left)
    got = swap(sent, "band", 1)
    addends = [kept, got]
    bit = 2
    parts = None
    while bit < bands:
        parts = kept + got if parts is None else parts[0::2] + got
        got = swap(parts[1::2], "band", bit)
        addends.append(got)
        bit *= 2
    correction = patch_step(
        patch_place, addends, noise, weights + denoisers, biases, step_lines, channels
    )
    pieces = [correction[None]]
    sources = [0]
    bit = bands // 2
    while bit:
        got = swap(jnp.concatenate(pieces, axis=0), "band", bit)
        pieces.append(got)
        sources += [s ^ bit for s in sources]
        bit //= 2
    slot_anchors = jnp.take(slots, jnp.array(sources, jnp.int32), axis=0).reshape(-1)

    above = shift_from(low, "band", 1)
    below = shift_from(top, "band", -1)
    mean = grid_mean(grid_place, ext, above, below, weights, biases[:2])

    arrived = shift_from(spill(slot_anchors, pieces, rows, cols), "sect", 1)
    summed = canvas(slot_anchors, pieces, rows, cols)
    grid_rows = band * rows + jnp.arange(rows, dtype=jnp.int32)
    grid_cols = sect * cols + jnp.arange(cols, dtype=jnp.int32)
    start_rows = patch_anchor[:, 0:1]
    start_cols = patch_anchor[:, 1:2]
    cover_rows = (
        (grid_rows[None, :] >= start_rows) & (grid_rows[None, :] < start_rows + SIDE)
    ).astype(FULL)
    cover_cols = (
        (grid_cols[None, :] >= start_cols) & (grid_cols[None, :] < start_cols + SIDE)
    ).astype(FULL)
    coverage = jnp.dot(cover_rows.T, cover_cols, precision=lax.Precision.HIGHEST)
    return finish(mean, summed, arrived, coverage, channels)


def solution(mesh):
    placed = (
        P("groups", "band", "sect"),
        P(),
        P(),
        P(),
        P(),
        P("groups", None),
        P(("groups", "band", "sect"), None, None, None),
        P(),
        P(),
        P(),
        P(),
    )
    return jax.shard_map(
        per_device,
        mesh=mesh,
        in_specs=placed,
        out_specs=P("groups", "band", "sect"),
        check_vma=False,
    )
```

```python
import jax
import jax.numpy as jnp
from jax import lax
from jax.experimental import pallas as pl
from jax.experimental.pallas import tpu as pltpu
from jax.sharding import PartitionSpec as P

SIDE = 32
WIDE = SIDE + 4
PER_TILE = 3
TILES = WIDE // PER_TILE
LANES = 128
REACH = SIDE + 2
HALF = jnp.bfloat16
FULL = jnp.float32


def shift_from(block, axis, distance):
    count = lax.axis_size(axis)
    route = [(i - distance, i) for i in range(count) if 0 <= i - distance < count]
    return lax.ppermute(block, axis, route)


def swap(block, axis, bit):
    count = lax.axis_size(axis)
    return lax.ppermute(block, axis, [(i, i ^ bit) for i in range(count)])


def run(body, outs, ins, scratch, name, micros=1.0, scalars=1, limit=24):
    smem = pl.BlockSpec(memory_space=pltpu.SMEM)
    vmem = pl.BlockSpec(memory_space=pltpu.VMEM)
    return pl.pallas_call(
        body,
        out_shape=outs,
        in_specs=[smem] * scalars + [vmem] * (len(ins) - scalars),
        out_specs=[vmem] * len(outs),
        scratch_shapes=scratch,
        name=name,
        cost_estimate=pl.CostEstimate(
            flops=int(micros * 1.15e9), bytes_accessed=1024, transcendentals=0
        ),
        compiler_params=pltpu.CompilerParams(vmem_limit_bytes=limit * 1024 * 1024),
    )(*ins)


def slot_at(who_ref, at_ref, j, sects, rows, cols):
    reader = jnp.bitwise_xor(who_ref[0], j) * sects + who_ref[1]
    return at_ref[reader, 0] - who_ref[0] * rows, at_ref[reader, 1] - who_ref[1] * cols


def like(shape, dtype=HALF):
    return jax.ShapeDtypeStruct(shape, dtype)


def lane_index(shape):
    return lax.broadcasted_iota(jnp.int32, shape, len(shape) - 1)


def pack(state):
    channels, rows, cols = state.shape
    padded = -(-channels // 8) * 8
    deep = -(-padded // 16) * 16
    span = -(-rows * REACH // LANES)

    def body(state_ref, rows_ref, right_ref, left_ref, flat):
        flat[:channels] = state_ref[...]
        flat[channels:] = jnp.zeros((deep - channels, rows, cols), HALF)
        turned = jnp.swapaxes(flat[...], 0, 1)
        rows_ref[...] = turned
        lane = lane_index((deep, LANES))
        none = jnp.zeros((deep, LANES), HALF)
        tiles = [None] * span
        rim = none
        for r in range(rows):
            row = turned[r]
            at, off = divmod(r * REACH, LANES)
            moved = row if off == 0 else pltpu.roll(row, off, 1)
            if tiles[at] is None:
                tiles[at] = moved
            else:
                tiles[at] = jnp.where(lane >= off, moved, tiles[at])
            if off + REACH > LANES:
                tiles[at + 1] = moved
            moved = pltpu.roll(row, (2 * r + 2) % LANES, 1)
            rim = jnp.where((lane >= 2 * r) & (lane < 2 * r + 2), moved, rim)
        for at in range(span):
            right_ref[:, at * LANES : (at + 1) * LANES] = tiles[at][:padded]
        left_ref[...] = rim[:padded]

    return run(
        body,
        [like((rows, deep, cols)), like((padded, span * LANES)), like((padded, LANES))],
        [state],
        [pltpu.VMEM((deep, rows, cols), HALF)],
        "pack",
        micros=3.0,
        scalars=0,
    )


def prep(weights, noise):
    steps, channels, cells = noise.shape
    count = len(weights)
    tile_rows = LANES // SIDE

    def body(*refs):
        ins, noise_ref, outs, noise_out = refs[:count], refs[count], refs[count + 1 : -1], refs[-1]
        for w_ref, o_ref in zip(ins, outs):
            _, made, used = w_ref.shape
            o_ref[...] = jnp.zeros(o_ref.shape, HALF)
            for v in range(2):
                for a in range(3):
                    for b in range(3):
                        at = (3 * (a + v) + b) * LANES
                        o_ref[v * LANES : v * LANES + made, at : at + used] = w_ref[3 * a + b]
        for k in range(steps):
            for t in range(cells // LANES):
                block = noise_ref[k, :, t * LANES : (t + 1) * LANES].astype(FULL)
                block = jnp.concatenate(
                    [block, jnp.zeros((LANES - channels, LANES), FULL)], axis=0
                ).T.astype(HALF)
                for m in range(tile_rows):
                    r = t * tile_rows + m
                    noise_out[
                        k, r // 2 * SIDE : (r // 2 + 1) * SIDE, r % 2 * LANES : (r % 2 + 1) * LANES
                    ] = block[m * SIDE : (m + 1) * SIDE]

    made = [like((2 * LANES, 12 * LANES))] * count + [like((steps, cells // 2, 2 * LANES))]
    out = run(body, made, [*weights, noise], [], "prep", micros=4.0, scalars=0)
    return out[:count], out[count]


def extract(who, anchor, by_row, right, left, bands, sects):
    rows, deep, cols = by_row.shape
    padded = right.shape[0]
    width = cols + LANES
    batch = 4 if bands % 4 == 0 else bands
    chunk = 4

    def body(who_ref, at_ref, rows_ref, right_ref, left_ref,
             keep_ref, send_ref, ext_ref, top_ref, low_ref, ext, picked):
        lane = lane_index((padded, LANES))
        ext[:, padded:, :] = jnp.zeros((rows, deep - padded, width), HALF)
        ext[:, :, :cols] = rows_ref[...]
        rim = left_ref[...]
        none = jnp.zeros((padded, LANES), HALF)
        for r in range(rows):
            at, off = divmod(r * REACH, LANES)
            piece = right_ref[:, at * LANES : (at + 1) * LANES]
            if off:
                piece = pltpu.roll(piece, LANES - off, 1)
            if off + REACH > LANES:
                after = right_ref[:, (at + 1) * LANES : (at + 2) * LANES]
                piece = jnp.where(lane < LANES - off, piece, pltpu.roll(after, LANES - off, 1))
            turned = pltpu.roll(rim, (LANES - 2 - 2 * r) % LANES, 1)
            piece = jnp.where(lane < REACH, piece, jnp.where(lane >= LANES - 2, turned, none))
            ext[r, :padded, cols:] = piece
        ext_ref[...] = ext[...]
        top_ref[...] = ext[:2]
        low_ref[...] = ext[rows - 2 :]
        for first in range(0, bands, batch):
            picks = []
            for j in range(first, first + batch):
                col0 = slot_at(who_ref, at_ref, j, sects, rows, cols)[1] - 2
                source = lax.broadcasted_iota(jnp.int32, (width, LANES), 0)
                target = lane_index((width, LANES))
                inner = target
                for m in range(1, PER_TILE):
                    inner = jnp.where(target >= WIDE * m, target - WIDE * m, inner)
                want = jnp.bitwise_and(inner + col0, width - 1)
                picks.append(jnp.where(source == want, 1.0, 0.0).astype(HALF))
            pick = jnp.concatenate(picks, axis=1)

            def select(c, carry):
                view = ext[pl.ds(c * chunk, chunk)].reshape(chunk * deep, width)
                picked[pl.ds(c * chunk, chunk)] = jnp.dot(
                    view, pick, preferred_element_type=FULL
                ).reshape(chunk, deep, batch * LANES)
                return carry

            lax.fori_loop(0, rows // chunk, select, 0)
            for j in range(first, first + batch):
                out_ref = send_ref if j % 2 else keep_ref
                row0 = slot_at(who_ref, at_ref, j, sects, rows, cols)[0] - 2
                inside = (row0 > -WIDE) & (row0 < rows)

                @pl.when(inside)
                def _(j=j, row0=row0, out_ref=out_ref, first=first):
                    lanes = slice((j - first) * LANES, (j - first + 1) * LANES)
                    zone = lane_index((padded, LANES))
                    for t in range(TILES):
                        total = jnp.zeros((padded, LANES), FULL)
                        for m in range(PER_TILE):
                            r = row0 + t * PER_TILE + m
                            low = jnp.where((r >= 0) & (r < rows), WIDE * m, width)
                            keep = (zone >= low) & (zone < WIDE * (m + 1))
                            value = picked[jnp.clip(r, 0, rows - 1), :padded, lanes]
                            total = jnp.where(keep, value, total)
                        out_ref[j // 2, :, t * LANES : (t + 1) * LANES] = total.astype(HALF)

                @pl.when(jnp.logical_not(inside))
                def _(j=j, out_ref=out_ref):
                    out_ref[j // 2] = jnp.zeros((padded, TILES * LANES), HALF)

    part = like((bands // 2, padded, TILES * LANES))
    edge = like((2, deep, width))
    return run(
        body,
        [part, part, like((rows, deep, width)), edge, edge],
        [who, anchor, by_row, right, left],
        [pltpu.VMEM((rows, deep, width), HALF), pltpu.VMEM((rows, deep, batch * LANES), FULL)],
        "extract",
        micros=3.0,
        scalars=2,
    )


def pair_bias(bias):
    line = jnp.pad(bias, ((0, LANES - bias.shape[0]),))
    return jnp.concatenate([line, line])[None, :]


def product(view, weight):
    return lax.dot_general(
        view, weight, (((1,), (1,)), ((), ())), preferred_element_type=FULL
    )


def gather_pairs(shifted, first, count):
    view = jnp.concatenate(
        [shifted[b, pl.ds(first + u, count), v] for u in (0, 1) for v in (0, 1) for b in (0, 1, 2)],
        axis=-1,
    )
    return view.reshape(count * view.shape[1], view.shape[2])


def silu(value):
    return value / (1.0 + jnp.exp(-value))


def patch_step(who, anchor, addends, noise, weights, biases, step_bias, sects, limits):
    padded = addends[0].shape[1]
    steps = noise.shape[0]
    half = SIDE // 2
    loose = 48

    def body(*refs):
        who_ref, at_ref = refs[:2]
        parts = refs[2 : 2 + len(addends)]
        mine = who_ref[0] * sects + who_ref[1]
        row0, col0 = at_ref[mine, 0], at_ref[mine, 1]
        (noise_ref, w_in, w_out, d_in, d_out, b_in, b_out, b_step, b_den, out_ref,
         flat, state_sh, hid, hid_sh, pad, pad_sh, corr) = refs[2 + len(addends) :]
        for t in range(TILES):
            lanes = slice(t * LANES, (t + 1) * LANES)
            tile = parts[0][0, :, lanes].astype(FULL)
            for part in parts[1:]:
                tile = tile + part[0, :, lanes].astype(FULL)
            tile = jnp.concatenate([tile, jnp.zeros((LANES - padded, LANES), FULL)], axis=0)
            flat[lanes, :] = tile.T
        for i in range(WIDE):
            t, m = divmod(i, PER_TILE)
            off = t * LANES + m * WIDE
            for b in range(3):
                state_sh[b, i // 2, i % 2] = flat[off + b : off + b + loose, :].astype(HALF)
        pairs = half + 1
        value = product(gather_pairs(state_sh, 0, pairs), w_in[...])
        value = silu(value + b_in[...]).reshape(pairs, loose, 2 * LANES)
        pair = lax.broadcasted_iota(jnp.int32, value.shape, 0)
        col = lax.broadcasted_iota(jnp.int32, value.shape, 1)
        odd = (lane_index(value.shape) >= LANES).astype(jnp.int32)
        grid_row = row0 - 1 + 2 * pair + odd
        grid_col = col0 - 1 + col
        keep = (
            (grid_row >= 0) & (grid_row < limits[0])
            & (grid_col >= 0) & (grid_col < limits[1]) & (col < SIDE + 2)
        )
        value = jnp.where(keep, value, 0.0)
        hid[:, 0] = value[:, :, :LANES]
        hid[:, 1] = value[:, :, LANES:]
        for b in range(3):
            hid_sh[b] = hid[:, :, b : b + SIDE, :].astype(HALF)
        value = product(gather_pairs(hid_sh, 0, half), w_out[...])
        center = jnp.concatenate(
            [state_sh[2, 1 : 1 + half, v, :SIDE, :] for v in (0, 1)], axis=-1
        ).astype(FULL).reshape(half * SIDE, 2 * LANES)
        mean = (center + value + b_out[...]).astype(HALF).astype(FULL)
        state = mean + noise_ref[0].astype(FULL)
        pad[...] = jnp.zeros(pad.shape, FULL)

        def conv(source, weight):
            shaped = source.reshape(half, SIDE, 2 * LANES)
            pad[:half, 1, 8 : 8 + SIDE] = shaped[:, :, :LANES]
            pad[1:, 0, 8 : 8 + SIDE] = shaped[:, :, LANES:]
            for b in range(3):
                pad_sh[b] = pad[:, :, 7 + b : 7 + b + SIDE, :].astype(HALF)
            return product(gather_pairs(pad_sh, 0, half), weight[...])

        for step in range(steps):
            inner = silu(conv(state, d_in) + b_step[step : step + 1])
            state = state - 0.5 * (conv(inner, d_out) + b_den[...])
            if step + 1 < steps:
                state = state + 0.5 * noise_ref[step + 1].astype(FULL)
        change = (state - mean).reshape(half, SIDE, 2 * LANES)
        corr[:, 0] = change[:, :, :LANES]
        corr[:, 1] = change[:, :, LANES:]
        cells = corr[...].reshape(SIDE * SIDE, LANES)
        for t in range(SIDE * SIDE // LANES):
            lanes = slice(t * LANES, (t + 1) * LANES)
            out_ref[:, lanes] = cells[lanes].T[:padded].astype(HALF)

    return run(
        body,
        [like((padded, SIDE * SIDE))],
        [who, anchor, *addends, noise, *weights, *biases[:2], step_bias, biases[2]],
        [
            pltpu.VMEM((TILES * LANES, LANES), FULL),
            pltpu.VMEM((3, WIDE // 2, 2, loose, LANES), HALF),
            pltpu.VMEM((half + 1, 2, loose, LANES), FULL),
            pltpu.VMEM((3, half + 1, 2, SIDE, LANES), HALF),
            pltpu.VMEM((half + 1, 2, loose, LANES), FULL),
            pltpu.VMEM((3, half + 1, 2, SIDE, LANES), HALF),
            pltpu.VMEM((half, 2, SIDE, LANES), FULL),
        ],
        "patch",
        micros=8.0,
        scalars=2,
    )[0]


def grid_mean(who, ext, rim, lower, padded, weights, biases, limits):
    rows, deep, width = ext.shape
    cols = width - LANES
    loose = cols + 16
    made = rows // 2
    pairs_in, pairs_out = made // 4 + 1, made // 4
    hidden_pairs = made // 2 + 1
    if hidden_pairs % pairs_in:
        hidden_pairs += pairs_in - hidden_pairs % pairs_in
    state_pairs = hidden_pairs + 1
    base = rows - made - 2 if lower else -2

    def body(who_ref, ext_ref, rim_ref, w_in, w_out, b_in, b_out, out_ref,
             line, state_sh, hid, hid_sh):
        row0 = who_ref[0] * rows + base + 1
        col0 = who_ref[1] * cols - 1

        def spread(i, v, slot, source):
            value = source.astype(FULL)
            if deep < LANES:
                value = jnp.concatenate([value, jnp.zeros((LANES - deep, width), FULL)], axis=0)
            value = value.T
            line[slot, 8 : 8 + cols] = value[:cols]
            line[slot, 8 + cols :] = value[cols : cols + 16]
            line[slot, :8] = value[width - 8 :]
            for b in range(3):
                state_sh[b, i, v] = line[slot, 6 + b : 6 + b + loose, :].astype(HALF)

        for pair in range(made // 2 + 2, state_pairs):
            for b in range(3):
                state_sh[b, pair] = jnp.zeros((2, loose, LANES), HALF)
        edge = made // 2 + 1 if lower else 0
        for v in range(2):
            spread(edge, v, v, rim_ref[v])
        skip = 0 if lower else 1

        def spread_rows(i, carry):
            for v in range(2):
                spread(i + skip, v, v, ext_ref[2 * (i + skip) + v + base])
            return carry

        lax.fori_loop(0, made // 2 + 1, spread_rows, 0)

        def first(chunk, carry):
            start = chunk * pairs_in
            value = product(gather_pairs(state_sh, start, pairs_in), w_in[...])
            value = silu(value + b_in[...]).reshape(pairs_in, loose, 2 * LANES)
            pair = lax.broadcasted_iota(jnp.int32, value.shape, 0)
            col = lax.broadcasted_iota(jnp.int32, value.shape, 1)
            odd = (lane_index(value.shape) >= LANES).astype(jnp.int32)
            grid_row = row0 + 2 * (start + pair) + odd
            grid_col = col0 + col
            keep = (
                (grid_row >= 0) & (grid_row < limits[0])
                & (grid_col >= 0) & (grid_col < limits[1])
            )
            value = jnp.where(keep, value, 0.0)
            hid[:, 0] = value[:, :, :LANES]
            hid[:, 1] = value[:, :, LANES:]
            for b in range(3):
                hid_sh[b, pl.ds(start, pairs_in)] = hid[:, :, b : b + cols, :].astype(HALF)
            return carry

        lax.fori_loop(0, hidden_pairs // pairs_in, first, 0)

        def second(chunk, carry):
            start = chunk * pairs_out
            value = product(gather_pairs(hid_sh, start, pairs_out), w_out[...]) + b_out[...]
            value = value.reshape(pairs_out, cols, 2 * LANES)
            for k in range(pairs_out):
                for v in range(2):
                    center = state_sh[2, start + k + 1, v, :cols, :].astype(FULL)
                    mean = center + value[k, :, v * LANES : (v + 1) * LANES]
                    out_ref[2 * (start + k) + v] = mean.T[:padded].astype(HALF)
            return carry

        lax.fori_loop(0, made // 2 // pairs_out, second, 0)

    return run(
        body,
        [like((made, padded, cols))],
        [who, ext, rim, *weights, *biases],
        [
            pltpu.VMEM((2, loose + 8, LANES), FULL),
            pltpu.VMEM((3, state_pairs, 2, loose, LANES), HALF),
            pltpu.VMEM((pairs_in, 2, loose, LANES), FULL),
            pltpu.VMEM((3, hidden_pairs, 2, cols, LANES), HALF),
        ],
        "mean_low" if lower else "mean_top",
        micros=5.0,
    )[0]


def spill(who, anchor, pieces, sources, sects, rows, cols):
    padded = pieces[0].shape[-2]

    def body(who_ref, at_ref, *refs):
        out_ref, total = refs[-2:]
        lane = lane_index((padded, LANES))
        none = jnp.zeros((padded, LANES), HALF)
        total[...] = jnp.zeros(total.shape, FULL)
        for piece, j in zip(refs, sources):
            row0, col0 = slot_at(who_ref, at_ref, j, sects, rows, cols)

            @pl.when(col0 > cols - SIDE)
            def _(piece=piece, row0=row0, col0=col0):
                def one(r, carry):
                    i = r - row0
                    source = pl.multiple_of((i // 4) * LANES, LANES)
                    target = pl.multiple_of((r // 4) * LANES, LANES)
                    low = SIDE * (r % 4)
                    turn = jnp.bitwise_and(low - SIDE * (i % 4) + col0 - cols, LANES - 1)
                    value = pltpu.roll(piece[:, pl.ds(source, LANES)], turn, 1)
                    keep = (lane >= low) & (lane < low + col0 - (cols - SIDE))
                    total[:, pl.ds(target, LANES)] += jnp.where(keep, value, none).astype(FULL)
                    return carry

                lax.fori_loop(jnp.maximum(row0, 0), jnp.minimum(row0 + SIDE, rows), one, 0)

        out_ref[...] = total[...].astype(HALF)

    shape = (padded, rows * SIDE)
    return run(
        body, [like(shape)], [who, anchor, *pieces], [pltpu.VMEM(shape, FULL)], "spill",
        micros=1.5, scalars=2,
    )[0]


def canvas(who, anchor, pieces, sources, sects, rows, cols):
    padded = pieces[0].shape[-2]
    total = anchor.shape[0]

    def body(who_ref, at_ref, *refs):
        out_ref, inverse_ref = refs[-2:]
        lane = lane_index((padded, LANES))
        none = jnp.zeros((padded, LANES), HALF)
        out_ref[...] = jnp.zeros(out_ref.shape, FULL)
        for piece, j in zip(refs, sources):
            row0, col0 = slot_at(who_ref, at_ref, j, sects, rows, cols)

            def one(k, carry, piece=piece, row0=row0, col0=col0):
                value = piece[:, pl.ds(pl.multiple_of(k * LANES, LANES), LANES)]
                for m in range(4):
                    r = row0 + 4 * k + m
                    low = jnp.where((r >= 0) & (r < rows), col0, 2 * LANES)
                    moved = pltpu.roll(value, jnp.bitwise_and(col0 - SIDE * m, LANES - 1), 1)
                    keep = (lane >= low) & (lane < col0 + SIDE)
                    out_ref[jnp.clip(r, 0, rows - 1)] += jnp.where(keep, moved, none).astype(FULL)
                return carry

            start = jnp.clip(-row0, 0, SIDE) // 4
            stop = (jnp.clip(rows - row0, 0, SIDE) + 3) // 4
            lax.fori_loop(start, stop, one, 0)
        row = lax.broadcasted_iota(jnp.int32, (rows, cols), 0) + who_ref[0] * rows
        col = lane_index((rows, cols)) + who_ref[1] * cols

        def cover(p, count):
            down, across = row - at_ref[p, 0], col - at_ref[p, 1]
            hit = (down >= 0) & (down < SIDE) & (across >= 0) & (across < SIDE)
            return count + jnp.where(hit, 1.0, 0.0)

        count = lax.fori_loop(0, total, cover, jnp.zeros((rows, cols), FULL))
        inverse_ref[...] = 1.0 / jnp.maximum(count, 1.0)

    return run(
        body, [like((rows, padded, cols), FULL), like((rows, cols), FULL)],
        [who, anchor, *pieces], [], "canvas", micros=2.5, scalars=2,
    )


def finish(means, summed, arrived, inverse, channels):
    rows, padded, cols = summed.shape
    deep = -(-padded // 16) * 16
    half = means[0].shape[0]

    def body(top_ref, low_ref, sum_ref, spill_ref, inverse_ref, out_ref, flat):
        lane = lane_index((padded, LANES))
        none = jnp.zeros((padded, LANES), HALF)
        flat[:, padded:] = jnp.zeros((rows, deep - padded, cols), HALF)
        for r in range(rows):
            at, low = divmod(r * SIDE, LANES)
            extra = spill_ref[:, at * LANES : (at + 1) * LANES]
            if low:
                extra = pltpu.roll(extra, LANES - low, 1)
            extra = jnp.where(lane < SIDE, extra, none).astype(FULL)
            mean = top_ref[r] if r < half else low_ref[r - half]
            value = mean.astype(FULL) + (sum_ref[r] + extra) * inverse_ref[r : r + 1]
            flat[r, :padded] = value.astype(HALF)
        out_ref[...] = jnp.swapaxes(flat[...], 0, 1)[:channels]

    return run(
        body,
        [like((channels, rows, cols))],
        [*means, summed, arrived, inverse],
        [pltpu.VMEM((rows, deep, cols), HALF)],
        "finish",
        micros=3.0,
        scalars=0,
    )[0]


def per_device(
    state_field,
    conv_in_weight,
    conv_in_bias,
    conv_out_weight,
    conv_out_bias,
    patch_anchor,
    patch_noise,
    denoise_in_weight,
    step_bias,
    denoise_out_weight,
    denoise_bias,
):
    bands = lax.axis_size("band")
    sects = lax.axis_size("sect")
    channels, rows, cols = state_field.shape
    limits = (rows * bands, cols * sects)
    who = jnp.stack([lax.axis_index("band"), lax.axis_index("sect")]).astype(jnp.int32)

    by_row, right_rim, left_rim = pack(state_field)
    padded = right_rim.shape[0]
    right = shift_from(right_rim, "sect", -1)
    left = shift_from(left_rim, "sect", 1)

    made, noise = prep(
        [conv_in_weight, conv_out_weight, denoise_in_weight, denoise_out_weight], patch_noise[0]
    )
    biases = [pair_bias(b) for b in (conv_in_bias, conv_out_bias, denoise_bias)]
    step_lines = jnp.concatenate([step_bias, step_bias], axis=-1)

    kept, sent, ext, top, low = extract(
        who, patch_anchor, by_row, right, left, bands, sects
    )
    got = swap(sent, "band", 1)
    addends = [kept, got]
    bit = 2
    parts = None
    while bit < bands:
        parts = kept + got if parts is None else parts[0::2] + got
        got = swap(parts[1::2], "band", bit)
        addends.append(got)
        bit *= 2
    above = shift_from(low, "band", 1)
    below = shift_from(top, "band", -1)
    correction = patch_step(
        who, patch_anchor, addends, noise, made, biases, step_lines, sects, limits
    )
    pieces = [correction]
    sources = [0]
    bit = bands // 2
    while bit:
        pieces += [swap(piece, "band", bit) for piece in pieces]
        sources += [s ^ bit for s in sources]
        bit //= 2
    means = [
        grid_mean(who, ext, rim, lower, padded, made[:2], biases[:2], limits)
        for lower, rim in ((False, above), (True, below))
    ]
    arrived = shift_from(
        spill(who, patch_anchor, pieces, sources, sects, rows, cols), "sect", 1
    )
    summed, inverse = canvas(who, patch_anchor, pieces, sources, sects, rows, cols)
    return finish(means, summed, arrived, inverse, channels)


def solution(mesh):
    placed = (
        P("groups", "band", "sect"),
        P(),
        P(),
        P(),
        P(),
        P("groups", None),
        P(("groups", "band", "sect"), None, None, None),
        P(),
        P(),
        P(),
        P(),
    )
    return jax.shard_map(
        per_device,
        mesh=mesh,
        in_specs=placed,
        out_specs=P("groups", "band", "sect"),
        check_vma=False,
    )
```

```python
import jax
import jax.numpy as jnp
from jax import lax
from jax.experimental import pallas as pl
from jax.experimental.pallas import tpu as pltpu
from jax.sharding import PartitionSpec as P


SIDE = 32
WIDE = SIDE + 4
PER_TILE = 3
TILES = WIDE // PER_TILE
LANES = 128
REACH = SIDE + 2
CHUNKS = 1
HALF = jnp.bfloat16
FULL = jnp.float32


def shift_from(block, axis, distance):
    count = lax.axis_size(axis)
    route = [(i - distance, i) for i in range(count) if 0 <= i - distance < count]
    return lax.ppermute(block, axis, route)


def swap(block, axis, bit):
    count = lax.axis_size(axis)
    return lax.ppermute(block, axis, [(i, i ^ bit) for i in range(count)])


def run(body, outs, ins, scratch, micros=1.0, scalars=1, limit=16):
    smem = pl.BlockSpec(memory_space=pltpu.SMEM)
    vmem = pl.BlockSpec(memory_space=pltpu.VMEM)
    return pl.pallas_call(
        body,
        out_shape=outs,
        in_specs=[smem] * scalars + [vmem] * (len(ins) - scalars),
        out_specs=[vmem] * len(outs),
        scratch_shapes=scratch,
        cost_estimate=pl.CostEstimate(
            flops=int(micros * 1.15e9), bytes_accessed=1024, transcendentals=0
        ),
        compiler_params=pltpu.CompilerParams(vmem_limit_bytes=limit * 1024 * 1024),
    )(*ins)


def slot_at(who_ref, at_ref, j, sects, rows, cols):
    reader = jnp.bitwise_xor(who_ref[0], j) * sects + who_ref[1]
    return at_ref[reader, 0] - who_ref[0] * rows, at_ref[reader, 1] - who_ref[1] * cols


def like(shape, dtype=HALF):
    return jax.ShapeDtypeStruct(shape, dtype)


def lane_index(shape):
    return lax.broadcasted_iota(jnp.int32, shape, len(shape) - 1)


def turn_rows(state_ref, flat):
    channels = state_ref.shape[0]
    flat[:channels] = state_ref[...]
    flat[channels:] = jnp.zeros((flat.shape[0] - channels,) + flat.shape[1:], HALF)
    return jnp.swapaxes(flat[...], 0, 1)


def pack(who, anchor, state):
    channels, rows, cols = state.shape
    padded = -(-channels // 8) * 8
    deep = -(-padded // 16) * 16
    span = -(-rows * REACH // LANES)

    def body(who_ref, at_ref, state_ref, right_ref, left_ref, flat):
        turned = turn_rows(state_ref, flat)
        lane = lane_index((deep, LANES))
        tiles = [None] * span
        rim = jnp.zeros((deep, LANES), HALF)
        for r in range(rows):
            row = turned[r]
            at, off = divmod(r * REACH, LANES)
            moved = row if off == 0 else pltpu.roll(row, off, 1)
            if tiles[at] is None:
                tiles[at] = moved
            else:
                tiles[at] = jnp.where(lane >= off, moved, tiles[at])
            if off + REACH > LANES:
                tiles[at + 1] = moved
            moved = pltpu.roll(row, (2 * r + 2) % LANES, 1)
            rim = jnp.where((lane >= 2 * r) & (lane < 2 * r + 2), moved, rim)
        for at in range(span):
            right_ref[:, at * LANES : (at + 1) * LANES] = tiles[at][:padded]
        left_ref[...] = rim[:padded]

    return run(
        body,
        [like((padded, span * LANES)), like((padded, LANES))],
        [who, anchor, state],
        [pltpu.VMEM((deep, rows, cols), HALF)],
        micros=1.0,
        scalars=2,
    )


def prep(weights, biases, noise):
    steps, channels, cells = noise.shape
    count = len(weights)
    tile_rows = LANES // SIDE
    lines = len(biases)

    def body(*refs):
        ins, lines_in, noise_ref = refs[:count], refs[count : count + lines], refs[count + lines]
        outs = refs[count + lines + 1 :]
        lines_out, noise_out = outs[count : count + lines], outs[count + lines]
        for k, (w_ref, o_ref) in enumerate(zip(ins, outs)):
            _, down, across = w_ref.shape
            o_ref[...] = jnp.zeros(o_ref.shape, HALF)
            for v in range(2):
                for a in range(3):
                    for b in range(3):
                        tap = (3 * (a + v) + b) * LANES
                        row, col = (v * LANES, tap) if k % 2 else (tap, v * LANES)
                        o_ref[row : row + down, col : col + across] = w_ref[3 * a + b]
        for line_ref, o_ref in zip(lines_in, lines_out):
            used = line_ref.shape[1]
            o_ref[...] = jnp.zeros(o_ref.shape, FULL)
            o_ref[:, :used] = line_ref[...]
            o_ref[:, LANES : LANES + used] = line_ref[...]
        for k in range(steps):
            for t in range(cells // LANES):
                block = noise_ref[k, :, t * LANES : (t + 1) * LANES].astype(FULL)
                block = jnp.concatenate(
                    [block, jnp.zeros((LANES - channels, LANES), FULL)], axis=0
                ).T.astype(HALF)
                for m in range(tile_rows):
                    r = t * tile_rows + m
                    noise_out[
                        k, r // 2 * SIDE : (r // 2 + 1) * SIDE, r % 2 * LANES : (r % 2 + 1) * LANES
                    ] = block[m * SIDE : (m + 1) * SIDE]

    sizes = [(12 * LANES, 2 * LANES), (2 * LANES, 12 * LANES)]
    made = [like(sizes[k % 2]) for k in range(count)]
    made += [like((line.shape[0], 2 * LANES), FULL) for line in biases]
    made += [like((steps, cells // 2, 2 * LANES))]
    out = run(body, made, [*weights, *biases, noise], [], micros=2.0, scalars=0)
    return out[:count], out[count : count + lines], out[count + lines]


def add_parts(kept, got, keep_odd):
    count, padded, lanes = kept.shape

    def body(kept_ref, got_ref, out_ref):
        for k in range(count // 2):
            out_ref[k] = kept_ref[2 * k + keep_odd] + got_ref[2 * k + keep_odd]

    return run(body, [like((count // 2, padded, lanes))], [kept, got], [], micros=0.3, scalars=0)[0]


def extract(who, anchor, state, right, left, bands, sects):
    _, rows, cols = state.shape
    padded = right.shape[0]
    deep = -(-padded // 16) * 16
    width = cols + LANES
    batch = 4 if bands % 4 == 0 else bands
    chunk = 4

    def body(who_ref, at_ref, state_ref, right_ref, left_ref,
             keep_ref, send_ref, top_ref, low_ref, flat, ext, picked):
        lane = lane_index((padded, LANES))
        ext[:, padded:, :] = jnp.zeros((rows, deep - padded, width), HALF)
        ext[:, :, :cols] = turn_rows(state_ref, flat)
        rim = left_ref[...]
        none = jnp.zeros((padded, LANES), HALF)
        for r in range(rows):
            at, off = divmod(r * REACH, LANES)
            piece = right_ref[:, at * LANES : (at + 1) * LANES]
            if off:
                piece = pltpu.roll(piece, LANES - off, 1)
            if off + REACH > LANES:
                after = right_ref[:, (at + 1) * LANES : (at + 2) * LANES]
                piece = jnp.where(lane < LANES - off, piece, pltpu.roll(after, LANES - off, 1))
            turned = pltpu.roll(rim, (LANES - 2 - 2 * r) % LANES, 1)
            piece = jnp.where(lane < REACH, piece, jnp.where(lane >= LANES - 2, turned, none))
            ext[r, :padded, cols:] = piece
        top_ref[...] = ext[:2]
        low_ref[...] = ext[rows - 2 :]
        for first in range(0, bands, batch):
            picks = []
            for j in range(first, first + batch):
                col0 = slot_at(who_ref, at_ref, j, sects, rows, cols)[1] - 2
                source = lax.broadcasted_iota(jnp.int32, (width, LANES), 0)
                target = lane_index((width, LANES))
                inner = target
                for m in range(1, PER_TILE):
                    inner = jnp.where(target >= WIDE * m, target - WIDE * m, inner)
                want = jnp.bitwise_and(inner + col0, width - 1)
                picks.append(jnp.where(source == want, 1.0, 0.0).astype(HALF))
            pick = jnp.concatenate(picks, axis=1)

            def select(c, carry):
                view = ext[pl.ds(c * chunk, chunk)].reshape(chunk * deep, width)
                picked[pl.ds(c * chunk, chunk)] = jnp.dot(
                    view, pick, preferred_element_type=FULL
                ).reshape(chunk, deep, batch * LANES)
                return carry

            lax.fori_loop(0, rows // chunk, select, 0)
            for j in range(first, first + batch):
                out_ref = send_ref if j % 2 else keep_ref
                row0 = slot_at(who_ref, at_ref, j, sects, rows, cols)[0] - 2
                inside = (row0 > -WIDE) & (row0 < rows)

                @pl.when(inside)
                def _(j=j, row0=row0, out_ref=out_ref, first=first):
                    lanes = slice((j - first) * LANES, (j - first + 1) * LANES)
                    zone = lane_index((padded, LANES))
                    for t in range(TILES):
                        total = jnp.zeros((padded, LANES), FULL)
                        for m in range(PER_TILE):
                            r = row0 + t * PER_TILE + m
                            low = jnp.where((r >= 0) & (r < rows), WIDE * m, width)
                            keep = (zone >= low) & (zone < WIDE * (m + 1))
                            value = picked[jnp.clip(r, 0, rows - 1), :padded, lanes]
                            total = jnp.where(keep, value, total)
                        out_ref[j // 2, :, t * LANES : (t + 1) * LANES] = total.astype(HALF)

                @pl.when(jnp.logical_not(inside))
                def _(j=j, out_ref=out_ref):
                    out_ref[j // 2] = jnp.zeros((padded, TILES * LANES), HALF)

    part = like((bands // 2, padded, TILES * LANES))
    edge = like((2, deep, width))
    return run(
        body,
        [part, part, edge, edge],
        [who, anchor, state, right, left],
        [pltpu.VMEM((deep, rows, cols), HALF), pltpu.VMEM((rows, deep, width), HALF), pltpu.VMEM((rows, deep, batch * LANES), FULL)],
        micros=3.0,
        scalars=2,
    )


def product(view, weight):
    turned = weight.shape[0] == 2 * LANES
    return lax.dot_general(
        view, weight, (((1,), (1 if turned else 0,)), ((), ())), preferred_element_type=FULL
    )


def gather_pairs(shifted, first, count):
    view = jnp.concatenate(
        [shifted[b, pl.ds(first + u, count), v] for u in (0, 1) for v in (0, 1) for b in (0, 1, 2)],
        axis=-1,
    )
    return view.reshape(count * view.shape[1], view.shape[2])


def silu(value):
    return value / (1.0 + jnp.exp(-value))


def patch_step(who, anchor, addends, noise, weights, biases, step_bias, sects, limits):
    padded = addends[0].shape[1]
    steps = noise.shape[0]
    half = SIDE // 2
    loose = 48

    def body(*refs):
        who_ref, at_ref = refs[:2]
        parts = refs[2 : 2 + len(addends)]
        mine = who_ref[0] * sects + who_ref[1]
        row0, col0 = at_ref[mine, 0], at_ref[mine, 1]
        (noise_ref, w_in, w_out, d_in, d_out, b_in, b_out, b_step, b_den, out_ref,
         flat, state_sh, hid, hid_sh, pad, pad_sh, corr, state) = refs[2 + len(addends) :]
        for t in range(TILES):
            lanes = slice(t * LANES, (t + 1) * LANES)
            tile = parts[0][0, :, lanes].astype(FULL)
            for part in parts[1:]:
                tile = tile + part[0, :, lanes].astype(FULL)
            tile = jnp.concatenate([tile, jnp.zeros((LANES - padded, LANES), FULL)], axis=0)
            flat[lanes, :] = tile.T
        for i in range(WIDE):
            t, m = divmod(i, PER_TILE)
            off = t * LANES + m * WIDE
            for b in range(3):
                state_sh[b, i // 2, i % 2] = flat[off + b : off + b + loose, :].astype(HALF)
        pairs = half + 1
        value = product(gather_pairs(state_sh, 0, pairs), w_in[...])
        value = silu(value + b_in[...]).reshape(pairs, loose, 2 * LANES)
        pair = lax.broadcasted_iota(jnp.int32, value.shape, 0)
        col = lax.broadcasted_iota(jnp.int32, value.shape, 1)
        odd = (lane_index(value.shape) >= LANES).astype(jnp.int32)
        grid_row = row0 - 1 + 2 * pair + odd
        grid_col = col0 - 1 + col
        keep = (
            (grid_row >= 0) & (grid_row < limits[0])
            & (grid_col >= 0) & (grid_col < limits[1]) & (col < SIDE + 2)
        )
        value = jnp.where(keep, value, 0.0)
        hid[:, 0] = value[:, :, :LANES]
        hid[:, 1] = value[:, :, LANES:]
        for b in range(3):
            hid_sh[b] = hid[:, :, b : b + SIDE, :].astype(HALF)
        value = product(gather_pairs(hid_sh, 0, half), w_out[...])
        center = jnp.concatenate(
            [state_sh[2, 1 : 1 + half, v, :SIDE, :] for v in (0, 1)], axis=-1
        ).astype(FULL).reshape(half * SIDE, 2 * LANES)
        mean = (center + value + b_out[...]).astype(HALF).astype(FULL)
        state[...] = mean + noise_ref[0].astype(FULL)
        pad[...] = jnp.zeros(pad.shape, FULL)
        deal = half // CHUNKS
        trips = jnp.where(who_ref[0] >= 0, CHUNKS, 0)

        def fill(source, first, count):
            shaped = source.reshape(count, SIDE, 2 * LANES)
            pad[pl.ds(first, count), 1, 8 : 8 + SIDE] = shaped[:, :, :LANES]
            pad[pl.ds(first + 1, count), 0, 8 : 8 + SIDE] = shaped[:, :, LANES:]

        def shift():
            for b in range(3):
                pad_sh[b] = pad[:, :, 7 + b : 7 + b + SIDE, :].astype(HALF)

        for step in range(steps):
            fill(state[...], 0, half)
            shift()

            def first(c, carry, step=step):
                value = product(gather_pairs(pad_sh, c * deal, deal), d_in[...])
                fill(silu(value + b_step[step : step + 1]), c * deal, deal)
                return carry

            lax.fori_loop(0, trips, first, 0)
            shift()

            def second(c, carry, step=step):
                value = product(gather_pairs(pad_sh, c * deal, deal), d_out[...])
                cells = pl.ds(pl.multiple_of(c * deal * SIDE, deal * SIDE), deal * SIDE)
                value = state[cells] - 0.5 * (value + b_den[...])
                if step + 1 < steps:
                    value = value + 0.5 * noise_ref[step + 1, cells].astype(FULL)
                state[cells] = value
                return carry

            lax.fori_loop(0, trips, second, 0)
        change = (state[...] - mean).reshape(half, SIDE, 2 * LANES)
        corr[:, 0] = change[:, :, :LANES]
        corr[:, 1] = change[:, :, LANES:]
        cells = corr[...].reshape(SIDE * SIDE, LANES)
        for t in range(SIDE * SIDE // LANES):
            lanes = slice(t * LANES, (t + 1) * LANES)
            out_ref[:, lanes] = cells[lanes].T[:padded].astype(HALF)

    return run(
        body,
        [like((padded, SIDE * SIDE))],
        [who, anchor, *addends, noise, *weights, *biases[:2], step_bias, biases[2]],
        [
            pltpu.VMEM((TILES * LANES, LANES), FULL),
            pltpu.VMEM((3, WIDE // 2, 2, loose, LANES), HALF),
            pltpu.VMEM((half + 1, 2, loose, LANES), FULL),
            pltpu.VMEM((3, half + 1, 2, SIDE, LANES), HALF),
            pltpu.VMEM((half + 1, 2, loose, LANES), FULL),
            pltpu.VMEM((3, half + 1, 2, SIDE, LANES), HALF),
            pltpu.VMEM((half, 2, SIDE, LANES), FULL),
            pltpu.VMEM((half * SIDE, 2 * LANES), FULL),
        ],
        micros=8.0,
        scalars=2,
    )[0]


def grid_mean(who, state, right, left, rim, lower, weights, biases, limits):
    _, rows, cols = state.shape
    padded = right.shape[0]
    deep = -(-padded // 16) * 16
    width = cols + LANES
    span = right.shape[1]
    loose = cols + 16
    made = rows // 2
    pairs_in, pairs_out = made // 4 + 1, made // 4
    hidden_pairs = made // 2 + 1
    if hidden_pairs % pairs_in:
        hidden_pairs += pairs_in - hidden_pairs % pairs_in
    state_pairs = hidden_pairs + 1
    base = rows - made - 2 if lower else -2

    def body(who_ref, state_ref, right_ref, left_ref, rim_ref, w_in, w_out, b_in, b_out, out_ref,
             flat, turned, after, before, line, state_sh, hid, hid_sh):
        row0 = who_ref[0] * rows + base + 1
        col0 = who_ref[1] * cols - 1

        turned[:, :deep] = turn_rows(state_ref, flat)
        turned[:, deep:] = jnp.zeros((rows, LANES - deep, cols), HALF)

        def upright(value):
            value = value.astype(FULL)
            return jnp.concatenate(
                [value, jnp.zeros((LANES - value.shape[0], value.shape[1]), FULL)], axis=0
            ).T

        for t in range(span // LANES):
            lanes = slice(t * LANES, (t + 1) * LANES)
            after[lanes] = upright(right_ref[:, lanes])
        before[...] = upright(left_ref[...])
        line[...] = jnp.zeros(line.shape, FULL)

        def shift(i, v):
            for b in range(3):
                state_sh[b, i, v] = line[v, 6 + b : 6 + b + loose, :].astype(HALF)

        for pair in range(made // 2 + 2, state_pairs):
            for b in range(3):
                state_sh[b, pair] = jnp.zeros((2, loose, LANES), HALF)
        edge = made // 2 + 1 if lower else 0
        for v in range(2):
            value = upright(rim_ref[v])
            line[v, 8 : 8 + cols] = value[:cols]
            line[v, 8 + cols :] = value[cols : cols + 16]
            line[v, :8] = value[width - 8 :]
            shift(edge, v)
        skip = 0 if lower else 1

        def spread_rows(i, carry):
            for v in range(2):
                r = 2 * (i + skip) + v + base
                line[v, 8 : 8 + cols] = turned[r].astype(FULL).T
                line[v, 8 + cols : 10 + cols] = after[pl.ds(r * REACH, 2)]
                line[v, 6:8] = before[pl.ds(2 * r, 2)]
                shift(i + skip, v)
            return carry

        lax.fori_loop(0, made // 2 + 1, spread_rows, 0)

        def first(chunk, carry):
            start = chunk * pairs_in
            value = product(gather_pairs(state_sh, start, pairs_in), w_in[...])
            value = silu(value + b_in[...]).reshape(pairs_in, loose, 2 * LANES)
            pair = lax.broadcasted_iota(jnp.int32, value.shape, 0)
            col = lax.broadcasted_iota(jnp.int32, value.shape, 1)
            odd = (lane_index(value.shape) >= LANES).astype(jnp.int32)
            grid_row = row0 + 2 * (start + pair) + odd
            grid_col = col0 + col
            keep = (
                (grid_row >= 0) & (grid_row < limits[0])
                & (grid_col >= 0) & (grid_col < limits[1])
            )
            value = jnp.where(keep, value, 0.0)
            hid[:, 0] = value[:, :, :LANES]
            hid[:, 1] = value[:, :, LANES:]
            for b in range(3):
                hid_sh[b, pl.ds(start, pairs_in)] = hid[:, :, b : b + cols, :].astype(HALF)
            return carry

        lax.fori_loop(0, hidden_pairs // pairs_in, first, 0)

        def second(chunk, carry):
            start = chunk * pairs_out
            value = product(gather_pairs(hid_sh, start, pairs_out), w_out[...]) + b_out[...]
            value = value.reshape(pairs_out, cols, 2 * LANES)
            for k in range(pairs_out):
                for v in range(2):
                    center = state_sh[2, start + k + 1, v, :cols, :].astype(FULL)
                    mean = center + value[k, :, v * LANES : (v + 1) * LANES]
                    out_ref[2 * (start + k) + v] = mean.T[:padded].astype(HALF)
            return carry

        lax.fori_loop(0, made // 2 // pairs_out, second, 0)

    return run(
        body,
        [like((made, padded, cols))],
        [who, state, right, left, rim, *weights, *biases],
        [
            pltpu.VMEM((deep, rows, cols), HALF),
            pltpu.VMEM((rows, LANES, cols), HALF),
            pltpu.VMEM((span, LANES), FULL),
            pltpu.VMEM((LANES, LANES), FULL),
            pltpu.VMEM((2, loose + 8, LANES), FULL),
            pltpu.VMEM((3, state_pairs, 2, loose, LANES), HALF),
            pltpu.VMEM((pairs_in, 2, loose, LANES), FULL),
            pltpu.VMEM((3, hidden_pairs, 2, cols, LANES), HALF),
        ],
        micros=5.0,
    )[0]


def spill(who, anchor, pieces, sources, sects, rows, cols):
    padded = pieces[0].shape[-2]

    def body(who_ref, at_ref, *refs):
        out_ref, total = refs[-2:]
        lane = lane_index((padded, LANES))
        none = jnp.zeros((padded, LANES), HALF)
        total[...] = jnp.zeros(total.shape, FULL)
        for piece, j in zip(refs, sources):
            row0, col0 = slot_at(who_ref, at_ref, j, sects, rows, cols)

            @pl.when(col0 > cols - SIDE)
            def _(piece=piece, row0=row0, col0=col0):
                def one(r, carry):
                    i = r - row0
                    source = pl.multiple_of((i // 4) * LANES, LANES)
                    target = pl.multiple_of((r // 4) * LANES, LANES)
                    low = SIDE * (r % 4)
                    turn = jnp.bitwise_and(low - SIDE * (i % 4) + col0 - cols, LANES - 1)
                    value = pltpu.roll(piece[:, pl.ds(source, LANES)], turn, 1)
                    keep = (lane >= low) & (lane < low + col0 - (cols - SIDE))
                    total[:, pl.ds(target, LANES)] += jnp.where(keep, value, none).astype(FULL)
                    return carry

                lax.fori_loop(jnp.maximum(row0, 0), jnp.minimum(row0 + SIDE, rows), one, 0)

        out_ref[...] = total[...].astype(HALF)

    shape = (padded, rows * SIDE)
    return run(
        body, [like(shape)], [who, anchor, *pieces], [pltpu.VMEM(shape, FULL)],
        micros=1.5, scalars=2,
    )[0]


def canvas(who, anchor, pieces, sources, sects, rows, cols):
    padded = pieces[0].shape[-2]
    total = anchor.shape[0]

    def body(who_ref, at_ref, *refs):
        out_ref, inverse_ref = refs[-2:]
        lane = lane_index((padded, LANES))
        none = jnp.zeros((padded, LANES), HALF)
        out_ref[...] = jnp.zeros(out_ref.shape, FULL)
        for piece, j in zip(refs, sources):
            row0, col0 = slot_at(who_ref, at_ref, j, sects, rows, cols)

            def one(k, carry, piece=piece, row0=row0, col0=col0):
                value = piece[:, pl.ds(pl.multiple_of(k * LANES, LANES), LANES)]
                for m in range(4):
                    r = row0 + 4 * k + m
                    low = jnp.where((r >= 0) & (r < rows), col0, 2 * LANES)
                    moved = pltpu.roll(value, jnp.bitwise_and(col0 - SIDE * m, LANES - 1), 1)
                    keep = (lane >= low) & (lane < col0 + SIDE)
                    out_ref[jnp.clip(r, 0, rows - 1)] += jnp.where(keep, moved, none).astype(FULL)
                return carry

            start = jnp.clip(-row0, 0, SIDE) // 4
            stop = (jnp.clip(rows - row0, 0, SIDE) + 3) // 4
            lax.fori_loop(start, stop, one, 0)
        row = lax.broadcasted_iota(jnp.int32, (rows, cols), 0) + who_ref[0] * rows
        col = lane_index((rows, cols)) + who_ref[1] * cols

        def cover(p, count):
            down, across = row - at_ref[p, 0], col - at_ref[p, 1]
            hit = (down >= 0) & (down < SIDE) & (across >= 0) & (across < SIDE)
            return count + jnp.where(hit, 1.0, 0.0)

        count = lax.fori_loop(0, total, cover, jnp.zeros((rows, cols), FULL))
        inverse_ref[...] = 1.0 / jnp.maximum(count, 1.0)

    return run(
        body, [like((rows, padded, cols), FULL), like((rows, cols), FULL)],
        [who, anchor, *pieces], [], micros=2.5, scalars=2,
    )


def finish(means, summed, arrived, inverse, channels):
    rows, padded, cols = summed.shape
    deep = -(-padded // 16) * 16
    half = means[0].shape[0]

    def body(top_ref, low_ref, sum_ref, spill_ref, inverse_ref, out_ref, flat):
        lane = lane_index((padded, LANES))
        none = jnp.zeros((padded, LANES), HALF)
        flat[:, padded:] = jnp.zeros((rows, deep - padded, cols), HALF)
        for r in range(rows):
            at, low = divmod(r * SIDE, LANES)
            extra = spill_ref[:, at * LANES : (at + 1) * LANES]
            if low:
                extra = pltpu.roll(extra, LANES - low, 1)
            extra = jnp.where(lane < SIDE, extra, none).astype(FULL)
            mean = top_ref[r] if r < half else low_ref[r - half]
            value = mean.astype(FULL) + (sum_ref[r] + extra) * inverse_ref[r : r + 1]
            flat[r, :padded] = value.astype(HALF)
        out_ref[...] = jnp.swapaxes(flat[...], 0, 1)[:channels]

    return run(
        body,
        [like((channels, rows, cols))],
        [*means, summed, arrived, inverse],
        [pltpu.VMEM((rows, deep, cols), HALF)],
        micros=3.0,
        scalars=0,
    )[0]


def step(
    state_field,
    conv_in_weight,
    conv_in_bias,
    conv_out_weight,
    conv_out_bias,
    patch_anchor,
    patch_noise,
    denoise_in_weight,
    step_bias,
    denoise_out_weight,
    denoise_bias,
):
    bands = lax.axis_size("band")
    sects = lax.axis_size("sect")
    channels, rows, cols = state_field.shape
    limits = (rows * bands, cols * sects)
    who = jnp.stack([lax.axis_index("band"), lax.axis_index("sect")]).astype(jnp.int32)

    right_rim, left_rim = pack(who, patch_anchor, state_field)
    right = shift_from(right_rim, "sect", -1)
    left = shift_from(left_rim, "sect", 1)

    made, lines, noise = prep(
        [
            conv_in_weight.transpose(0, 2, 1),
            conv_out_weight,
            denoise_in_weight.transpose(0, 2, 1),
            denoise_out_weight,
        ],
        [conv_in_bias[None, :], conv_out_bias[None, :], denoise_bias[None, :], step_bias],
        patch_noise[0],
    )
    biases, step_lines = lines[:3], lines[3]

    kept, sent, top, low = extract(who, patch_anchor, state_field, right, left, bands, sects)
    got = swap(sent, "band", 1)
    addends = [kept, got]
    bit = 2
    while bit < bands:
        odd = add_parts(kept, got, 1)
        kept = add_parts(kept, got, 0) if 2 * bit < bands else kept
        got = swap(odd, "band", bit)
        addends.append(got)
        bit *= 2
    above = shift_from(low, "band", 1)
    below = shift_from(top, "band", -1)
    correction = patch_step(
        who, patch_anchor, addends, noise, made, biases, step_lines, sects, limits
    )
    pieces = [correction]
    sources = [0]
    bit = bands // 2
    while bit:
        fresh = []
        for piece in pieces:
            fresh.append(swap(piece, "band", bit))
        pieces += fresh
        sources += [s ^ bit for s in sources]
        bit //= 2

    def grid(lower, rim):
        return grid_mean(
            who, state_field, right, left, rim, lower, made[:2], biases[:2], limits
        )

    top_mean = grid(False, above)
    low_mean = grid(True, below)
    spilled = spill(who, patch_anchor, pieces, sources, sects, rows, cols)
    arrived = shift_from(spilled, "sect", 1)
    summed, inverse = canvas(who, patch_anchor, pieces, sources, sects, rows, cols)
    return finish([top_mean, low_mean], summed, arrived, inverse, channels)


def solution(mesh):
    placed = (
        P("groups", "band", "sect"),
        P(),
        P(),
        P(),
        P(),
        P("groups", None),
        P(("groups", "band", "sect"), None, None, None),
        P(),
        P(),
        P(),
        P(),
    )
    return jax.shard_map(
        step,
        mesh=mesh,
        in_specs=placed,
        out_specs=P("groups", "band", "sect"),
        check_vma=False,
    )
```

```python
import jax
import jax.numpy as jnp
from jax import lax
from jax.experimental import pallas as pl
from jax.experimental.pallas import tpu as pltpu
from jax.sharding import PartitionSpec as P


SIDE = 32
WIDE = SIDE + 4
PER_TILE = 3
TILES = WIDE // PER_TILE
LANES = 128
REACH = SIDE + 2
CHUNKS = 1
HALF = jnp.bfloat16
FULL = jnp.float32


def shift_from(block, axis, distance):
    count = lax.axis_size(axis)
    route = [(i - distance, i) for i in range(count) if 0 <= i - distance < count]
    return lax.ppermute(block, axis, route)


def swap(block, axis, bit):
    count = lax.axis_size(axis)
    return lax.ppermute(block, axis, [(i, i ^ bit) for i in range(count)])


def run(body, outs, ins, scratch, micros=1.0, scalars=1, limit=16):
    smem = pl.BlockSpec(memory_space=pltpu.SMEM)
    vmem = pl.BlockSpec(memory_space=pltpu.VMEM)
    return pl.pallas_call(
        body,
        out_shape=outs,
        in_specs=[smem] * scalars + [vmem] * (len(ins) - scalars),
        out_specs=[vmem] * len(outs),
        scratch_shapes=scratch,
        cost_estimate=pl.CostEstimate(
            flops=int(micros * 1.15e9), bytes_accessed=1024, transcendentals=0
        ),
        compiler_params=pltpu.CompilerParams(vmem_limit_bytes=limit * 1024 * 1024),
    )(*ins)


def slot_at(who_ref, at_ref, j, sects, rows, cols):
    reader = jnp.bitwise_xor(who_ref[0], j) * sects + who_ref[1]
    return at_ref[0, reader] - who_ref[0] * rows, at_ref[1, reader] - who_ref[1] * cols


def like(shape, dtype=HALF):
    return jax.ShapeDtypeStruct(shape, dtype)


def lane_index(shape):
    return lax.broadcasted_iota(jnp.int32, shape, len(shape) - 1)


def turn_rows(state_ref, flat):
    channels = state_ref.shape[0]
    flat[:channels] = state_ref[...]
    flat[channels:] = jnp.zeros((flat.shape[0] - channels,) + flat.shape[1:], HALF)
    return jnp.swapaxes(flat[...], 0, 1)


def pack(who, anchor, state):
    channels, rows, cols = state.shape
    padded = -(-channels // 8) * 8
    deep = -(-padded // 16) * 16
    span = -(-rows * REACH // LANES)

    def body(who_ref, at_ref, state_ref, right_ref, left_ref, rows_ref, flat):
        turned = turn_rows(state_ref, flat)
        rows_ref[...] = turned
        lane = lane_index((deep, LANES))
        tiles = [None] * span
        rim = jnp.zeros((deep, LANES), HALF)
        for r in range(rows):
            row = turned[r]
            at, off = divmod(r * REACH, LANES)
            moved = row if off == 0 else pltpu.roll(row, off, 1)
            if tiles[at] is None:
                tiles[at] = moved
            else:
                tiles[at] = jnp.where(lane >= off, moved, tiles[at])
            if off + REACH > LANES:
                tiles[at + 1] = moved
            moved = pltpu.roll(row, (2 * r + 2) % LANES, 1)
            rim = jnp.where((lane >= 2 * r) & (lane < 2 * r + 2), moved, rim)
        for at in range(span):
            right_ref[:, at * LANES : (at + 1) * LANES] = tiles[at][:padded]
        left_ref[...] = rim[:padded]

    return run(
        body,
        [like((padded, span * LANES)), like((padded, LANES)), like((rows, deep, cols))],
        [who, anchor, state],
        [pltpu.VMEM((deep, rows, cols), HALF)],
        micros=1.0,
        scalars=2,
    )


def prep(who, anchor, weights, biases, noise, bands, sects, rows, cols):
    steps, channels, cells = noise.shape
    count = len(weights)
    tile_rows = LANES // SIDE
    lines = len(biases)
    width = cols + LANES

    def body(who_ref, at_ref, *refs):
        ins, lines_in, noise_ref = refs[:count], refs[count : count + lines], refs[count + lines]
        outs = refs[count + lines + 1 :]
        lines_out, noise_out = outs[count : count + lines], outs[count + lines]
        pick_ref, place_ref = outs[count + lines + 1 :]
        for k, (w_ref, o_ref) in enumerate(zip(ins, outs)):
            _, down, across = w_ref.shape
            o_ref[...] = jnp.zeros(o_ref.shape, HALF)
            for v in range(2):
                for a in range(3):
                    for b in range(3):
                        tap = (3 * (a + v) + b) * LANES
                        row, col = (v * LANES, tap) if k % 2 else (tap, v * LANES)
                        o_ref[row : row + down, col : col + across] = w_ref[3 * a + b]
        for line_ref, o_ref in zip(lines_in, lines_out):
            used = line_ref.shape[1]
            o_ref[...] = jnp.zeros(o_ref.shape, FULL)
            o_ref[:, :used] = line_ref[...]
            o_ref[:, LANES : LANES + used] = line_ref[...]
        for k in range(steps):
            for t in range(cells // LANES):
                block = noise_ref[k, :, t * LANES : (t + 1) * LANES].astype(FULL)
                block = jnp.concatenate(
                    [block, jnp.zeros((LANES - channels, LANES), FULL)], axis=0
                ).T.astype(HALF)
                for m in range(tile_rows):
                    r = t * tile_rows + m
                    noise_out[
                        k, r // 2 * SIDE : (r // 2 + 1) * SIDE, r % 2 * LANES : (r % 2 + 1) * LANES
                    ] = block[m * SIDE : (m + 1) * SIDE]
        source = lax.broadcasted_iota(jnp.int32, (width, LANES), 0)
        inner = lane_index((width, LANES))
        for _ in range(1, PER_TILE):
            inner = jnp.where(inner >= WIDE, inner - WIDE, inner)
        cell = lax.broadcasted_iota(jnp.int32, (LANES, 2 * LANES), 0)
        target = lane_index((LANES, 2 * LANES))
        for j in range(bands):
            row0, col0 = slot_at(who_ref, at_ref, j, sects, rows, cols)
            want = jnp.bitwise_and(inner + (col0 - 2), width - 1)
            pick_ref[:, j * LANES : (j + 1) * LANES] = jnp.where(source == want, 1.0, 0.0).astype(HALF)
            across = jnp.bitwise_and(cell, SIDE - 1) + col0
            for m in range(tile_rows):
                turn = jnp.bitwise_and(m - row0, tile_rows - 1)
                there = jnp.where(across < cols, across, across - cols + LANES + m * SIDE)
                hit = (target == there) & (cell >= turn * SIDE) & (cell < (turn + 1) * SIDE)
                place_ref[m, j * LANES : (j + 1) * LANES] = jnp.where(hit, 1.0, 0.0).astype(HALF)

    sizes = [(12 * LANES, 2 * LANES), (2 * LANES, 12 * LANES)]
    made = [like(sizes[k % 2]) for k in range(count)]
    made += [like((line.shape[0], 2 * LANES), FULL) for line in biases]
    made += [like((steps, cells // 2, 2 * LANES))]
    made += [like((width, bands * LANES)), like((tile_rows, bands * LANES, 2 * LANES))]
    out = run(body, made, [who, anchor, *weights, *biases, noise], [], micros=2.5, scalars=2)
    return out[:count], out[count : count + lines], *out[count + lines :]


def add_parts(kept, got, keep_odd):
    count, padded, lanes = kept.shape

    def body(kept_ref, got_ref, out_ref):
        for k in range(count // 2):
            out_ref[k] = kept_ref[2 * k + keep_odd] + got_ref[2 * k + keep_odd]

    return run(body, [like((count // 2, padded, lanes))], [kept, got], [], micros=0.3, scalars=0)[0]


def extract(who, anchor, turned, right, left, pick, bands, sects):
    rows, deep, cols = turned.shape
    padded = right.shape[0]
    width = cols + LANES
    batch = 4 if bands % 4 == 0 else bands
    chunk = 4

    def body(who_ref, at_ref, rows_ref, right_ref, left_ref, pick_ref,
             keep_ref, send_ref, top_ref, low_ref, ext, picked):
        lane = lane_index((padded, LANES))
        ext[:, padded:, :] = jnp.zeros((rows, deep - padded, width), HALF)
        ext[:, :, :cols] = rows_ref[...]
        rim = left_ref[...]
        none = jnp.zeros((padded, LANES), HALF)
        for r in range(rows):
            at, off = divmod(r * REACH, LANES)
            piece = right_ref[:, at * LANES : (at + 1) * LANES]
            if off:
                piece = pltpu.roll(piece, LANES - off, 1)
            if off + REACH > LANES:
                after = right_ref[:, (at + 1) * LANES : (at + 2) * LANES]
                piece = jnp.where(lane < LANES - off, piece, pltpu.roll(after, LANES - off, 1))
            turned = pltpu.roll(rim, (LANES - 2 - 2 * r) % LANES, 1)
            piece = jnp.where(lane < REACH, piece, jnp.where(lane >= LANES - 2, turned, none))
            ext[r, :padded, cols:] = piece
        top_ref[...] = ext[:2]
        low_ref[...] = ext[rows - 2 :]
        for first in range(0, bands, batch):
            chosen = slice(first * LANES, (first + batch) * LANES)

            def select(c, carry, chosen=chosen):
                view = ext[pl.ds(c * chunk, chunk)].reshape(chunk * deep, width)
                picked[pl.ds(c * chunk, chunk)] = jnp.dot(
                    view, pick_ref[:, chosen], preferred_element_type=FULL
                ).reshape(chunk, deep, batch * LANES)
                return carry

            lax.fori_loop(0, rows // chunk, select, 0)
            for j in range(first, first + batch):
                out_ref = send_ref if j % 2 else keep_ref
                row0 = slot_at(who_ref, at_ref, j, sects, rows, cols)[0] - 2
                inside = (row0 > -WIDE) & (row0 < rows)

                @pl.when(inside)
                def _(j=j, row0=row0, out_ref=out_ref, first=first):
                    lanes = slice((j - first) * LANES, (j - first + 1) * LANES)
                    zone = lane_index((padded, LANES))
                    for t in range(TILES):
                        total = jnp.zeros((padded, LANES), FULL)
                        for m in range(PER_TILE):
                            r = row0 + t * PER_TILE + m
                            low = jnp.where((r >= 0) & (r < rows), WIDE * m, width)
                            keep = (zone >= low) & (zone < WIDE * (m + 1))
                            value = picked[jnp.clip(r, 0, rows - 1), :padded, lanes]
                            total = jnp.where(keep, value, total)
                        out_ref[j // 2, :, t * LANES : (t + 1) * LANES] = total.astype(HALF)

                @pl.when(jnp.logical_not(inside))
                def _(j=j, out_ref=out_ref):
                    out_ref[j // 2] = jnp.zeros((padded, TILES * LANES), HALF)

    part = like((bands // 2, padded, TILES * LANES))
    edge = like((2, deep, width))
    return run(
        body,
        [part, part, edge, edge],
        [who, anchor, turned, right, left, pick],
        [pltpu.VMEM((rows, deep, width), HALF), pltpu.VMEM((rows, deep, batch * LANES), FULL)],
        micros=3.0,
        scalars=2,
    )


def product(view, weight):
    turned = weight.shape[0] == 2 * LANES
    return lax.dot_general(
        view, weight, (((1,), (1 if turned else 0,)), ((), ())), preferred_element_type=FULL
    )


def gather_pairs(shifted, first, count):
    view = jnp.concatenate(
        [shifted[b, pl.ds(first + u, count), v] for u in (0, 1) for v in (0, 1) for b in (0, 1, 2)],
        axis=-1,
    )
    return view.reshape(count * view.shape[1], view.shape[2])


def silu(value):
    return value / (1.0 + jnp.exp(-value))


def patch_step(who, anchor, addends, noise, weights, biases, step_bias, sects, limits):
    padded = addends[0].shape[1]
    steps = noise.shape[0]
    half = SIDE // 2
    loose = 48

    def body(*refs):
        who_ref, at_ref = refs[:2]
        parts = refs[2 : 2 + len(addends)]
        mine = who_ref[0] * sects + who_ref[1]
        row0, col0 = at_ref[0, mine], at_ref[1, mine]
        (noise_ref, w_in, w_out, d_in, d_out, b_in, b_out, b_step, b_den, out_ref,
         flat, state_sh, hid, hid_sh, pad, pad_sh, corr, state) = refs[2 + len(addends) :]
        for t in range(TILES):
            lanes = slice(t * LANES, (t + 1) * LANES)
            tile = parts[0][0, :, lanes].astype(FULL)
            for part in parts[1:]:
                tile = tile + part[0, :, lanes].astype(FULL)
            tile = jnp.concatenate([tile, jnp.zeros((LANES - padded, LANES), FULL)], axis=0)
            flat[lanes, :] = tile.T
        for i in range(WIDE):
            t, m = divmod(i, PER_TILE)
            off = t * LANES + m * WIDE
            for b in range(3):
                state_sh[b, i // 2, i % 2] = flat[off + b : off + b + loose, :].astype(HALF)
        pairs = half + 1
        value = product(gather_pairs(state_sh, 0, pairs), w_in[...])
        value = silu(value + b_in[...]).reshape(pairs, loose, 2 * LANES)
        pair = lax.broadcasted_iota(jnp.int32, value.shape, 0)
        col = lax.broadcasted_iota(jnp.int32, value.shape, 1)
        odd = (lane_index(value.shape) >= LANES).astype(jnp.int32)
        grid_row = row0 - 1 + 2 * pair + odd
        grid_col = col0 - 1 + col
        keep = (
            (grid_row >= 0) & (grid_row < limits[0])
            & (grid_col >= 0) & (grid_col < limits[1]) & (col < SIDE + 2)
        )
        value = jnp.where(keep, value, 0.0)
        hid[:, 0] = value[:, :, :LANES]
        hid[:, 1] = value[:, :, LANES:]
        for b in range(3):
            hid_sh[b] = hid[:, :, b : b + SIDE, :].astype(HALF)
        value = product(gather_pairs(hid_sh, 0, half), w_out[...])
        center = jnp.concatenate(
            [state_sh[2, 1 : 1 + half, v, :SIDE, :] for v in (0, 1)], axis=-1
        ).astype(FULL).reshape(half * SIDE, 2 * LANES)
        mean = (center + value + b_out[...]).astype(HALF).astype(FULL)
        state[...] = mean + noise_ref[0].astype(FULL)
        pad[...] = jnp.zeros(pad.shape, FULL)
        deal = half // CHUNKS
        trips = jnp.where(who_ref[0] >= 0, CHUNKS, 0)

        def fill(source, first, count):
            shaped = source.reshape(count, SIDE, 2 * LANES)
            pad[pl.ds(first, count), 1, 8 : 8 + SIDE] = shaped[:, :, :LANES]
            pad[pl.ds(first + 1, count), 0, 8 : 8 + SIDE] = shaped[:, :, LANES:]

        def shift():
            for b in range(3):
                pad_sh[b] = pad[:, :, 7 + b : 7 + b + SIDE, :].astype(HALF)

        for step in range(steps):
            fill(state[...], 0, half)
            shift()

            def first(c, carry, step=step):
                value = product(gather_pairs(pad_sh, c * deal, deal), d_in[...])
                fill(silu(value + b_step[step : step + 1]), c * deal, deal)
                return carry

            lax.fori_loop(0, trips, first, 0)
            shift()

            def second(c, carry, step=step):
                value = product(gather_pairs(pad_sh, c * deal, deal), d_out[...])
                cells = pl.ds(pl.multiple_of(c * deal * SIDE, deal * SIDE), deal * SIDE)
                value = state[cells] - 0.5 * (value + b_den[...])
                if step + 1 < steps:
                    value = value + 0.5 * noise_ref[step + 1, cells].astype(FULL)
                state[cells] = value
                return carry

            lax.fori_loop(0, trips, second, 0)
        change = (state[...] - mean).reshape(half, SIDE, 2 * LANES)
        corr[:, 0] = change[:, :, :LANES]
        corr[:, 1] = change[:, :, LANES:]
        cells = corr[...].reshape(SIDE * SIDE, LANES)
        for t in range(SIDE * SIDE // LANES):
            lanes = slice(t * LANES, (t + 1) * LANES)
            out_ref[:, lanes] = cells[lanes].T[:padded].astype(HALF)

    return run(
        body,
        [like((padded, SIDE * SIDE))],
        [who, anchor, *addends, noise, *weights, *biases[:2], step_bias, biases[2]],
        [
            pltpu.VMEM((TILES * LANES, LANES), FULL),
            pltpu.VMEM((3, WIDE // 2, 2, loose, LANES), HALF),
            pltpu.VMEM((half + 1, 2, loose, LANES), FULL),
            pltpu.VMEM((3, half + 1, 2, SIDE, LANES), HALF),
            pltpu.VMEM((half + 1, 2, loose, LANES), FULL),
            pltpu.VMEM((3, half + 1, 2, SIDE, LANES), HALF),
            pltpu.VMEM((half, 2, SIDE, LANES), FULL),
            pltpu.VMEM((half * SIDE, 2 * LANES), FULL),
        ],
        micros=8.0,
        scalars=2,
    )[0]


def spread(turned, right, left):
    rows, _, cols = turned.shape
    span = right.shape[1]
    loose = cols + 16

    def body(rows_ref, right_ref, left_ref, out_ref, after, before, line):
        def upright(value):
            value = value.astype(FULL)
            return jnp.concatenate(
                [value, jnp.zeros((LANES - value.shape[0], value.shape[1]), FULL)], axis=0
            ).T

        for t in range(span // LANES):
            lanes = slice(t * LANES, (t + 1) * LANES)
            after[lanes] = upright(right_ref[:, lanes])
        before[...] = upright(left_ref[...])
        line[...] = jnp.zeros(line.shape, FULL)

        def spread_rows(i, carry):
            for v in range(2):
                r = 2 * i + v
                line[v, 8 : 8 + cols] = upright(rows_ref[r])
                line[v, 8 + cols : 10 + cols] = after[pl.ds(r * REACH, 2)]
                line[v, 6:8] = before[pl.ds(2 * r, 2)]
                for b in range(3):
                    out_ref[b, i, v] = line[v, 6 + b : 6 + b + loose, :].astype(HALF)
            return carry

        lax.fori_loop(0, rows // 2, spread_rows, 0)

    return run(
        body,
        [like((3, rows // 2, 2, loose, LANES))],
        [turned, right, left],
        [
            pltpu.VMEM((span, LANES), FULL),
            pltpu.VMEM((LANES, LANES), FULL),
            pltpu.VMEM((2, loose + 8, LANES), FULL),
        ],
        micros=2.5,
        scalars=0,
    )[0]


def grid_mean(who, shifted, rim, lower, padded, weights, biases, limits):
    rows = 2 * shifted.shape[1]
    _, deep, width = rim.shape
    cols = width - LANES
    loose = cols + 16
    made = rows // 2
    pairs_in, pairs_out = made // 4 + 1, made // 4
    hidden_pairs = made // 2 + 1
    if hidden_pairs % pairs_in:
        hidden_pairs += pairs_in - hidden_pairs % pairs_in
    state_pairs = hidden_pairs + 1
    base = rows - made - 2 if lower else -2

    def body(who_ref, shifted_ref, rim_ref, w_in, w_out, b_in, b_out, out_ref,
             line, state_sh, hid, hid_sh):
        row0 = who_ref[0] * rows + base + 1
        col0 = who_ref[1] * cols - 1

        for pair in range(made // 2 + 2, state_pairs):
            for b in range(3):
                state_sh[b, pair] = jnp.zeros((2, loose, LANES), HALF)
        edge = made // 2 + 1 if lower else 0
        skip = 0 if lower else 1
        given = made // 2 + 1
        at = (rows - made) // 2 - 1 if lower else 0
        for b in range(3):
            state_sh[b, skip : skip + given] = shifted_ref[b, at : at + given]
        for v in range(2):
            value = jnp.concatenate(
                [rim_ref[v].astype(FULL), jnp.zeros((LANES - deep, width), FULL)], axis=0
            ).T
            line[v, 8 : 8 + cols] = value[:cols]
            line[v, 8 + cols :] = value[cols : cols + 16]
            line[v, :8] = value[width - 8 :]
            for b in range(3):
                state_sh[b, edge, v] = line[v, 6 + b : 6 + b + loose, :].astype(HALF)

        def first(chunk, carry):
            start = chunk * pairs_in
            value = product(gather_pairs(state_sh, start, pairs_in), w_in[...])
            value = silu(value + b_in[...]).reshape(pairs_in, loose, 2 * LANES)
            pair = lax.broadcasted_iota(jnp.int32, value.shape, 0)
            col = lax.broadcasted_iota(jnp.int32, value.shape, 1)
            odd = (lane_index(value.shape) >= LANES).astype(jnp.int32)
            grid_row = row0 + 2 * (start + pair) + odd
            grid_col = col0 + col
            keep = (
                (grid_row >= 0) & (grid_row < limits[0])
                & (grid_col >= 0) & (grid_col < limits[1])
            )
            value = jnp.where(keep, value, 0.0)
            hid[:, 0] = value[:, :, :LANES]
            hid[:, 1] = value[:, :, LANES:]
            for b in range(3):
                hid_sh[b, pl.ds(start, pairs_in)] = hid[:, :, b : b + cols, :].astype(HALF)
            return carry

        lax.fori_loop(0, hidden_pairs // pairs_in, first, 0)

        def second(chunk, carry):
            start = chunk * pairs_out
            value = product(gather_pairs(hid_sh, start, pairs_out), w_out[...]) + b_out[...]
            value = value.reshape(pairs_out, cols, 2 * LANES)
            for k in range(pairs_out):
                for v in range(2):
                    center = state_sh[2, start + k + 1, v, :cols, :].astype(FULL)
                    mean = center + value[k, :, v * LANES : (v + 1) * LANES]
                    out_ref[2 * (start + k) + v] = mean.T[:padded].astype(HALF)
            return carry

        lax.fori_loop(0, made // 2 // pairs_out, second, 0)

    return run(
        body,
        [like((made, padded, cols))],
        [who, shifted, rim, *weights, *biases],
        [
            pltpu.VMEM((2, loose + 8, LANES), FULL),
            pltpu.VMEM((3, state_pairs, 2, loose, LANES), HALF),
            pltpu.VMEM((pairs_in, 2, loose, LANES), FULL),
            pltpu.VMEM((3, hidden_pairs, 2, cols, LANES), HALF),
        ],
        micros=3.5,
    )[0]


def canvas(who, anchor, pieces, sources, place, sects, rows, cols):
    padded = pieces[0].shape[-2]
    deep = -(-padded // 16) * 16
    total = anchor.shape[1]
    slots = len(pieces)
    tile_rows = LANES // SIDE
    groups = rows // tile_rows

    def body(who_ref, at_ref, *refs):
        place_ref, spill_ref, out_ref, inverse_ref, view = refs[slots:]
        none = jnp.zeros((padded, LANES), HALF)
        for piece, j in zip(refs, sources):
            lanes = slice(j * LANES, (j + 1) * LANES)
            row0 = slot_at(who_ref, at_ref, j, sects, rows, cols)[0]
            for r in range(rows):
                i = r - row0
                tile = jnp.clip(jnp.right_shift(i, tile_rows.bit_length() - 1), 0, SIDE // tile_rows - 1)
                value = piece[:, pl.ds(pl.multiple_of(tile * LANES, LANES), LANES)]
                inside = (i >= 0) & (i < SIDE)
                view[r % tile_rows, r // tile_rows, :padded, lanes] = jnp.where(
                    inside, value, none
                )
        view[:, :, padded:, :] = jnp.zeros(
            (tile_rows, groups, deep - padded, slots * LANES), HALF
        )
        spilled = None
        for m in range(tile_rows):
            value = jnp.dot(
                view[m].reshape(groups * deep, slots * LANES), place_ref[m],
                preferred_element_type=FULL,
            ).reshape(groups, deep, 2 * LANES)
            for k in range(groups):
                out_ref[k * tile_rows + m] = value[k, :padded, :LANES]
            part = value[:, :padded, LANES:]
            spilled = part if spilled is None else spilled + part
        for k in range(groups):
            spill_ref[:, k * LANES : (k + 1) * LANES] = spilled[k].astype(HALF)
        row = lax.broadcasted_iota(jnp.int32, (rows, cols), 0) + who_ref[0] * rows
        col = lane_index((rows, cols)) + who_ref[1] * cols

        def cover(p, count):
            down, across = row - at_ref[0, p], col - at_ref[1, p]
            hit = (down >= 0) & (down < SIDE) & (across >= 0) & (across < SIDE)
            return count + jnp.where(hit, 1.0, 0.0)

        count = lax.fori_loop(0, total, cover, jnp.zeros((rows, cols), FULL))
        inverse_ref[...] = 1.0 / jnp.maximum(count, 1.0)

    return run(
        body,
        [
            like((padded, rows * SIDE)),
            like((rows, padded, cols), FULL),
            like((rows, cols), FULL),
        ],
        [who, anchor, *pieces, place],
        [pltpu.VMEM((tile_rows, groups, deep, slots * LANES), HALF)],
        micros=1.5,
        scalars=2,
    )


def finish(means, summed, arrived, inverse, channels):
    rows, padded, cols = summed.shape
    deep = -(-padded // 16) * 16
    half = means[0].shape[0]

    def body(top_ref, low_ref, sum_ref, spill_ref, inverse_ref, out_ref, flat):
        lane = lane_index((padded, LANES))
        none = jnp.zeros((padded, LANES), HALF)
        flat[:, padded:] = jnp.zeros((rows, deep - padded, cols), HALF)
        for r in range(rows):
            at, low = divmod(r * SIDE, LANES)
            extra = spill_ref[:, at * LANES : (at + 1) * LANES]
            if low:
                extra = pltpu.roll(extra, LANES - low, 1)
            extra = jnp.where(lane < SIDE, extra, none).astype(FULL)
            mean = top_ref[r] if r < half else low_ref[r - half]
            value = mean.astype(FULL) + (sum_ref[r] + extra) * inverse_ref[r : r + 1]
            flat[r, :padded] = value.astype(HALF)
        out_ref[...] = jnp.swapaxes(flat[...], 0, 1)[:channels]

    return run(
        body,
        [like((channels, rows, cols))],
        [*means, summed, arrived, inverse],
        [pltpu.VMEM((rows, deep, cols), HALF)],
        micros=3.0,
        scalars=0,
    )[0]


def step(
    state_field,
    conv_in_weight,
    conv_in_bias,
    conv_out_weight,
    conv_out_bias,
    patch_anchor,
    patch_noise,
    denoise_in_weight,
    step_bias,
    denoise_out_weight,
    denoise_bias,
):
    bands = lax.axis_size("band")
    sects = lax.axis_size("sect")
    channels, rows, cols = state_field.shape
    limits = (rows * bands, cols * sects)
    who = jnp.stack([lax.axis_index("band"), lax.axis_index("sect")]).astype(jnp.int32)

    anchor = patch_anchor.T

    right_rim, left_rim, turned = pack(who, anchor, state_field)
    right = shift_from(right_rim, "sect", -1)
    left = shift_from(left_rim, "sect", 1)

    made, lines, noise, pick, place = prep(
        who,
        anchor,
        [
            conv_in_weight.transpose(0, 2, 1),
            conv_out_weight,
            denoise_in_weight.transpose(0, 2, 1),
            denoise_out_weight,
        ],
        [conv_in_bias[None, :], conv_out_bias[None, :], denoise_bias[None, :], step_bias],
        patch_noise[0],
        bands,
        sects,
        rows,
        cols,
    )
    biases, step_lines = lines[:3], lines[3]

    kept, sent, top, low = extract(who, anchor, turned, right, left, pick, bands, sects)
    got = swap(sent, "band", 1)
    addends = [kept, got]
    bit = 2
    while bit < bands:
        odd = add_parts(kept, got, 1)
        kept = add_parts(kept, got, 0) if 2 * bit < bands else kept
        got = swap(odd, "band", bit)
        addends.append(got)
        bit *= 2
    above = shift_from(low, "band", 1)
    below = shift_from(top, "band", -1)
    correction = patch_step(who, anchor, addends, noise, made, biases, step_lines, sects, limits)
    pieces = [correction]
    sources = [0]
    bit = bands // 2
    while bit:
        fresh = []
        for piece in pieces:
            fresh.append(swap(piece, "band", bit))
        pieces += fresh
        sources += [s ^ bit for s in sources]
        bit //= 2

    shifted = spread(turned, right, left)
    padded = right.shape[0]
    top_mean = grid_mean(who, shifted, above, False, padded, made[:2], biases[:2], limits)
    low_mean = grid_mean(who, shifted, below, True, padded, made[:2], biases[:2], limits)
    spilled, summed, inverse = canvas(
        who, anchor, pieces, sources, place, sects, rows, cols
    )
    arrived = shift_from(spilled, "sect", 1)
    return finish([top_mean, low_mean], summed, arrived, inverse, channels)


def solution(mesh):
    placed = (
        P("groups", "band", "sect"),
        P(),
        P(),
        P(),
        P(),
        P("groups", None),
        P(("groups", "band", "sect"), None, None, None),
        P(),
        P(),
        P(),
        P(),
    )
    return jax.shard_map(
        step,
        mesh=mesh,
        in_specs=placed,
        out_specs=P("groups", "band", "sect"),
        check_vma=False,
    )
```

```python
import jax
import jax.numpy as jnp
from jax import lax
from jax.experimental import pallas as pl
from jax.experimental.pallas import tpu as pltpu
from jax.sharding import PartitionSpec as P


SIDE = 32
WIDE = SIDE + 4
PER_TILE = 3
TILES = WIDE // PER_TILE
LANES = 128
REACH = SIDE + 2
CHUNKS = 1
HALF = jnp.bfloat16
FULL = jnp.float32


def shift_from(block, axis, distance):
    count = lax.axis_size(axis)
    route = [(i - distance, i) for i in range(count) if 0 <= i - distance < count]
    return lax.ppermute(block, axis, route)


def swap(block, axis, bit):
    count = lax.axis_size(axis)
    return lax.ppermute(block, axis, [(i, i ^ bit) for i in range(count)])


def run(body, outs, ins, scratch, micros=1.0, scalars=1, limit=16):
    smem = pl.BlockSpec(memory_space=pltpu.SMEM)
    vmem = pl.BlockSpec(memory_space=pltpu.VMEM)
    return pl.pallas_call(
        body,
        out_shape=outs,
        in_specs=[smem] * scalars + [vmem] * (len(ins) - scalars),
        out_specs=[vmem] * len(outs),
        scratch_shapes=scratch,
        cost_estimate=pl.CostEstimate(
            flops=int(micros * 1.15e9), bytes_accessed=1024, transcendentals=0
        ),
        compiler_params=pltpu.CompilerParams(vmem_limit_bytes=limit * 1024 * 1024),
    )(*ins)


def slot_at(who_ref, at_ref, j, sects, rows, cols):
    reader = jnp.bitwise_xor(who_ref[0], j) * sects + who_ref[1]
    return at_ref[0, reader] - who_ref[0] * rows, at_ref[1, reader] - who_ref[1] * cols


def like(shape, dtype=HALF):
    return jax.ShapeDtypeStruct(shape, dtype)


def lane_index(shape):
    return lax.broadcasted_iota(jnp.int32, shape, len(shape) - 1)


def turn_rows(state_ref, flat):
    channels = state_ref.shape[0]
    flat[:channels] = state_ref[...]
    flat[channels:] = jnp.zeros((flat.shape[0] - channels,) + flat.shape[1:], HALF)
    return jnp.swapaxes(flat[...], 0, 1)


def pack(who, state):
    channels, rows, cols = state.shape
    padded = -(-channels // 8) * 8
    deep = -(-padded // 16) * 16
    span = -(-rows * REACH // LANES)

    def body(who_ref, state_ref, right_ref, left_ref, rows_ref, flat):
        turned = turn_rows(state_ref, flat)
        rows_ref[...] = turned
        lane = lane_index((deep, LANES))
        tiles = [None] * span
        rim = jnp.zeros((deep, LANES), HALF)
        for r in range(rows):
            row = turned[r]
            at, off = divmod(r * REACH, LANES)
            moved = row if off == 0 else pltpu.roll(row, off, 1)
            if tiles[at] is None:
                tiles[at] = moved
            else:
                tiles[at] = jnp.where(lane >= off, moved, tiles[at])
            if off + REACH > LANES:
                tiles[at + 1] = moved
            moved = pltpu.roll(row, (2 * r + 2) % LANES, 1)
            rim = jnp.where((lane >= 2 * r) & (lane < 2 * r + 2), moved, rim)
        for at in range(span):
            right_ref[:, at * LANES : (at + 1) * LANES] = tiles[at][:padded]
        left_ref[...] = rim[:padded]

    return run(
        body,
        [like((padded, span * LANES)), like((padded, LANES)), like((rows, deep, cols))],
        [who, state],
        [pltpu.VMEM((deep, rows, cols), HALF)],
        micros=1.0,
    )


def prep(who, anchor, weights, biases, noise, bands, sects, rows, cols):
    steps, channels, cells = noise.shape
    count = len(weights)
    tile_rows = LANES // SIDE
    lines = len(biases)
    width = cols + LANES

    def body(who_ref, at_ref, *refs):
        ins, lines_in, noise_ref = refs[:count], refs[count : count + lines], refs[count + lines]
        outs = refs[count + lines + 1 :]
        lines_out, noise_out = outs[count : count + lines], outs[count + lines]
        pick_ref, place_ref = outs[count + lines + 1 :]
        for k, (w_ref, o_ref) in enumerate(zip(ins, outs)):
            _, down, across = w_ref.shape
            o_ref[...] = jnp.zeros(o_ref.shape, HALF)
            for v in range(2):
                for a in range(3):
                    for b in range(3):
                        tap = (3 * (a + v) + b) * LANES
                        row, col = (v * LANES, tap) if k % 2 else (tap, v * LANES)
                        o_ref[row : row + down, col : col + across] = w_ref[3 * a + b]
        for line_ref, o_ref in zip(lines_in, lines_out):
            used = line_ref.shape[1]
            o_ref[...] = jnp.zeros(o_ref.shape, FULL)
            o_ref[:, :used] = line_ref[...]
            o_ref[:, LANES : LANES + used] = line_ref[...]
        for k in range(steps):
            for t in range(cells // LANES):
                block = noise_ref[k, :, t * LANES : (t + 1) * LANES].astype(FULL)
                block = jnp.concatenate(
                    [block, jnp.zeros((LANES - channels, LANES), FULL)], axis=0
                ).T.astype(HALF)
                for m in range(tile_rows):
                    r = t * tile_rows + m
                    noise_out[
                        k, r // 2 * SIDE : (r // 2 + 1) * SIDE, r % 2 * LANES : (r % 2 + 1) * LANES
                    ] = block[m * SIDE : (m + 1) * SIDE]
        source = lax.broadcasted_iota(jnp.int32, (width, LANES), 0)
        inner = lane_index((width, LANES))
        for _ in range(1, PER_TILE):
            inner = jnp.where(inner >= WIDE, inner - WIDE, inner)
        cell = lax.broadcasted_iota(jnp.int32, (LANES, 2 * LANES), 0)
        target = lane_index((LANES, 2 * LANES))
        for j in range(bands):
            row0, col0 = slot_at(who_ref, at_ref, j, sects, rows, cols)
            want = jnp.bitwise_and(inner + (col0 - 2), width - 1)
            pick_ref[:, j * LANES : (j + 1) * LANES] = jnp.where(source == want, 1.0, 0.0).astype(HALF)
            across = jnp.bitwise_and(cell, SIDE - 1) + col0
            for m in range(tile_rows):
                turn = jnp.bitwise_and(m - row0, tile_rows - 1)
                there = jnp.where(across < cols, across, across - cols + LANES + m * SIDE)
                hit = (target == there) & (cell >= turn * SIDE) & (cell < (turn + 1) * SIDE)
                place_ref[m, j * LANES : (j + 1) * LANES] = jnp.where(hit, 1.0, 0.0).astype(HALF)

    sizes = [(12 * LANES, 2 * LANES), (2 * LANES, 12 * LANES)]
    made = [like(sizes[k % 2]) for k in range(count)]
    made += [like((line.shape[0], 2 * LANES), FULL) for line in biases]
    made += [like((steps, cells // 2, 2 * LANES))]
    made += [like((width, bands * LANES)), like((tile_rows, bands * LANES, 2 * LANES))]
    out = run(body, made, [who, anchor, *weights, *biases, noise], [], micros=2.5, scalars=2)
    return out[:count], out[count : count + lines], *out[count + lines :]


def add_parts(kept, got):
    def body(kept_ref, got_ref, out_ref):
        out_ref[...] = kept_ref[...] + got_ref[...]

    return run(body, [like(kept.shape)], [kept, got], [], micros=0.3, scalars=0)[0]


def window_tile(picked, t, row0, rows, padded, lanes):
    zone = lane_index((padded, LANES))
    total = jnp.zeros((padded, LANES), FULL)
    for m in range(PER_TILE):
        r = row0 + t * PER_TILE + m
        low = jnp.where((r >= 0) & (r < rows), WIDE * m, 2 * LANES)
        keep = (zone >= low) & (zone < WIDE * (m + 1))
        value = picked[jnp.clip(r, 0, rows - 1), :padded, lanes]
        total = jnp.where(keep, value, total)
    return total.astype(HALF)


def batches(bands):
    size = 4 if bands % 4 == 0 else bands
    return [range(first, first + size) for first in range(0, bands, size)], size


def select_rows(source, pick, picked):
    rows, deep, _ = source.shape
    chunk = rows // 2

    def select(c, carry):
        view = source[pl.ds(c * chunk, chunk)].reshape(chunk * deep, LANES)
        picked[pl.ds(c * chunk, chunk)] = jnp.dot(
            view, pick, preferred_element_type=FULL
        ).reshape(chunk, deep, pick.shape[1])
        return carry

    lax.fori_loop(0, rows // chunk, select, 0)


def extract_own(who, anchor, turned, pick, padded, bands, sects):
    rows, deep, cols = turned.shape
    groups, size = batches(bands)

    def body(who_ref, at_ref, rows_ref, pick_ref, out_ref, picked):
        for group in groups:
            select_rows(rows_ref, pick_ref[:cols, group[0] * LANES : (group[-1] + 1) * LANES], picked)
            for j in group:
                row0 = slot_at(who_ref, at_ref, j, sects, rows, cols)[0] - 2
                inside = (row0 > -WIDE) & (row0 < rows)

                @pl.when(inside)
                def _(j=j, row0=row0, at=(j - group[0]) * LANES):
                    for t in range(TILES):
                        out_ref[j, :, t * LANES : (t + 1) * LANES] = window_tile(
                            picked, t, row0, rows, padded, slice(at, at + LANES)
                        )

                @pl.when(jnp.logical_not(inside))
                def _(j=j):
                    out_ref[j] = jnp.zeros((padded, TILES * LANES), HALF)

    return run(
        body,
        [like((bands, padded, TILES * LANES))],
        [who, anchor, turned, pick],
        [pltpu.VMEM((rows, deep, size * LANES), FULL)],
        micros=1.5,
        scalars=2,
    )[0]


def extract_rim(who, anchor, parts, turned, right, left, pick, bands, sects):
    rows, deep, cols = turned.shape
    padded = right.shape[0]
    groups, size = batches(bands)

    def body(who_ref, at_ref, part_ref, rows_ref, right_ref, left_ref, pick_ref,
             own_ref, low_ref, odd_ref, high_ref, near_ref, cross_ref, ext, picked):
        lane = lane_index((padded, LANES))
        none = jnp.zeros((padded, LANES), HALF)
        rim = left_ref[...]

        def expand(r):
            at, off = divmod(r * REACH, LANES)
            piece = right_ref[:, at * LANES : (at + 1) * LANES]
            if off:
                piece = pltpu.roll(piece, LANES - off, 1)
            if off + REACH > LANES:
                after = right_ref[:, (at + 1) * LANES : (at + 2) * LANES]
                piece = jnp.where(lane < LANES - off, piece, pltpu.roll(after, LANES - off, 1))
            turn = pltpu.roll(rim, (LANES - 2 - 2 * r) % LANES, 1)
            ext[r, :padded] = jnp.where(
                lane < REACH, piece, jnp.where(lane >= LANES - 2, turn, none)
            )

        ext[:, padded:] = jnp.zeros((rows, deep - padded, LANES), HALF)
        outer = (0, 1, rows - 2, rows - 1)
        for r in outer:
            expand(r)
        even = jnp.bitwise_and(who_ref[0], 1) == 0
        for k in range(2):
            top, low = k, rows - 2 + k
            near_ref[k, :, :cols] = jnp.where(even, rows_ref[low], rows_ref[top])
            near_ref[k, :, cols:] = jnp.where(even, ext[low], ext[top])
            cross_ref[k, :, :cols] = jnp.where(even, rows_ref[top], rows_ref[low])
            cross_ref[k, :, cols:] = jnp.where(even, ext[top], ext[low])

        def target(j):
            if j < 2:
                return (own_ref, odd_ref)[j], 0
            return (low_ref, high_ref)[j % 2], j // 2 - 1

        crossing = []
        for j in range(bands):
            row0, col0 = slot_at(who_ref, at_ref, j, sects, rows, cols)
            row0 = row0 - 2
            inside = (row0 > -WIDE) & (row0 < rows)
            over = inside & ((col0 < 2) | (col0 > cols - REACH))
            crossing.append((row0, over))
            out_ref, at = target(j)
            out_ref[at] = part_ref[j]
        for group in groups:
            some = crossing[group[0]][1]
            for j in group[1:]:
                some = some | crossing[j][1]

            @pl.when(some)
            def _(group=group):
                if group[0] == 0:
                    for r in range(rows):
                        if r not in outer:
                            expand(r)
                else:
                    for r in range(rows):
                        expand(r)
                select_rows(
                    ext, pick_ref[cols:, group[0] * LANES : (group[-1] + 1) * LANES], picked
                )
                for j in group:
                    out_ref, at = target(j)
                    row0, over = crossing[j]

                    @pl.when(over)
                    def _(j=j, out_ref=out_ref, at=at, row0=row0, first=(j - group[0]) * LANES):
                        for t in range(TILES):
                            out_ref[at, :, t * LANES : (t + 1) * LANES] += window_tile(
                                picked, t, row0, rows, padded, slice(first, first + LANES)
                            )

    one = like((1, padded, TILES * LANES))
    rest = like((max(bands // 2 - 1, 1), padded, TILES * LANES))
    edge = like((2, deep, cols + LANES))
    return run(
        body,
        [one, rest, one, rest, edge, edge],
        [who, anchor, parts, turned, right, left, pick],
        [pltpu.VMEM((rows, deep, LANES), HALF), pltpu.VMEM((rows, deep, size * LANES), FULL)],
        micros=1.5,
        scalars=2,
    )


def product(view, weight):
    turned = weight.shape[0] == 2 * LANES
    return lax.dot_general(
        view, weight, (((1,), (1 if turned else 0,)), ((), ())), preferred_element_type=FULL
    )


def gather_pairs(shifted, first, count):
    view = jnp.concatenate(
        [shifted[b, pl.ds(first + u, count), v] for u in (0, 1) for v in (0, 1) for b in (0, 1, 2)],
        axis=-1,
    )
    return view.reshape(count * view.shape[1], view.shape[2])


def silu(value):
    return value / (1.0 + jnp.exp(-value))


def patch_step(who, anchor, addends, noise, weights, biases, step_bias, sects, limits):
    padded = addends[0].shape[1]
    steps = noise.shape[0]
    half = SIDE // 2
    loose = 48

    def body(*refs):
        who_ref, at_ref = refs[:2]
        parts = refs[2 : 2 + len(addends)]
        mine = who_ref[0] * sects + who_ref[1]
        row0, col0 = at_ref[0, mine], at_ref[1, mine]
        (noise_ref, w_in, w_out, d_in, d_out, b_in, b_out, b_step, b_den, out_ref,
         flat, state_sh, hid, hid_sh, pad, pad_sh, corr, state) = refs[2 + len(addends) :]
        for t in range(TILES):
            lanes = slice(t * LANES, (t + 1) * LANES)
            tile = parts[0][0, :, lanes].astype(FULL)
            for part in parts[1:]:
                tile = tile + part[0, :, lanes].astype(FULL)
            tile = jnp.concatenate([tile, jnp.zeros((LANES - padded, LANES), FULL)], axis=0)
            flat[lanes, :] = tile.T
        for i in range(WIDE):
            t, m = divmod(i, PER_TILE)
            off = t * LANES + m * WIDE
            for b in range(3):
                state_sh[b, i // 2, i % 2] = flat[off + b : off + b + loose, :].astype(HALF)
        pairs = half + 1
        value = product(gather_pairs(state_sh, 0, pairs), w_in[...])
        value = silu(value + b_in[...]).reshape(pairs, loose, 2 * LANES)
        pair = lax.broadcasted_iota(jnp.int32, value.shape, 0)
        col = lax.broadcasted_iota(jnp.int32, value.shape, 1)
        odd = (lane_index(value.shape) >= LANES).astype(jnp.int32)
        grid_row = row0 - 1 + 2 * pair + odd
        grid_col = col0 - 1 + col
        keep = (
            (grid_row >= 0) & (grid_row < limits[0])
            & (grid_col >= 0) & (grid_col < limits[1]) & (col < SIDE + 2)
        )
        value = jnp.where(keep, value, 0.0)
        hid[:, 0] = value[:, :, :LANES]
        hid[:, 1] = value[:, :, LANES:]
        for b in range(3):
            hid_sh[b] = hid[:, :, b : b + SIDE, :].astype(HALF)
        value = product(gather_pairs(hid_sh, 0, half), w_out[...])
        center = jnp.concatenate(
            [state_sh[2, 1 : 1 + half, v, :SIDE, :] for v in (0, 1)], axis=-1
        ).astype(FULL).reshape(half * SIDE, 2 * LANES)
        mean = (center + value + b_out[...]).astype(HALF).astype(FULL)
        state[...] = mean + noise_ref[0].astype(FULL)
        pad[...] = jnp.zeros(pad.shape, FULL)
        deal = half // CHUNKS
        trips = jnp.where(who_ref[0] >= 0, CHUNKS, 0)

        def fill(source, first, count):
            shaped = source.reshape(count, SIDE, 2 * LANES)
            pad[pl.ds(first, count), 1, 8 : 8 + SIDE] = shaped[:, :, :LANES]
            pad[pl.ds(first + 1, count), 0, 8 : 8 + SIDE] = shaped[:, :, LANES:]

        def shift():
            for b in range(3):
                pad_sh[b] = pad[:, :, 7 + b : 7 + b + SIDE, :].astype(HALF)

        for step in range(steps):
            fill(state[...], 0, half)
            shift()

            def first(c, carry, step=step):
                value = product(gather_pairs(pad_sh, c * deal, deal), d_in[...])
                fill(silu(value + b_step[step : step + 1]), c * deal, deal)
                return carry

            lax.fori_loop(0, trips, first, 0)
            shift()

            def second(c, carry, step=step):
                value = product(gather_pairs(pad_sh, c * deal, deal), d_out[...])
                cells = pl.ds(pl.multiple_of(c * deal * SIDE, deal * SIDE), deal * SIDE)
                value = state[cells] - 0.5 * (value + b_den[...])
                if step + 1 < steps:
                    value = value + 0.5 * noise_ref[step + 1, cells].astype(FULL)
                state[cells] = value
                return carry

            lax.fori_loop(0, trips, second, 0)
        change = (state[...] - mean).reshape(half, SIDE, 2 * LANES)
        corr[:, 0] = change[:, :, :LANES]
        corr[:, 1] = change[:, :, LANES:]
        cells = corr[...].reshape(SIDE * SIDE, LANES)
        for t in range(SIDE * SIDE // LANES):
            lanes = slice(t * LANES, (t + 1) * LANES)
            out_ref[:, lanes] = cells[lanes].T[:padded].astype(HALF)

    return run(
        body,
        [like((padded, SIDE * SIDE))],
        [who, anchor, *addends, noise, *weights, *biases[:2], step_bias, biases[2]],
        [
            pltpu.VMEM((TILES * LANES, LANES), FULL),
            pltpu.VMEM((3, WIDE // 2, 2, loose, LANES), HALF),
            pltpu.VMEM((half + 1, 2, loose, LANES), FULL),
            pltpu.VMEM((3, half + 1, 2, SIDE, LANES), HALF),
            pltpu.VMEM((half + 1, 2, loose, LANES), FULL),
            pltpu.VMEM((3, half + 1, 2, SIDE, LANES), HALF),
            pltpu.VMEM((half, 2, SIDE, LANES), FULL),
            pltpu.VMEM((half * SIDE, 2 * LANES), FULL),
        ],
        micros=8.0,
        scalars=2,
    )[0]


def spread(turned, right, left):
    rows, _, cols = turned.shape
    span = right.shape[1]
    loose = cols + 16

    def body(rows_ref, right_ref, left_ref, out_ref, after, before, line):
        def upright(value):
            value = value.astype(FULL)
            return jnp.concatenate(
                [value, jnp.zeros((LANES - value.shape[0], value.shape[1]), FULL)], axis=0
            ).T

        for t in range(span // LANES):
            lanes = slice(t * LANES, (t + 1) * LANES)
            after[lanes] = upright(right_ref[:, lanes])
        before[...] = upright(left_ref[...])
        line[...] = jnp.zeros(line.shape, FULL)

        def spread_rows(i, carry):
            for v in range(2):
                r = 2 * i + v
                line[v, 8 : 8 + cols] = upright(rows_ref[r])
                line[v, 8 + cols : 10 + cols] = after[pl.ds(r * REACH, 2)]
                line[v, 6:8] = before[pl.ds(2 * r, 2)]
                for b in range(3):
                    out_ref[b, i, v] = line[v, 6 + b : 6 + b + loose, :].astype(HALF)
            return carry

        lax.fori_loop(0, rows // 2, spread_rows, 0)

    return run(
        body,
        [like((3, rows // 2, 2, loose, LANES))],
        [turned, right, left],
        [
            pltpu.VMEM((span, LANES), FULL),
            pltpu.VMEM((LANES, LANES), FULL),
            pltpu.VMEM((2, loose + 8, LANES), FULL),
        ],
        micros=2.5,
        scalars=0,
    )[0]


def grid_mean(who, shifted, near, cross, lower, padded, weights, biases, limits):
    rows = 2 * shifted.shape[1]
    _, deep, width = near.shape
    cols = width - LANES
    loose = cols + 16
    made = rows // 2
    pairs_in, pairs_out = made // 4 + 1, made // 4
    hidden_pairs = made // 2 + 1
    if hidden_pairs % pairs_in:
        hidden_pairs += pairs_in - hidden_pairs % pairs_in
    state_pairs = hidden_pairs + 1
    base = rows - made - 2 if lower else -2

    def body(who_ref, shifted_ref, near_ref, cross_ref, w_in, w_out, b_in, b_out, out_ref,
             line, state_sh, hid, hid_sh):
        row0 = who_ref[0] * rows + base + 1
        col0 = who_ref[1] * cols - 1

        for pair in range(made // 2 + 2, state_pairs):
            for b in range(3):
                state_sh[b, pair] = jnp.zeros((2, loose, LANES), HALF)
        edge = made // 2 + 1 if lower else 0
        skip = 0 if lower else 1
        given = made // 2 + 1
        at = (rows - made) // 2 - 1 if lower else 0
        for b in range(3):
            state_sh[b, skip : skip + given] = shifted_ref[b, at : at + given]
        pair = jnp.bitwise_and(who_ref[0], 1) == (0 if lower else 1)
        for v in range(2):
            rim = jnp.where(pair, near_ref[v], cross_ref[v])
            value = jnp.concatenate(
                [rim.astype(FULL), jnp.zeros((LANES - deep, width), FULL)], axis=0
            ).T
            line[v, 8 : 8 + cols] = value[:cols]
            line[v, 8 + cols :] = value[cols : cols + 16]
            line[v, :8] = value[width - 8 :]
            for b in range(3):
                state_sh[b, edge, v] = line[v, 6 + b : 6 + b + loose, :].astype(HALF)

        def first(chunk, carry):
            start = chunk * pairs_in
            value = product(gather_pairs(state_sh, start, pairs_in), w_in[...])
            value = silu(value + b_in[...]).reshape(pairs_in, loose, 2 * LANES)
            pair = lax.broadcasted_iota(jnp.int32, value.shape, 0)
            col = lax.broadcasted_iota(jnp.int32, value.shape, 1)
            odd = (lane_index(value.shape) >= LANES).astype(jnp.int32)
            grid_row = row0 + 2 * (start + pair) + odd
            grid_col = col0 + col
            keep = (
                (grid_row >= 0) & (grid_row < limits[0])
                & (grid_col >= 0) & (grid_col < limits[1])
            )
            value = jnp.where(keep, value, 0.0)
            hid[:, 0] = value[:, :, :LANES]
            hid[:, 1] = value[:, :, LANES:]
            for b in range(3):
                hid_sh[b, pl.ds(start, pairs_in)] = hid[:, :, b : b + cols, :].astype(HALF)
            return carry

        lax.fori_loop(0, hidden_pairs // pairs_in, first, 0)

        def second(chunk, carry):
            start = chunk * pairs_out
            value = product(gather_pairs(hid_sh, start, pairs_out), w_out[...]) + b_out[...]
            value = value.reshape(pairs_out, cols, 2 * LANES)
            for k in range(pairs_out):
                for v in range(2):
                    center = state_sh[2, start + k + 1, v, :cols, :].astype(FULL)
                    mean = center + value[k, :, v * LANES : (v + 1) * LANES]
                    out_ref[2 * (start + k) + v] = mean.T[:padded].astype(HALF)
            return carry

        lax.fori_loop(0, made // 2 // pairs_out, second, 0)

    return run(
        body,
        [like((made, padded, cols))],
        [who, shifted, near, cross, *weights, *biases],
        [
            pltpu.VMEM((2, loose + 8, LANES), FULL),
            pltpu.VMEM((3, state_pairs, 2, loose, LANES), HALF),
            pltpu.VMEM((pairs_in, 2, loose, LANES), FULL),
            pltpu.VMEM((3, hidden_pairs, 2, cols, LANES), HALF),
        ],
        micros=3.5,
    )[0]


def canvas(who, anchor, pieces, sources, place, sects, rows, cols):
    padded = pieces[0].shape[-2]
    deep = -(-padded // 16) * 16
    total = anchor.shape[1]
    slots = len(pieces)
    tile_rows = LANES // SIDE
    groups = rows // tile_rows

    def body(who_ref, at_ref, *refs):
        place_ref, spill_ref, out_ref, inverse_ref, view = refs[slots:]
        none = jnp.zeros((padded, LANES), HALF)
        for piece, j in zip(refs, sources):
            lanes = slice(j * LANES, (j + 1) * LANES)
            row0 = slot_at(who_ref, at_ref, j, sects, rows, cols)[0]
            for r in range(rows):
                i = r - row0
                tile = jnp.clip(jnp.right_shift(i, tile_rows.bit_length() - 1), 0, SIDE // tile_rows - 1)
                value = piece[:, pl.ds(pl.multiple_of(tile * LANES, LANES), LANES)]
                inside = (i >= 0) & (i < SIDE)
                view[r % tile_rows, r // tile_rows, :padded, lanes] = jnp.where(
                    inside, value, none
                )
        view[:, :, padded:, :] = jnp.zeros(
            (tile_rows, groups, deep - padded, slots * LANES), HALF
        )
        spilled = None
        for m in range(tile_rows):
            value = jnp.dot(
                view[m].reshape(groups * deep, slots * LANES), place_ref[m],
                preferred_element_type=FULL,
            ).reshape(groups, deep, 2 * LANES)
            for k in range(groups):
                out_ref[k * tile_rows + m] = value[k, :padded, :LANES]
            part = value[:, :padded, LANES:]
            spilled = part if spilled is None else spilled + part
        for k in range(groups):
            spill_ref[:, k * LANES : (k + 1) * LANES] = spilled[k].astype(HALF)
        row = lax.broadcasted_iota(jnp.int32, (rows, cols), 0) + who_ref[0] * rows
        col = lane_index((rows, cols)) + who_ref[1] * cols

        def cover(p, count):
            down, across = row - at_ref[0, p], col - at_ref[1, p]
            hit = (down >= 0) & (down < SIDE) & (across >= 0) & (across < SIDE)
            return count + jnp.where(hit, 1.0, 0.0)

        count = lax.fori_loop(0, total, cover, jnp.zeros((rows, cols), FULL))
        inverse_ref[...] = 1.0 / jnp.maximum(count, 1.0)

    return run(
        body,
        [
            like((padded, rows * SIDE)),
            like((rows, padded, cols), FULL),
            like((rows, cols), FULL),
        ],
        [who, anchor, *pieces, place],
        [pltpu.VMEM((tile_rows, groups, deep, slots * LANES), HALF)],
        micros=1.5,
        scalars=2,
    )


def finish(means, summed, arrived, inverse, channels):
    rows, padded, cols = summed.shape
    deep = -(-padded // 16) * 16
    half = means[0].shape[0]

    def body(top_ref, low_ref, sum_ref, spill_ref, inverse_ref, out_ref, flat):
        lane = lane_index((padded, LANES))
        none = jnp.zeros((padded, LANES), HALF)
        flat[:, padded:] = jnp.zeros((rows, deep - padded, cols), HALF)
        for r in range(rows):
            at, low = divmod(r * SIDE, LANES)
            extra = spill_ref[:, at * LANES : (at + 1) * LANES]
            if low:
                extra = pltpu.roll(extra, LANES - low, 1)
            extra = jnp.where(lane < SIDE, extra, none).astype(FULL)
            mean = top_ref[r] if r < half else low_ref[r - half]
            value = mean.astype(FULL) + (sum_ref[r] + extra) * inverse_ref[r : r + 1]
            flat[r, :padded] = value.astype(HALF)
        out_ref[...] = jnp.swapaxes(flat[...], 0, 1)[:channels]

    return run(
        body,
        [like((channels, rows, cols))],
        [*means, summed, arrived, inverse],
        [pltpu.VMEM((rows, deep, cols), HALF)],
        micros=3.0,
        scalars=0,
    )[0]


def step(
    state_field,
    conv_in_weight,
    conv_in_bias,
    conv_out_weight,
    conv_out_bias,
    patch_anchor,
    patch_noise,
    denoise_in_weight,
    step_bias,
    denoise_out_weight,
    denoise_bias,
):
    bands = lax.axis_size("band")
    sects = lax.axis_size("sect")
    channels, rows, cols = state_field.shape
    limits = (rows * bands, cols * sects)
    who = jnp.stack([lax.axis_index("band"), lax.axis_index("sect")]).astype(jnp.int32)

    anchor = patch_anchor.T

    right_rim, left_rim, turned = pack(who, state_field)
    right = shift_from(right_rim, "sect", -1)
    left = shift_from(left_rim, "sect", 1)

    made, lines, noise, pick, place = prep(
        who,
        anchor,
        [
            conv_in_weight.transpose(0, 2, 1),
            conv_out_weight,
            denoise_in_weight.transpose(0, 2, 1),
            denoise_out_weight,
        ],
        [conv_in_bias[None, :], conv_out_bias[None, :], denoise_bias[None, :], step_bias],
        patch_noise[0],
        bands,
        sects,
        rows,
        cols,
    )
    biases, step_lines = lines[:3], lines[3]

    padded = right_rim.shape[0]
    parts = extract_own(who, anchor, turned, pick, padded, bands, sects)
    own, kept, own_sent, sent, edge_near, edge_cross = extract_rim(
        who, anchor, parts, turned, right, left, pick, bands, sects
    )
    addends = [own]
    if bands > 2:
        got = swap(sent, "band", 1)
        kept = add_parts(kept, got)
    bit = 2
    while bit < bands:
        got = swap(kept[0::2], "band", bit)
        addends.append(got)
        kept = kept[1::2] + got[1:]
        bit *= 2
    addends.append(swap(own_sent, "band", 1))
    rim_near = swap(edge_near, "band", 1)
    steps = [(i, i + 1) for i in range(1, bands - 1, 2)]
    rim_cross = lax.ppermute(edge_cross, "band", steps + [(j, i) for i, j in steps])
    correction = patch_step(who, anchor, addends, noise, made, biases, step_lines, sects, limits)
    pieces = [correction]
    sources = [0]
    bit = bands // 2
    while bit:
        fresh = []
        for piece in pieces:
            fresh.append(swap(piece, "band", bit))
        pieces += fresh
        sources += [s ^ bit for s in sources]
        bit //= 2

    shifted = spread(turned, right, left)
    top_mean = grid_mean(who, shifted, rim_near, rim_cross, False, padded, made[:2], biases[:2], limits)
    low_mean = grid_mean(who, shifted, rim_near, rim_cross, True, padded, made[:2], biases[:2], limits)
    spilled, summed, inverse = canvas(
        who, anchor, pieces, sources, place, sects, rows, cols
    )
    arrived = shift_from(spilled, "sect", 1)
    return finish([top_mean, low_mean], summed, arrived, inverse, channels)


def solution(mesh):
    placed = (
        P("groups", "band", "sect"),
        P(),
        P(),
        P(),
        P(),
        P("groups", None),
        P(("groups", "band", "sect"), None, None, None),
        P(),
        P(),
        P(),
        P(),
    )
    return jax.shard_map(
        step,
        mesh=mesh,
        in_specs=placed,
        out_specs=P("groups", "band", "sect"),
        check_vma=False,
    )
```

```python
import jax
import jax.numpy as jnp
from jax import lax
from jax.experimental import pallas as pl
from jax.experimental.pallas import tpu as pltpu
from jax.sharding import PartitionSpec as P


SIDE = 32
WIDE = SIDE + 4
PER_TILE = 3
TILES = WIDE // PER_TILE
LANES = 128
REACH = SIDE + 2
CHUNKS = 1
HALF = jnp.bfloat16
FULL = jnp.float32


def shift_from(block, axis, distance):
    count = lax.axis_size(axis)
    route = [(i - distance, i) for i in range(count) if 0 <= i - distance < count]
    return lax.ppermute(block, axis, route)


def swap(block, axis, bit):
    count = lax.axis_size(axis)
    return lax.ppermute(block, axis, [(i, i ^ bit) for i in range(count)])


def run(body, outs, ins, scratch, micros=1.0, limit=16):
    vmem = pl.BlockSpec(memory_space=pltpu.VMEM)
    return pl.pallas_call(
        body,
        out_shape=outs,
        in_specs=[vmem] * len(ins),
        out_specs=[vmem] * len(outs),
        scratch_shapes=scratch,
        cost_estimate=pl.CostEstimate(
            flops=int(micros * 1.15e9), bytes_accessed=1024, transcendentals=0
        ),
        compiler_params=pltpu.CompilerParams(vmem_limit_bytes=limit * 1024 * 1024),
    )(*ins)


def here():
    return lax.axis_index("band"), lax.axis_index("sect")


def slots_at(at_ref, readers, sects, rows, cols):
    band, sect = here()
    count = at_ref.shape[1]
    bits = (cols * sects - 1).bit_length()
    both = jnp.left_shift(at_ref[0:1, :], bits) + at_ref[1:2, :]
    lane = lane_index((1, count))
    found = []
    for reader in readers:
        mine = lane == reader * sects + sect
        code = jnp.sum(jnp.where(mine, both, 0).astype(FULL)).astype(jnp.int32)
        row, col = jnp.right_shift(code, bits), jnp.bitwise_and(code, (1 << bits) - 1)
        found.append((row - band * rows, col - sect * cols))
    return found


def slot_anchors(at_ref, slots, sects, rows, cols):
    band, _ = here()
    return slots_at(at_ref, [jnp.bitwise_xor(band, j) for j in slots], sects, rows, cols)


def like(shape, dtype=HALF):
    return jax.ShapeDtypeStruct(shape, dtype)


def lane_index(shape):
    return lax.broadcasted_iota(jnp.int32, shape, len(shape) - 1)


def turn_rows(state_ref, flat):
    channels = state_ref.shape[0]
    flat[:channels] = state_ref[...]
    flat[channels:] = jnp.zeros((flat.shape[0] - channels,) + flat.shape[1:], HALF)
    return jnp.swapaxes(flat[...], 0, 1)


def pack(state):
    channels, rows, cols = state.shape
    padded = -(-channels // 8) * 8
    deep = -(-padded // 16) * 16
    span = -(-rows * REACH // LANES)

    def body(state_ref, right_ref, left_ref, rows_ref, flat):
        turned = turn_rows(state_ref, flat)
        rows_ref[...] = turned
        lane = lane_index((deep, LANES))
        tiles = [None] * span
        rim = jnp.zeros((deep, LANES), HALF)
        for r in range(rows):
            row = turned[r]
            at, off = divmod(r * REACH, LANES)
            moved = row if off == 0 else pltpu.roll(row, off, 1)
            if tiles[at] is None:
                tiles[at] = moved
            else:
                tiles[at] = jnp.where(lane >= off, moved, tiles[at])
            if off + REACH > LANES:
                tiles[at + 1] = moved
            moved = pltpu.roll(row, (2 * r + 2) % LANES, 1)
            rim = jnp.where((lane >= 2 * r) & (lane < 2 * r + 2), moved, rim)
        for at in range(span):
            right_ref[:, at * LANES : (at + 1) * LANES] = tiles[at][:padded]
        left_ref[...] = rim[:padded]

    return run(
        body,
        [like((padded, span * LANES)), like((padded, LANES)), like((rows, deep, cols))],
        [state],
        [pltpu.VMEM((deep, rows, cols), HALF)],
        micros=1.0,
    )


def prep(weights, biases, noise):
    steps, channels, cells = noise.shape
    count = len(weights)
    tile_rows = LANES // SIDE
    lines = len(biases)

    def body(*refs):
        ins, lines_in, noise_ref = refs[:count], refs[count : count + lines], refs[count + lines]
        outs = refs[count + lines + 1 :]
        lines_out, noise_out = outs[count : count + lines], outs[count + lines]
        for k, (w_ref, o_ref) in enumerate(zip(ins, outs)):
            _, down, across = w_ref.shape
            o_ref[...] = jnp.zeros(o_ref.shape, HALF)
            for v in range(2):
                for a in range(3):
                    for b in range(3):
                        tap = (3 * (a + v) + b) * LANES
                        row, col = (v * LANES, tap) if k % 2 else (tap, v * LANES)
                        o_ref[row : row + down, col : col + across] = w_ref[3 * a + b]
        for line_ref, o_ref in zip(lines_in, lines_out):
            used = line_ref.shape[1]
            o_ref[...] = jnp.zeros(o_ref.shape, FULL)
            o_ref[:, :used] = line_ref[...]
            o_ref[:, LANES : LANES + used] = line_ref[...]
        for k in range(steps):
            for t in range(cells // LANES):
                block = noise_ref[k, :, t * LANES : (t + 1) * LANES].astype(FULL)
                block = jnp.concatenate(
                    [block, jnp.zeros((LANES - channels, LANES), FULL)], axis=0
                ).T.astype(HALF)
                for m in range(tile_rows):
                    r = t * tile_rows + m
                    noise_out[
                        k, r // 2 * SIDE : (r // 2 + 1) * SIDE, r % 2 * LANES : (r % 2 + 1) * LANES
                    ] = block[m * SIDE : (m + 1) * SIDE]

    sizes = [(12 * LANES, 2 * LANES), (2 * LANES, 12 * LANES)]
    made = [like(sizes[k % 2]) for k in range(count)]
    made += [like((line.shape[0], 2 * LANES), FULL) for line in biases]
    made += [like((steps, cells // 2, 2 * LANES))]
    out = run(body, made, [*weights, *biases, noise], [], micros=1.5)
    return out[:count], out[count : count + lines], out[count + lines]


def picks(anchor, bands, sects, rows, cols):
    width = cols + LANES
    tile_rows = LANES // SIDE

    def body(at_ref, pick_ref, place_ref):
        source = lax.broadcasted_iota(jnp.int32, (width, LANES), 0)
        inner = lane_index((width, LANES))
        for _ in range(1, PER_TILE):
            inner = jnp.where(inner >= WIDE, inner - WIDE, inner)
        cell = lax.broadcasted_iota(jnp.int32, (LANES, 2 * LANES), 0)
        target = lane_index((LANES, 2 * LANES))
        anchors = slot_anchors(at_ref, range(bands), sects, rows, cols)
        for j, (row0, col0) in enumerate(anchors):
            want = jnp.bitwise_and(inner + (col0 - 2), width - 1)
            pick_ref[:, j * LANES : (j + 1) * LANES] = jnp.where(source == want, 1.0, 0.0).astype(HALF)
            across = jnp.bitwise_and(cell, SIDE - 1) + col0
            for m in range(tile_rows):
                turn = jnp.bitwise_and(m - row0, tile_rows - 1)
                there = jnp.where(across < cols, across, across - cols + LANES + m * SIDE)
                hit = (target == there) & (cell >= turn * SIDE) & (cell < (turn + 1) * SIDE)
                place_ref[m, j * LANES : (j + 1) * LANES] = jnp.where(hit, 1.0, 0.0).astype(HALF)

    return run(
        body,
        [like((width, bands * LANES)), like((tile_rows, bands * LANES, 2 * LANES))],
        [anchor],
        [],
        micros=1.0,
    )


def add_parts(kept, got):
    def body(kept_ref, got_ref, out_ref):
        out_ref[...] = kept_ref[...] + got_ref[...]

    return run(body, [like(kept.shape)], [kept, got], [], micros=0.3)[0]


def window_tile(picked, t, row0, rows, padded, lanes):
    zone = lane_index((padded, LANES))
    total = jnp.zeros((padded, LANES), FULL)
    for m in range(PER_TILE):
        r = row0 + t * PER_TILE + m
        low = jnp.where((r >= 0) & (r < rows), WIDE * m, 2 * LANES)
        keep = (zone >= low) & (zone < WIDE * (m + 1))
        value = picked[jnp.clip(r, 0, rows - 1), :padded, lanes]
        total = jnp.where(keep, value, total)
    return total.astype(HALF)


def batches(bands):
    size = 4 if bands % 4 == 0 else bands
    return [range(first, first + size) for first in range(0, bands, size)], size


def select_rows(source, pick, picked):
    rows, deep, _ = source.shape
    chunk = rows // 2

    def select(c, carry):
        view = source[pl.ds(c * chunk, chunk)].reshape(chunk * deep, LANES)
        picked[pl.ds(c * chunk, chunk)] = jnp.dot(
            view, pick, preferred_element_type=FULL
        ).reshape(chunk, deep, pick.shape[1])
        return carry

    lax.fori_loop(0, rows // chunk, select, 0)


def extract_own(anchor, turned, pick, padded, bands, sects):
    rows, deep, cols = turned.shape
    groups, size = batches(bands)

    def body(at_ref, rows_ref, pick_ref, out_ref, picked):
        anchors = slot_anchors(at_ref, range(bands), sects, rows, cols)
        for group in groups:
            select_rows(rows_ref, pick_ref[:cols, group[0] * LANES : (group[-1] + 1) * LANES], picked)
            for j in group:
                row0 = anchors[j][0] - 2
                inside = (row0 > -WIDE) & (row0 < rows)

                @pl.when(inside)
                def _(j=j, row0=row0, at=(j - group[0]) * LANES):
                    for t in range(TILES):
                        out_ref[j, :, t * LANES : (t + 1) * LANES] = window_tile(
                            picked, t, row0, rows, padded, slice(at, at + LANES)
                        )

                @pl.when(jnp.logical_not(inside))
                def _(j=j):
                    out_ref[j] = jnp.zeros((padded, TILES * LANES), HALF)

    return run(
        body,
        [like((bands, padded, TILES * LANES))],
        [anchor, turned, pick],
        [pltpu.VMEM((rows, deep, size * LANES), FULL)],
        micros=1.5
    )[0]


def extract_rim(anchor, parts, turned, right, left, pick, bands, sects):
    rows, deep, cols = turned.shape
    padded = right.shape[0]
    groups, size = batches(bands)

    def body(at_ref, part_ref, rows_ref, right_ref, left_ref, pick_ref,
             own_ref, low_ref, odd_ref, high_ref, near_ref, cross_ref, ext, picked):
        lane = lane_index((padded, LANES))
        none = jnp.zeros((padded, LANES), HALF)
        rim = left_ref[...]

        def expand(r):
            at, off = divmod(r * REACH, LANES)
            piece = right_ref[:, at * LANES : (at + 1) * LANES]
            if off:
                piece = pltpu.roll(piece, LANES - off, 1)
            if off + REACH > LANES:
                after = right_ref[:, (at + 1) * LANES : (at + 2) * LANES]
                piece = jnp.where(lane < LANES - off, piece, pltpu.roll(after, LANES - off, 1))
            turn = pltpu.roll(rim, (LANES - 2 - 2 * r) % LANES, 1)
            ext[r, :padded] = jnp.where(
                lane < REACH, piece, jnp.where(lane >= LANES - 2, turn, none)
            )

        ext[:, padded:] = jnp.zeros((rows, deep - padded, LANES), HALF)
        outer = (0, 1, rows - 2, rows - 1)
        for r in outer:
            expand(r)
        even = jnp.bitwise_and(here()[0], 1) == 0
        for k in range(2):
            top, low = k, rows - 2 + k
            near_ref[k, :, :cols] = jnp.where(even, rows_ref[low], rows_ref[top])
            near_ref[k, :, cols:] = jnp.where(even, ext[low], ext[top])
            cross_ref[k, :, :cols] = jnp.where(even, rows_ref[top], rows_ref[low])
            cross_ref[k, :, cols:] = jnp.where(even, ext[top], ext[low])

        def target(j):
            if j < 2:
                return (own_ref, odd_ref)[j], 0
            return (low_ref, high_ref)[j % 2], j // 2 - 1

        crossing = []
        anchors = slot_anchors(at_ref, range(bands), sects, rows, cols)
        for j, (row0, col0) in enumerate(anchors):
            row0 = row0 - 2
            inside = (row0 > -WIDE) & (row0 < rows)
            over = inside & ((col0 < 2) | (col0 > cols - REACH))
            crossing.append((row0, over))
            out_ref, at = target(j)
            out_ref[at] = part_ref[j]
        for group in groups:
            some = crossing[group[0]][1]
            for j in group[1:]:
                some = some | crossing[j][1]

            @pl.when(some)
            def _(group=group):
                if group[0] == 0:
                    for r in range(rows):
                        if r not in outer:
                            expand(r)
                else:
                    for r in range(rows):
                        expand(r)
                select_rows(
                    ext, pick_ref[cols:, group[0] * LANES : (group[-1] + 1) * LANES], picked
                )
                for j in group:
                    out_ref, at = target(j)
                    row0, over = crossing[j]

                    @pl.when(over)
                    def _(j=j, out_ref=out_ref, at=at, row0=row0, first=(j - group[0]) * LANES):
                        for t in range(TILES):
                            out_ref[at, :, t * LANES : (t + 1) * LANES] += window_tile(
                                picked, t, row0, rows, padded, slice(first, first + LANES)
                            )

    one = like((1, padded, TILES * LANES))
    rest = like((max(bands // 2 - 1, 1), padded, TILES * LANES))
    edge = like((2, deep, cols + LANES))
    return run(
        body,
        [one, rest, one, rest, edge, edge],
        [anchor, parts, turned, right, left, pick],
        [pltpu.VMEM((rows, deep, LANES), HALF), pltpu.VMEM((rows, deep, size * LANES), FULL)],
        micros=1.5
    )


def product(view, weight):
    turned = weight.shape[0] == 2 * LANES
    return lax.dot_general(
        view, weight, (((1,), (1 if turned else 0,)), ((), ())), preferred_element_type=FULL
    )


def gather_pairs(shifted, first, count):
    view = jnp.concatenate(
        [shifted[b, pl.ds(first + u, count), v] for u in (0, 1) for v in (0, 1) for b in (0, 1, 2)],
        axis=-1,
    )
    return view.reshape(count * view.shape[1], view.shape[2])


def silu(value):
    return value / (1.0 + jnp.exp(-value))


def patch_step(anchor, addends, noise, weights, biases, step_bias, sects, limits):
    padded = addends[0].shape[1]
    steps = noise.shape[0]
    half = SIDE // 2
    loose = 48

    def body(*refs):
        at_ref, parts = refs[0], refs[1 : 1 + len(addends)]
        band, sect = here()
        mine = lane_index(at_ref.shape) == band * sects + sect
        at = jnp.sum(jnp.where(mine, at_ref[...], 0).astype(FULL), axis=1, keepdims=True)
        row0, col0 = at.astype(jnp.int32)[0:1][None], at.astype(jnp.int32)[1:2][None]
        (noise_ref, w_in, w_out, d_in, d_out, b_in, b_out, b_step, b_den, out_ref,
         flat, state_sh, hid, hid_sh, pad, pad_sh, corr, state) = refs[1 + len(addends) :]
        for t in range(TILES):
            lanes = slice(t * LANES, (t + 1) * LANES)
            tile = parts[0][0, :, lanes].astype(FULL)
            for part in parts[1:]:
                tile = tile + part[0, :, lanes].astype(FULL)
            tile = jnp.concatenate([tile, jnp.zeros((LANES - padded, LANES), FULL)], axis=0)
            flat[lanes, :] = tile.T
        for i in range(WIDE):
            t, m = divmod(i, PER_TILE)
            off = t * LANES + m * WIDE
            for b in range(3):
                state_sh[b, i // 2, i % 2] = flat[off + b : off + b + loose, :].astype(HALF)
        pairs = half + 1
        value = product(gather_pairs(state_sh, 0, pairs), w_in[...])
        value = silu(value + b_in[...]).reshape(pairs, loose, 2 * LANES)
        pair = lax.broadcasted_iota(jnp.int32, value.shape, 0)
        col = lax.broadcasted_iota(jnp.int32, value.shape, 1)
        odd = (lane_index(value.shape) >= LANES).astype(jnp.int32)
        grid_row = row0 - 1 + 2 * pair + odd
        grid_col = col0 - 1 + col
        keep = (
            (grid_row >= 0) & (grid_row < limits[0])
            & (grid_col >= 0) & (grid_col < limits[1]) & (col < SIDE + 2)
        )
        value = jnp.where(keep, value, 0.0)
        hid[:, 0] = value[:, :, :LANES]
        hid[:, 1] = value[:, :, LANES:]
        for b in range(3):
            hid_sh[b] = hid[:, :, b : b + SIDE, :].astype(HALF)
        value = product(gather_pairs(hid_sh, 0, half), w_out[...])
        center = jnp.concatenate(
            [state_sh[2, 1 : 1 + half, v, :SIDE, :] for v in (0, 1)], axis=-1
        ).astype(FULL).reshape(half * SIDE, 2 * LANES)
        mean = (center + value + b_out[...]).astype(HALF).astype(FULL)
        state[...] = mean + noise_ref[0].astype(FULL)
        pad[...] = jnp.zeros(pad.shape, FULL)
        deal = half // CHUNKS
        trips = jnp.where(band >= 0, CHUNKS, 0)

        def fill(source, first, count):
            shaped = source.reshape(count, SIDE, 2 * LANES)
            pad[pl.ds(first, count), 1, 8 : 8 + SIDE] = shaped[:, :, :LANES]
            pad[pl.ds(first + 1, count), 0, 8 : 8 + SIDE] = shaped[:, :, LANES:]

        def shift():
            for b in range(3):
                pad_sh[b] = pad[:, :, 7 + b : 7 + b + SIDE, :].astype(HALF)

        for step in range(steps):
            fill(state[...], 0, half)
            shift()

            def first(c, carry, step=step):
                value = product(gather_pairs(pad_sh, c * deal, deal), d_in[...])
                fill(silu(value + b_step[step : step + 1]), c * deal, deal)
                return carry

            lax.fori_loop(0, trips, first, 0)
            shift()

            def second(c, carry, step=step):
                value = product(gather_pairs(pad_sh, c * deal, deal), d_out[...])
                cells = pl.ds(pl.multiple_of(c * deal * SIDE, deal * SIDE), deal * SIDE)
                value = state[cells] - 0.5 * (value + b_den[...])
                if step + 1 < steps:
                    value = value + 0.5 * noise_ref[step + 1, cells].astype(FULL)
                state[cells] = value
                return carry

            lax.fori_loop(0, trips, second, 0)
        change = (state[...] - mean).reshape(half, SIDE, 2 * LANES)
        corr[:, 0] = change[:, :, :LANES]
        corr[:, 1] = change[:, :, LANES:]
        cells = corr[...].reshape(SIDE * SIDE, LANES)
        for t in range(SIDE * SIDE // LANES):
            lanes = slice(t * LANES, (t + 1) * LANES)
            out_ref[:, lanes] = cells[lanes].T[:padded].astype(HALF)

    return run(
        body,
        [like((padded, SIDE * SIDE))],
        [anchor, *addends, noise, *weights, *biases[:2], step_bias, biases[2]],
        [
            pltpu.VMEM((TILES * LANES, LANES), FULL),
            pltpu.VMEM((3, WIDE // 2, 2, loose, LANES), HALF),
            pltpu.VMEM((half + 1, 2, loose, LANES), FULL),
            pltpu.VMEM((3, half + 1, 2, SIDE, LANES), HALF),
            pltpu.VMEM((half + 1, 2, loose, LANES), FULL),
            pltpu.VMEM((3, half + 1, 2, SIDE, LANES), HALF),
            pltpu.VMEM((half, 2, SIDE, LANES), FULL),
            pltpu.VMEM((half * SIDE, 2 * LANES), FULL),
        ],
        micros=8.0
    )[0]


def spread(turned, right, left):
    rows, _, cols = turned.shape
    span = right.shape[1]
    loose = cols + 16

    def body(rows_ref, right_ref, left_ref, out_ref, after, before, line):
        def upright(value):
            value = value.astype(FULL)
            return jnp.concatenate(
                [value, jnp.zeros((LANES - value.shape[0], value.shape[1]), FULL)], axis=0
            ).T

        for t in range(span // LANES):
            lanes = slice(t * LANES, (t + 1) * LANES)
            after[lanes] = upright(right_ref[:, lanes])
        before[...] = upright(left_ref[...])
        line[...] = jnp.zeros(line.shape, FULL)

        def spread_rows(i, carry):
            for v in range(2):
                r = 2 * i + v
                line[v, 8 : 8 + cols] = upright(rows_ref[r])
                line[v, 8 + cols : 10 + cols] = after[pl.ds(r * REACH, 2)]
                line[v, 6:8] = before[pl.ds(2 * r, 2)]
                for b in range(3):
                    out_ref[b, i, v] = line[v, 6 + b : 6 + b + loose, :].astype(HALF)
            return carry

        lax.fori_loop(0, rows // 2, spread_rows, 0)

    return run(
        body,
        [like((3, rows // 2, 2, loose, LANES))],
        [turned, right, left],
        [
            pltpu.VMEM((span, LANES), FULL),
            pltpu.VMEM((LANES, LANES), FULL),
            pltpu.VMEM((2, loose + 8, LANES), FULL),
        ],
        micros=2.5
    )[0]


def grid_mean(shifted, near, cross, lower, padded, weights, biases, limits):
    rows = 2 * shifted.shape[1]
    _, deep, width = near.shape
    cols = width - LANES
    loose = cols + 16
    made = rows // 2
    pairs_in, pairs_out = made // 4 + 1, made // 4
    hidden_pairs = made // 2 + 1
    if hidden_pairs % pairs_in:
        hidden_pairs += pairs_in - hidden_pairs % pairs_in
    state_pairs = hidden_pairs + 1
    base = rows - made - 2 if lower else -2

    def body(shifted_ref, near_ref, cross_ref, w_in, w_out, b_in, b_out, out_ref,
             line, state_sh, hid, hid_sh):
        band, sect = here()
        row0 = band * rows + base + 1
        col0 = sect * cols - 1

        for pair in range(made // 2 + 2, state_pairs):
            for b in range(3):
                state_sh[b, pair] = jnp.zeros((2, loose, LANES), HALF)
        edge = made // 2 + 1 if lower else 0
        skip = 0 if lower else 1
        given = made // 2 + 1
        at = (rows - made) // 2 - 1 if lower else 0
        for b in range(3):
            state_sh[b, skip : skip + given] = shifted_ref[b, at : at + given]
        pair = jnp.bitwise_and(band, 1) == (0 if lower else 1)
        for v in range(2):
            rim = jnp.where(pair, near_ref[v], cross_ref[v])
            value = jnp.concatenate(
                [rim.astype(FULL), jnp.zeros((LANES - deep, width), FULL)], axis=0
            ).T
            line[v, 8 : 8 + cols] = value[:cols]
            line[v, 8 + cols :] = value[cols : cols + 16]
            line[v, :8] = value[width - 8 :]
            for b in range(3):
                state_sh[b, edge, v] = line[v, 6 + b : 6 + b + loose, :].astype(HALF)

        def first(chunk, carry):
            start = chunk * pairs_in
            value = product(gather_pairs(state_sh, start, pairs_in), w_in[...])
            value = silu(value + b_in[...]).reshape(pairs_in, loose, 2 * LANES)
            pair = lax.broadcasted_iota(jnp.int32, value.shape, 0)
            col = lax.broadcasted_iota(jnp.int32, value.shape, 1)
            odd = (lane_index(value.shape) >= LANES).astype(jnp.int32)
            grid_row = row0 + 2 * (start + pair) + odd
            grid_col = col0 + col
            keep = (
                (grid_row >= 0) & (grid_row < limits[0])
                & (grid_col >= 0) & (grid_col < limits[1])
            )
            value = jnp.where(keep, value, 0.0)
            hid[:, 0] = value[:, :, :LANES]
            hid[:, 1] = value[:, :, LANES:]
            for b in range(3):
                hid_sh[b, pl.ds(start, pairs_in)] = hid[:, :, b : b + cols, :].astype(HALF)
            return carry

        lax.fori_loop(0, hidden_pairs // pairs_in, first, 0)

        def second(chunk, carry):
            start = chunk * pairs_out
            value = product(gather_pairs(hid_sh, start, pairs_out), w_out[...]) + b_out[...]
            value = value.reshape(pairs_out, cols, 2 * LANES)
            for k in range(pairs_out):
                for v in range(2):
                    center = state_sh[2, start + k + 1, v, :cols, :].astype(FULL)
                    mean = center + value[k, :, v * LANES : (v + 1) * LANES]
                    out_ref[2 * (start + k) + v] = mean.T[:padded].astype(HALF)
            return carry

        lax.fori_loop(0, made // 2 // pairs_out, second, 0)

    return run(
        body,
        [like((made, padded, cols))],
        [shifted, near, cross, *weights, *biases],
        [
            pltpu.VMEM((2, loose + 8, LANES), FULL),
            pltpu.VMEM((3, state_pairs, 2, loose, LANES), HALF),
            pltpu.VMEM((pairs_in, 2, loose, LANES), FULL),
            pltpu.VMEM((3, hidden_pairs, 2, cols, LANES), HALF),
        ],
        micros=3.5,
    )[0]


def canvas(anchor, pieces, sources, place, sects, rows, cols):
    padded = pieces[0].shape[-2]
    deep = -(-padded // 16) * 16
    total = anchor.shape[1]
    slots = len(pieces)
    tile_rows = LANES // SIDE
    groups = rows // tile_rows

    def body(at_ref, *refs):
        band, sect = here()
        place_ref, spill_ref, out_ref, inverse_ref, view = refs[slots:]
        none = jnp.zeros((padded, LANES), HALF)
        anchors = slot_anchors(at_ref, sources, sects, rows, cols)
        for piece, j, (row0, _) in zip(refs, sources, anchors):
            lanes = slice(j * LANES, (j + 1) * LANES)
            for r in range(rows):
                i = r - row0
                tile = jnp.clip(jnp.right_shift(i, tile_rows.bit_length() - 1), 0, SIDE // tile_rows - 1)
                value = piece[:, pl.ds(pl.multiple_of(tile * LANES, LANES), LANES)]
                inside = (i >= 0) & (i < SIDE)
                view[r % tile_rows, r // tile_rows, :padded, lanes] = jnp.where(
                    inside, value, none
                )
        view[:, :, padded:, :] = jnp.zeros(
            (tile_rows, groups, deep - padded, slots * LANES), HALF
        )
        spilled = None
        for m in range(tile_rows):
            value = jnp.dot(
                view[m].reshape(groups * deep, slots * LANES), place_ref[m],
                preferred_element_type=FULL,
            ).reshape(groups, deep, 2 * LANES)
            for k in range(groups):
                out_ref[k * tile_rows + m] = value[k, :padded, :LANES]
            part = value[:, :padded, LANES:]
            spilled = part if spilled is None else spilled + part
        for k in range(groups):
            spill_ref[:, k * LANES : (k + 1) * LANES] = spilled[k].astype(HALF)
        tall, wide = (rows, total), (total, cols)
        down = lax.broadcasted_iota(jnp.int32, tall, 0) + band * rows - at_ref[0:1, :]
        across = lane_index(wide) + sect * cols - at_ref[1:2, :].astype(FULL).T.astype(jnp.int32)
        down = jnp.where((down >= 0) & (down < SIDE), 1.0, 0.0)
        across = jnp.where((across >= 0) & (across < SIDE), 1.0, 0.0)
        count = jnp.dot(down.astype(HALF), across.astype(HALF), preferred_element_type=FULL)
        inverse_ref[...] = 1.0 / jnp.maximum(count, 1.0)

    return run(
        body,
        [
            like((padded, rows * SIDE)),
            like((rows, padded, cols), FULL),
            like((rows, cols), FULL),
        ],
        [anchor, *pieces, place],
        [pltpu.VMEM((tile_rows, groups, deep, slots * LANES), HALF)],
        micros=1.5
    )


def finish(means, summed, arrived, inverse, channels):
    rows, padded, cols = summed.shape
    deep = -(-padded // 16) * 16
    half = means[0].shape[0]

    def body(top_ref, low_ref, sum_ref, spill_ref, inverse_ref, out_ref, flat):
        lane = lane_index((padded, LANES))
        none = jnp.zeros((padded, LANES), HALF)
        flat[:, padded:] = jnp.zeros((rows, deep - padded, cols), HALF)
        for r in range(rows):
            at, low = divmod(r * SIDE, LANES)
            extra = spill_ref[:, at * LANES : (at + 1) * LANES]
            if low:
                extra = pltpu.roll(extra, LANES - low, 1)
            extra = jnp.where(lane < SIDE, extra, none).astype(FULL)
            mean = top_ref[r] if r < half else low_ref[r - half]
            value = mean.astype(FULL) + (sum_ref[r] + extra) * inverse_ref[r : r + 1]
            flat[r, :padded] = value.astype(HALF)
        out_ref[...] = jnp.swapaxes(flat[...], 0, 1)[:channels]

    return run(
        body,
        [like((channels, rows, cols))],
        [*means, summed, arrived, inverse],
        [pltpu.VMEM((rows, deep, cols), HALF)],
        micros=3.0
    )[0]


def step(
    state_field,
    conv_in_weight,
    conv_in_bias,
    conv_out_weight,
    conv_out_bias,
    patch_anchor,
    patch_noise,
    denoise_in_weight,
    step_bias,
    denoise_out_weight,
    denoise_bias,
):
    bands = lax.axis_size("band")
    sects = lax.axis_size("sect")
    channels, rows, cols = state_field.shape
    limits = (rows * bands, cols * sects)

    anchor = patch_anchor.T

    right_rim, left_rim, turned = pack(state_field)
    right = shift_from(right_rim, "sect", -1)
    left = shift_from(left_rim, "sect", 1)

    made, lines, noise = prep(
        [
            conv_in_weight.transpose(0, 2, 1),
            conv_out_weight,
            denoise_in_weight.transpose(0, 2, 1),
            denoise_out_weight,
        ],
        [conv_in_bias[None, :], conv_out_bias[None, :], denoise_bias[None, :], step_bias],
        patch_noise[0],
    )
    biases, step_lines = lines[:3], lines[3]

    padded = right_rim.shape[0]
    pick, place = picks(anchor, bands, sects, rows, cols)
    parts = extract_own(anchor, turned, pick, padded, bands, sects)
    own, kept, own_sent, sent, edge_near, edge_cross = extract_rim(
        anchor, parts, turned, right, left, pick, bands, sects
    )
    addends = [own]
    if bands > 2:
        got = swap(sent, "band", 1)
        kept = add_parts(kept, got)
    bit = 2
    while bit < bands:
        got = swap(kept[0::2], "band", bit)
        addends.append(got)
        kept = kept[1::2] + got[1:]
        bit *= 2
    addends.append(swap(own_sent, "band", 1))
    rim_near = swap(edge_near, "band", 1)
    steps = [(i, i + 1) for i in range(1, bands - 1, 2)]
    rim_cross = lax.ppermute(edge_cross, "band", steps + [(j, i) for i, j in steps])
    correction = patch_step(
        anchor, addends, noise, made, biases, step_lines, sects, limits
    )
    pieces = [correction]
    sources = [0]
    bit = bands // 2
    while bit:
        fresh = []
        for piece in pieces:
            fresh.append(swap(piece, "band", bit))
        pieces += fresh
        sources += [s ^ bit for s in sources]
        bit //= 2

    shifted = spread(turned, right, left)
    top_mean = grid_mean(shifted, rim_near, rim_cross, False, padded, made[:2], biases[:2], limits)
    low_mean = grid_mean(shifted, rim_near, rim_cross, True, padded, made[:2], biases[:2], limits)
    spilled, summed, inverse = canvas(
        anchor, pieces, sources, place, sects, rows, cols
    )
    arrived = shift_from(spilled, "sect", 1)
    return finish([top_mean, low_mean], summed, arrived, inverse, channels)


def solution(mesh):
    placed = (
        P("groups", "band", "sect"),
        P(),
        P(),
        P(),
        P(),
        P("groups", None),
        P(("groups", "band", "sect"), None, None, None),
        P(),
        P(),
        P(),
        P(),
    )
    return jax.shard_map(
        step,
        mesh=mesh,
        in_specs=placed,
        out_specs=P("groups", "band", "sect"),
        check_vma=False,
    )
```

```python
import jax
import jax.numpy as jnp
from jax import lax
from jax.experimental import pallas as pl
from jax.experimental.pallas import tpu as pltpu
from jax.sharding import PartitionSpec as P


SIDE = 32
WIDE = SIDE + 4
PER_TILE = 3
TILES = WIDE // PER_TILE
LANES = 128
REACH = SIDE + 2
CHUNKS = 1
HALF = jnp.bfloat16
FULL = jnp.float32


def cycle_from(block, axis, distance):
    count = lax.axis_size(axis)
    return lax.ppermute(block, axis, [((i - distance) % count, i) for i in range(count)])


def swap(block, axis, bit):
    count = lax.axis_size(axis)
    return lax.ppermute(block, axis, [(i, i ^ bit) for i in range(count)])


def run(body, outs, ins, scratch, micros=1.0, limit=16, in_space=pltpu.VMEM, out_space=pltpu.VMEM):
    return pl.pallas_call(
        body,
        out_shape=outs,
        in_specs=[pl.BlockSpec(memory_space=in_space)] * len(ins),
        out_specs=[pl.BlockSpec(memory_space=out_space)] * len(outs),
        scratch_shapes=scratch,
        cost_estimate=pl.CostEstimate(
            flops=int(micros * 1.15e9), bytes_accessed=1024, transcendentals=0
        ),
        compiler_params=pltpu.CompilerParams(vmem_limit_bytes=limit * 1024 * 1024),
    )(*ins)


def here():
    return lax.axis_index("band"), lax.axis_index("sect")


def slots_at(at_ref, readers, sects, rows, cols):
    band, sect = here()
    count = at_ref.shape[1]
    bits = (cols * sects - 1).bit_length()
    both = jnp.left_shift(at_ref[0:1, :], bits) + at_ref[1:2, :]
    lane = lane_index((1, count))
    found = []
    for reader in readers:
        mine = lane == reader * sects + sect
        code = jnp.sum(jnp.where(mine, both, 0).astype(FULL)).astype(jnp.int32)
        row, col = jnp.right_shift(code, bits), jnp.bitwise_and(code, (1 << bits) - 1)
        found.append((row - band * rows, col - sect * cols))
    return found


def slot_anchors(at_ref, slots, sects, rows, cols):
    band, _ = here()
    return slots_at(at_ref, [jnp.bitwise_xor(band, j) for j in slots], sects, rows, cols)


def like(shape, dtype=HALF):
    return jax.ShapeDtypeStruct(shape, dtype)


def lane_index(shape):
    return lax.broadcasted_iota(jnp.int32, shape, len(shape) - 1)


def pack(state):
    channels, rows, cols = state.shape
    padded = -(-channels // 8) * 8
    deep = -(-padded // 16) * 16
    span = -(-rows * REACH // LANES)
    chunk = 8

    def body(state_ref, right_ref, left_ref, rows_ref, flat, sems):
        copies = [
            pltpu.make_async_copy(
                state_ref.at[:, pl.ds(first, chunk), :],
                flat.at[first // chunk, pl.ds(0, channels)],
                sems.at[first // chunk],
            )
            for first in range(0, rows, chunk)
        ]
        for copy in copies:
            copy.start()
        turned = []
        for k, copy in enumerate(copies):
            flat[k, channels:] = jnp.zeros((deep - channels, chunk, cols), HALF)
            copy.wait()
            part = jnp.swapaxes(flat[k], 0, 1)
            rows_ref[k * chunk : (k + 1) * chunk] = part
            turned += [part[i] for i in range(chunk)]
        lane = lane_index((deep, LANES))
        tiles = [None] * span
        rim = jnp.zeros((deep, LANES), HALF)
        for r in range(rows):
            row = turned[r]
            at, off = divmod(r * REACH, LANES)
            moved = row if off == 0 else pltpu.roll(row, off, 1)
            if tiles[at] is None:
                tiles[at] = moved
            else:
                tiles[at] = jnp.where(lane >= off, moved, tiles[at])
            if off + REACH > LANES:
                tiles[at + 1] = moved
            moved = pltpu.roll(row, (2 * r + 2) % LANES, 1)
            rim = jnp.where((lane >= 2 * r) & (lane < 2 * r + 2), moved, rim)
        for at in range(span):
            right_ref[:, at * LANES : (at + 1) * LANES] = tiles[at][:padded]
        left_ref[...] = rim[:padded]

    return run(
        body,
        [like((padded, span * LANES)), like((padded, LANES)), like((rows, deep, cols))],
        [state],
        [
            pltpu.VMEM((rows // chunk, deep, chunk, cols), HALF),
            pltpu.SemaphoreType.DMA((rows // chunk,)),
        ],
        micros=1.0,
        in_space=pltpu.HBM,
    )


def prep(weights, biases, noise):
    steps, channels, cells = noise.shape
    count = len(weights)
    tile_rows = LANES // SIDE
    lines = len(biases)

    def body(*refs):
        ins, lines_in, noise_ref = refs[:count], refs[count : count + lines], refs[count + lines]
        outs = refs[count + lines + 1 :]
        lines_out, noise_out = outs[count : count + lines], outs[count + lines]
        for k, (w_ref, o_ref) in enumerate(zip(ins, outs)):
            _, down, across = w_ref.shape
            o_ref[...] = jnp.zeros(o_ref.shape, HALF)
            for v in range(2):
                for a in range(3):
                    for b in range(3):
                        tap = (3 * (a + v) + b) * LANES
                        row, col = (v * LANES, tap) if k % 2 else (tap, v * LANES)
                        o_ref[row : row + down, col : col + across] = w_ref[3 * a + b]
        for line_ref, o_ref in zip(lines_in, lines_out):
            used = line_ref.shape[1]
            o_ref[...] = jnp.zeros(o_ref.shape, FULL)
            o_ref[:, :used] = line_ref[...]
            o_ref[:, LANES : LANES + used] = line_ref[...]
        for k in range(steps):
            for t in range(cells // LANES):
                block = noise_ref[k, :, t * LANES : (t + 1) * LANES].astype(FULL)
                block = jnp.concatenate(
                    [block, jnp.zeros((LANES - channels, LANES), FULL)], axis=0
                ).T.astype(HALF)
                for m in range(tile_rows):
                    r = t * tile_rows + m
                    noise_out[
                        k, r // 2 * SIDE : (r // 2 + 1) * SIDE, r % 2 * LANES : (r % 2 + 1) * LANES
                    ] = block[m * SIDE : (m + 1) * SIDE]

    sizes = [(12 * LANES, 2 * LANES), (2 * LANES, 12 * LANES)]
    made = [like(sizes[k % 2]) for k in range(count)]
    made += [like((line.shape[0], 2 * LANES), FULL) for line in biases]
    made += [like((steps, cells // 2, 2 * LANES))]
    out = run(body, made, [*weights, *biases, noise], [], micros=1.5)
    return out[:count], out[count : count + lines], out[count + lines]


def picks(anchor, bands, sects, rows, cols):
    width = cols + LANES
    tile_rows = LANES // SIDE

    def body(at_ref, pick_ref, place_ref):
        source = lax.broadcasted_iota(jnp.int32, (width, LANES), 0)
        inner = lane_index((width, LANES))
        for _ in range(1, PER_TILE):
            inner = jnp.where(inner >= WIDE, inner - WIDE, inner)
        cell = lax.broadcasted_iota(jnp.int32, (LANES, 2 * LANES), 0)
        target = lane_index((LANES, 2 * LANES))
        anchors = slot_anchors(at_ref, range(bands), sects, rows, cols)
        for j, (row0, col0) in enumerate(anchors):
            want = jnp.bitwise_and(inner + (col0 - 2), width - 1)
            pick_ref[:, j * LANES : (j + 1) * LANES] = jnp.where(source == want, 1.0, 0.0).astype(HALF)
            across = jnp.bitwise_and(cell, SIDE - 1) + col0
            for m in range(tile_rows):
                turn = jnp.bitwise_and(m - row0, tile_rows - 1)
                there = jnp.where(across < cols, across, across - cols + LANES + m * SIDE)
                hit = (target == there) & (cell >= turn * SIDE) & (cell < (turn + 1) * SIDE)
                place_ref[m, j * LANES : (j + 1) * LANES] = jnp.where(hit, 1.0, 0.0).astype(HALF)

    return run(
        body,
        [like((width, bands * LANES)), like((tile_rows, bands * LANES, 2 * LANES))],
        [anchor],
        [],
        micros=1.0,
    )


def add_parts(kept, got):
    def body(kept_ref, got_ref, out_ref):
        out_ref[...] = kept_ref[...] + got_ref[...]

    return run(body, [like(kept.shape)], [kept, got], [], micros=0.3)[0]


def window_tile(picked, t, row0, rows, padded, lanes):
    zone = lane_index((padded, LANES))
    total = jnp.zeros((padded, LANES), FULL)
    for m in range(PER_TILE):
        r = row0 + t * PER_TILE + m
        low = jnp.where((r >= 0) & (r < rows), WIDE * m, 2 * LANES)
        keep = (zone >= low) & (zone < WIDE * (m + 1))
        value = picked[jnp.clip(r, 0, rows - 1), :padded, lanes]
        total = jnp.where(keep, value, total)
    return total.astype(HALF)


def batches(bands):
    size = 4 if bands % 4 == 0 else bands
    return [range(first, first + size) for first in range(0, bands, size)], size


def select_rows(source, pick, picked):
    rows, deep, _ = source.shape
    chunk = rows // 2

    def select(c, carry):
        view = source[pl.ds(c * chunk, chunk)].reshape(chunk * deep, LANES)
        picked[pl.ds(c * chunk, chunk)] = jnp.dot(
            view, pick, preferred_element_type=FULL
        ).reshape(chunk, deep, pick.shape[1])
        return carry

    lax.fori_loop(0, rows // chunk, select, 0)


def extract_own(anchor, turned, pick, padded, bands, sects):
    rows, deep, cols = turned.shape
    groups, size = batches(bands)

    def body(at_ref, rows_ref, pick_ref, out_ref, picked):
        anchors = slot_anchors(at_ref, range(bands), sects, rows, cols)
        for group in groups:
            select_rows(rows_ref, pick_ref[:cols, group[0] * LANES : (group[-1] + 1) * LANES], picked)
            for j in group:
                row0 = anchors[j][0] - 2
                inside = (row0 > -WIDE) & (row0 < rows)

                @pl.when(inside)
                def _(j=j, row0=row0, at=(j - group[0]) * LANES):
                    for t in range(TILES):
                        out_ref[j, :, t * LANES : (t + 1) * LANES] = window_tile(
                            picked, t, row0, rows, padded, slice(at, at + LANES)
                        )

                @pl.when(jnp.logical_not(inside))
                def _(j=j):
                    out_ref[j] = jnp.zeros((padded, TILES * LANES), HALF)

    return run(
        body,
        [like((bands, padded, TILES * LANES))],
        [anchor, turned, pick],
        [pltpu.VMEM((rows, deep, size * LANES), FULL)],
        micros=1.5
    )[0]


def extract_rim(anchor, parts, turned, right, left, pick, bands, sects):
    rows, deep, cols = turned.shape
    padded = right.shape[0]

    def body(at_ref, part_ref, rows_ref, right_ref, left_ref, pick_ref,
             own_ref, low_ref, odd_ref, high_ref, near_ref, cross_ref, ext, picked):
        lane = lane_index((padded, LANES))
        none = jnp.zeros((padded, LANES), HALF)
        rim = left_ref[...]
        sect = here()[1]
        reach = jnp.where(sect < sects - 1, REACH, 0)
        start = jnp.where(sect > 0, LANES - 2, LANES)

        def expand(r):
            at, off = divmod(r * REACH, LANES)
            piece = right_ref[:, at * LANES : (at + 1) * LANES]
            if off:
                piece = pltpu.roll(piece, LANES - off, 1)
            if off + REACH > LANES:
                after = right_ref[:, (at + 1) * LANES : (at + 2) * LANES]
                piece = jnp.where(lane < LANES - off, piece, pltpu.roll(after, LANES - off, 1))
            turn = pltpu.roll(rim, (LANES - 2 - 2 * r) % LANES, 1)
            ext[r, :padded] = jnp.where(
                lane < reach, piece, jnp.where(lane >= start, turn, none)
            )

        ext[:, padded:] = jnp.zeros((rows, deep - padded, LANES), HALF)
        outer = (0, 1, rows - 2, rows - 1)
        for r in outer:
            expand(r)
        even = jnp.bitwise_and(here()[0], 1) == 0
        for k in range(2):
            top, low = k, rows - 2 + k
            near_ref[k, :, :cols] = jnp.where(even, rows_ref[low], rows_ref[top])
            near_ref[k, :, cols:] = jnp.where(even, ext[low], ext[top])
            cross_ref[k, :, :cols] = jnp.where(even, rows_ref[top], rows_ref[low])
            cross_ref[k, :, cols:] = jnp.where(even, ext[top], ext[low])

        def target(j):
            if j < 2:
                return (own_ref, odd_ref)[j], 0
            return (low_ref, high_ref)[j % 2], j // 2 - 1

        crossing = []
        anchors = slot_anchors(at_ref, range(bands), sects, rows, cols)
        for j, (row0, col0) in enumerate(anchors):
            row0 = row0 - 2
            inside = (row0 > -WIDE) & (row0 < rows)
            over = inside & ((col0 < 2) | (col0 > cols - REACH))
            crossing.append((row0, over))
            out_ref, at = target(j)
            out_ref[at] = part_ref[j]
        some = crossing[0][1]
        for _, over in crossing[1:]:
            some = some | over

        @pl.when(some)
        def _():
            for r in range(rows):
                if r not in outer:
                    expand(r)

        for j in range(bands):
            out_ref, at = target(j)
            row0, over = crossing[j]

            @pl.when(over)
            def _(j=j, out_ref=out_ref, at=at, row0=row0):
                select_rows(ext, pick_ref[cols:, j * LANES : (j + 1) * LANES], picked)
                for t in range(TILES):
                    out_ref[at, :, t * LANES : (t + 1) * LANES] += window_tile(
                        picked, t, row0, rows, padded, slice(0, LANES)
                    )

    one = like((1, padded, TILES * LANES))
    rest = like((max(bands // 2 - 1, 1), padded, TILES * LANES))
    edge = like((2, deep, cols + LANES))
    return run(
        body,
        [one, rest, one, rest, edge, edge],
        [anchor, parts, turned, right, left, pick],
        [pltpu.VMEM((rows, deep, LANES), HALF), pltpu.VMEM((rows, deep, LANES), FULL)],
        micros=1.5
    )


def product(view, weight):
    turned = weight.shape[0] == 2 * LANES
    return lax.dot_general(
        view, weight, (((1,), (1 if turned else 0,)), ((), ())), preferred_element_type=FULL
    )


def gather_pairs(shifted, first, count):
    view = jnp.concatenate(
        [shifted[b, pl.ds(first + u, count), v] for u in (0, 1) for v in (0, 1) for b in (0, 1, 2)],
        axis=-1,
    )
    return view.reshape(count * view.shape[1], view.shape[2])


def silu(value):
    return value / (1.0 + jnp.exp(-value))


def patch_step(anchor, addends, noise, weights, biases, step_bias, sects, limits):
    padded = addends[0].shape[1]
    steps = noise.shape[0]
    half = SIDE // 2
    loose = 48

    def body(*refs):
        at_ref, parts = refs[0], refs[1 : 1 + len(addends)]
        band, sect = here()
        mine = lane_index(at_ref.shape) == band * sects + sect
        at = jnp.sum(jnp.where(mine, at_ref[...], 0).astype(FULL), axis=1, keepdims=True)
        row0, col0 = at.astype(jnp.int32)[0:1][None], at.astype(jnp.int32)[1:2][None]
        (noise_ref, w_in, w_out, d_in, d_out, b_in, b_out, b_step, b_den, out_ref,
         flat, state_sh, hid, hid_sh, pad, pad_sh, corr, state) = refs[1 + len(addends) :]
        for t in range(TILES):
            lanes = slice(t * LANES, (t + 1) * LANES)
            tile = parts[0][0, :, lanes].astype(FULL)
            for part in parts[1:]:
                tile = tile + part[0, :, lanes].astype(FULL)
            tile = jnp.concatenate([tile, jnp.zeros((LANES - padded, LANES), FULL)], axis=0)
            flat[lanes, :] = tile.T
        for i in range(WIDE):
            t, m = divmod(i, PER_TILE)
            off = t * LANES + m * WIDE
            for b in range(3):
                state_sh[b, i // 2, i % 2] = flat[off + b : off + b + loose, :].astype(HALF)
        pairs = half + 1
        value = product(gather_pairs(state_sh, 0, pairs), w_in[...])
        value = silu(value + b_in[...]).reshape(pairs, loose, 2 * LANES)
        pair = lax.broadcasted_iota(jnp.int32, value.shape, 0)
        col = lax.broadcasted_iota(jnp.int32, value.shape, 1)
        odd = (lane_index(value.shape) >= LANES).astype(jnp.int32)
        grid_row = row0 - 1 + 2 * pair + odd
        grid_col = col0 - 1 + col
        keep = (
            (grid_row >= 0) & (grid_row < limits[0])
            & (grid_col >= 0) & (grid_col < limits[1]) & (col < SIDE + 2)
        )
        value = jnp.where(keep, value, 0.0)
        hid[:, 0] = value[:, :, :LANES]
        hid[:, 1] = value[:, :, LANES:]
        for b in range(3):
            hid_sh[b] = hid[:, :, b : b + SIDE, :].astype(HALF)
        value = product(gather_pairs(hid_sh, 0, half), w_out[...])
        center = jnp.concatenate(
            [state_sh[2, 1 : 1 + half, v, :SIDE, :] for v in (0, 1)], axis=-1
        ).astype(FULL).reshape(half * SIDE, 2 * LANES)
        mean = (center + value + b_out[...]).astype(HALF).astype(FULL)
        state[...] = mean + noise_ref[0].astype(FULL)
        pad[...] = jnp.zeros(pad.shape, FULL)
        deal = half // CHUNKS
        trips = jnp.where(band >= 0, CHUNKS, 0)

        def fill(source, first, count):
            shaped = source.reshape(count, SIDE, 2 * LANES)
            pad[pl.ds(first, count), 1, 8 : 8 + SIDE] = shaped[:, :, :LANES]
            pad[pl.ds(first + 1, count), 0, 8 : 8 + SIDE] = shaped[:, :, LANES:]

        def shift():
            for b in range(3):
                pad_sh[b] = pad[:, :, 7 + b : 7 + b + SIDE, :].astype(HALF)

        for step in range(steps):
            fill(state[...], 0, half)
            shift()

            def first(c, carry, step=step):
                value = product(gather_pairs(pad_sh, c * deal, deal), d_in[...])
                fill(silu(value + b_step[step : step + 1]), c * deal, deal)
                return carry

            lax.fori_loop(0, trips, first, 0)
            shift()

            def second(c, carry, step=step):
                value = product(gather_pairs(pad_sh, c * deal, deal), d_out[...])
                cells = pl.ds(pl.multiple_of(c * deal * SIDE, deal * SIDE), deal * SIDE)
                value = state[cells] - 0.5 * (value + b_den[...])
                if step + 1 < steps:
                    value = value + 0.5 * noise_ref[step + 1, cells].astype(FULL)
                state[cells] = value
                return carry

            lax.fori_loop(0, trips, second, 0)
        change = (state[...] - mean).reshape(half, SIDE, 2 * LANES)
        corr[:, 0] = change[:, :, :LANES]
        corr[:, 1] = change[:, :, LANES:]
        cells = corr[...].reshape(SIDE * SIDE, LANES)
        for t in range(SIDE * SIDE // LANES):
            lanes = slice(t * LANES, (t + 1) * LANES)
            out_ref[:, lanes] = cells[lanes].T[:padded].astype(HALF)

    return run(
        body,
        [like((padded, SIDE * SIDE))],
        [anchor, *addends, noise, *weights, *biases[:2], step_bias, biases[2]],
        [
            pltpu.VMEM((TILES * LANES, LANES), FULL),
            pltpu.VMEM((3, WIDE // 2, 2, loose, LANES), HALF),
            pltpu.VMEM((half + 1, 2, loose, LANES), FULL),
            pltpu.VMEM((3, half + 1, 2, SIDE, LANES), HALF),
            pltpu.VMEM((half + 1, 2, loose, LANES), FULL),
            pltpu.VMEM((3, half + 1, 2, SIDE, LANES), HALF),
            pltpu.VMEM((half, 2, SIDE, LANES), FULL),
            pltpu.VMEM((half * SIDE, 2 * LANES), FULL),
        ],
        micros=8.0
    )[0]


def spread(turned, right, left, sects):
    rows, _, cols = turned.shape
    span = right.shape[1]
    loose = cols + 16

    def body(rows_ref, right_ref, left_ref, out_ref, after, before, line):
        sect = here()[1]

        def upright(value):
            value = value.astype(FULL)
            return jnp.concatenate(
                [value, jnp.zeros((LANES - value.shape[0], value.shape[1]), FULL)], axis=0
            ).T

        for t in range(span // LANES):
            lanes = slice(t * LANES, (t + 1) * LANES)
            after[lanes] = jnp.where(sect < sects - 1, upright(right_ref[:, lanes]), 0.0)
        before[...] = jnp.where(sect > 0, upright(left_ref[...]), 0.0)
        line[...] = jnp.zeros(line.shape, FULL)

        def spread_rows(i, carry):
            for v in range(2):
                r = 2 * i + v
                line[v, 8 : 8 + cols] = upright(rows_ref[r])
                line[v, 8 + cols : 10 + cols] = after[pl.ds(r * REACH, 2)]
                line[v, 6:8] = before[pl.ds(2 * r, 2)]
                for b in range(3):
                    out_ref[b, i, v] = line[v, 6 + b : 6 + b + loose, :].astype(HALF)
            return carry

        lax.fori_loop(0, rows // 2, spread_rows, 0)

    return run(
        body,
        [like((3, rows // 2, 2, loose, LANES))],
        [turned, right, left],
        [
            pltpu.VMEM((span, LANES), FULL),
            pltpu.VMEM((LANES, LANES), FULL),
            pltpu.VMEM((2, loose + 8, LANES), FULL),
        ],
        micros=2.5
    )[0]


def grid_mean(shifted, near, cross, lower, padded, weights, biases, limits):
    rows = 2 * shifted.shape[1]
    _, deep, width = near.shape
    cols = width - LANES
    loose = cols + 16
    made = rows // 2
    pairs_in, pairs_out = made // 4 + 1, made // 4
    hidden_pairs = made // 2 + 1
    if hidden_pairs % pairs_in:
        hidden_pairs += pairs_in - hidden_pairs % pairs_in
    state_pairs = hidden_pairs + 1
    base = rows - made - 2 if lower else -2

    def body(shifted_ref, near_ref, cross_ref, w_in, w_out, b_in, b_out, out_ref,
             line, state_sh, hid, hid_sh):
        band, sect = here()
        row0 = band * rows + base + 1
        col0 = sect * cols - 1

        for pair in range(made // 2 + 2, state_pairs):
            for b in range(3):
                state_sh[b, pair] = jnp.zeros((2, loose, LANES), HALF)
        edge = made // 2 + 1 if lower else 0
        skip = 0 if lower else 1
        given = made // 2 + 1
        at = (rows - made) // 2 - 1 if lower else 0
        for b in range(3):
            state_sh[b, skip : skip + given] = shifted_ref[b, at : at + given]
        pair = jnp.bitwise_and(band, 1) == (0 if lower else 1)
        for v in range(2):
            rim = jnp.where(pair, near_ref[v], cross_ref[v])
            value = jnp.concatenate(
                [rim.astype(FULL), jnp.zeros((LANES - deep, width), FULL)], axis=0
            ).T
            line[v, 8 : 8 + cols] = value[:cols]
            line[v, 8 + cols :] = value[cols : cols + 16]
            line[v, :8] = value[width - 8 :]
            for b in range(3):
                state_sh[b, edge, v] = line[v, 6 + b : 6 + b + loose, :].astype(HALF)

        def first(chunk, carry):
            start = chunk * pairs_in
            value = product(gather_pairs(state_sh, start, pairs_in), w_in[...])
            value = silu(value + b_in[...]).reshape(pairs_in, loose, 2 * LANES)
            pair = lax.broadcasted_iota(jnp.int32, value.shape, 0)
            col = lax.broadcasted_iota(jnp.int32, value.shape, 1)
            odd = (lane_index(value.shape) >= LANES).astype(jnp.int32)
            grid_row = row0 + 2 * (start + pair) + odd
            grid_col = col0 + col
            keep = (
                (grid_row >= 0) & (grid_row < limits[0])
                & (grid_col >= 0) & (grid_col < limits[1])
            )
            value = jnp.where(keep, value, 0.0)
            hid[:, 0] = value[:, :, :LANES]
            hid[:, 1] = value[:, :, LANES:]
            for b in range(3):
                hid_sh[b, pl.ds(start, pairs_in)] = hid[:, :, b : b + cols, :].astype(HALF)
            return carry

        lax.fori_loop(0, hidden_pairs // pairs_in, first, 0)

        def second(chunk, carry):
            start = chunk * pairs_out
            value = product(gather_pairs(hid_sh, start, pairs_out), w_out[...]) + b_out[...]
            value = value.reshape(pairs_out, cols, 2 * LANES)
            for k in range(pairs_out):
                for v in range(2):
                    center = state_sh[2, start + k + 1, v, :cols, :].astype(FULL)
                    mean = center + value[k, :, v * LANES : (v + 1) * LANES]
                    out_ref[2 * (start + k) + v] = mean.T[:padded].astype(HALF)
            return carry

        lax.fori_loop(0, made // 2 // pairs_out, second, 0)

    return run(
        body,
        [like((made, padded, cols))],
        [shifted, near, cross, *weights, *biases],
        [
            pltpu.VMEM((2, loose + 8, LANES), FULL),
            pltpu.VMEM((3, state_pairs, 2, loose, LANES), HALF),
            pltpu.VMEM((pairs_in, 2, loose, LANES), FULL),
            pltpu.VMEM((3, hidden_pairs, 2, cols, LANES), HALF),
        ],
        micros=3.5,
    )[0]


def canvas(anchor, pieces, sources, place, sects, rows, cols):
    padded = pieces[0].shape[-2]
    deep = -(-padded // 16) * 16
    total = anchor.shape[1]
    slots = len(pieces)
    tile_rows = LANES // SIDE
    groups = rows // tile_rows

    def body(at_ref, *refs):
        band, sect = here()
        place_ref, spill_ref, out_ref, inverse_ref, view = refs[slots:]
        none = jnp.zeros((padded, LANES), HALF)
        anchors = slot_anchors(at_ref, sources, sects, rows, cols)
        for piece, j, (row0, _) in zip(refs, sources, anchors):
            lanes = slice(j * LANES, (j + 1) * LANES)
            for r in range(rows):
                i = r - row0
                tile = jnp.clip(jnp.right_shift(i, tile_rows.bit_length() - 1), 0, SIDE // tile_rows - 1)
                value = piece[:, pl.ds(pl.multiple_of(tile * LANES, LANES), LANES)]
                inside = (i >= 0) & (i < SIDE)
                view[r % tile_rows, r // tile_rows, :padded, lanes] = jnp.where(
                    inside, value, none
                )
        view[:, :, padded:, :] = jnp.zeros(
            (tile_rows, groups, deep - padded, slots * LANES), HALF
        )
        spilled = None
        for m in range(tile_rows):
            value = jnp.dot(
                view[m].reshape(groups * deep, slots * LANES), place_ref[m],
                preferred_element_type=FULL,
            ).reshape(groups, deep, 2 * LANES)
            for k in range(groups):
                out_ref[k * tile_rows + m] = value[k, :padded, :LANES]
            part = value[:, :padded, LANES:]
            spilled = part if spilled is None else spilled + part
        for k in range(groups):
            spill_ref[:, k * LANES : (k + 1) * LANES] = spilled[k].astype(HALF)
        tall, wide = (rows, total), (total, cols)
        down = lax.broadcasted_iota(jnp.int32, tall, 0) + band * rows - at_ref[0:1, :]
        across = lane_index(wide) + sect * cols - at_ref[1:2, :].astype(FULL).T.astype(jnp.int32)
        down = jnp.where((down >= 0) & (down < SIDE), 1.0, 0.0)
        across = jnp.where((across >= 0) & (across < SIDE), 1.0, 0.0)
        count = jnp.dot(down.astype(HALF), across.astype(HALF), preferred_element_type=FULL)
        inverse_ref[...] = 1.0 / jnp.maximum(count, 1.0)

    return run(
        body,
        [
            like((padded, rows * SIDE)),
            like((rows, padded, cols), FULL),
            like((rows, cols), FULL),
        ],
        [anchor, *pieces, place],
        [pltpu.VMEM((tile_rows, groups, deep, slots * LANES), HALF)],
        micros=1.5
    )


def finish(means, summed, arrived, inverse, channels):
    rows, padded, cols = summed.shape
    deep = -(-padded // 16) * 16
    half = means[0].shape[0]
    chunk = 8

    def body(top_ref, low_ref, sum_ref, spill_ref, inverse_ref, out_ref, flat, ready, sems):
        lane = lane_index((padded, LANES))
        none = jnp.zeros((padded, LANES), HALF)
        reach = jnp.where(here()[1] > 0, SIDE, 0)
        flat[:, padded:] = jnp.zeros((chunk, deep - padded, cols), HALF)
        copies = []
        for first in range(0, rows, chunk):
            for r in range(first, first + chunk):
                at, low = divmod(r * SIDE, LANES)
                extra = spill_ref[:, at * LANES : (at + 1) * LANES]
                if low:
                    extra = pltpu.roll(extra, LANES - low, 1)
                extra = jnp.where(lane < reach, extra, none).astype(FULL)
                mean = top_ref[r] if r < half else low_ref[r - half]
                value = mean.astype(FULL) + (sum_ref[r] + extra) * inverse_ref[r : r + 1]
                flat[r - first, :padded] = value.astype(HALF)
            k = first // chunk
            ready[k] = jnp.swapaxes(flat[...], 0, 1)[:channels]
            copies.append(
                pltpu.make_async_copy(
                    ready.at[k], out_ref.at[:, pl.ds(first, chunk), :], sems.at[k]
                )
            )
            copies[-1].start()
        for copy in copies:
            copy.wait()

    return run(
        body,
        [like((channels, rows, cols))],
        [*means, summed, arrived, inverse],
        [
            pltpu.VMEM((chunk, deep, cols), HALF),
            pltpu.VMEM((rows // chunk, channels, chunk, cols), HALF),
            pltpu.SemaphoreType.DMA((rows // chunk,)),
        ],
        micros=2.0,
        out_space=pltpu.HBM,
    )[0]


def step(
    state_field,
    conv_in_weight,
    conv_in_bias,
    conv_out_weight,
    conv_out_bias,
    patch_anchor,
    patch_noise,
    denoise_in_weight,
    step_bias,
    denoise_out_weight,
    denoise_bias,
):
    bands = lax.axis_size("band")
    sects = lax.axis_size("sect")
    channels, rows, cols = state_field.shape
    limits = (rows * bands, cols * sects)

    anchor = patch_anchor.T

    right_rim, left_rim, turned = pack(state_field)
    right = cycle_from(right_rim, "sect", -1)
    left = cycle_from(left_rim, "sect", 1)

    made, lines, noise = prep(
        [
            conv_in_weight.transpose(0, 2, 1),
            conv_out_weight,
            denoise_in_weight.transpose(0, 2, 1),
            denoise_out_weight,
        ],
        [conv_in_bias[None, :], conv_out_bias[None, :], denoise_bias[None, :], step_bias],
        patch_noise[0],
    )
    biases, step_lines = lines[:3], lines[3]

    padded = right_rim.shape[0]
    pick, place = picks(anchor, bands, sects, rows, cols)
    parts = extract_own(anchor, turned, pick, padded, bands, sects)
    own, kept, own_sent, sent, edge_near, edge_cross = extract_rim(
        anchor, parts, turned, right, left, pick, bands, sects
    )
    addends = [own]
    if bands > 2:
        got = swap(sent, "band", 1)
        kept = add_parts(kept, got)
    bit = 2
    while bit < bands:
        got = swap(kept[0::2], "band", bit)
        addends.append(got)
        kept = kept[1::2] + got[1:]
        bit *= 2
    addends.append(swap(own_sent, "band", 1))
    rim_near = swap(edge_near, "band", 1)
    steps = [(i, i + 1) for i in range(1, bands - 1, 2)]
    rim_cross = lax.ppermute(edge_cross, "band", steps + [(j, i) for i, j in steps])
    correction = patch_step(
        anchor, addends, noise, made, biases, step_lines, sects, limits
    )
    pieces = [correction]
    sources = [0]
    bit = bands // 2
    while bit:
        fresh = []
        for piece in pieces:
            fresh.append(swap(piece, "band", bit))
        pieces += fresh
        sources += [s ^ bit for s in sources]
        bit //= 2

    shifted = spread(turned, right, left, sects)
    top_mean = grid_mean(shifted, rim_near, rim_cross, False, padded, made[:2], biases[:2], limits)
    low_mean = grid_mean(shifted, rim_near, rim_cross, True, padded, made[:2], biases[:2], limits)
    spilled, summed, inverse = canvas(
        anchor, pieces, sources, place, sects, rows, cols
    )
    arrived = cycle_from(spilled, "sect", 1)
    return finish([top_mean, low_mean], summed, arrived, inverse, channels)


def solution(mesh):
    placed = (
        P("groups", "band", "sect"),
        P(),
        P(),
        P(),
        P(),
        P("groups", None),
        P(("groups", "band", "sect"), None, None, None),
        P(),
        P(),
        P(),
        P(),
    )
    return jax.shard_map(
        step,
        mesh=mesh,
        in_specs=placed,
        out_specs=P("groups", "band", "sect"),
        check_vma=False,
    )
```

```python
import jax
import jax.numpy as jnp
from jax import lax
from jax.experimental import pallas as pl
from jax.experimental.pallas import tpu as pltpu
from jax.sharding import PartitionSpec as P


SIDE = 32
WIDE = SIDE + 4
PER_TILE = 3
TILES = WIDE // PER_TILE
LANES = 128
REACH = SIDE + 2
CHUNKS = 1
HALF = jnp.bfloat16
FULL = jnp.float32


def shift_from(block, axis, distance):
    count = lax.axis_size(axis)
    route = [(i - distance, i) for i in range(count) if 0 <= i - distance < count]
    return lax.ppermute(block, axis, route)


def swap(block, axis, bit):
    count = lax.axis_size(axis)
    return lax.ppermute(block, axis, [(i, i ^ bit) for i in range(count)])


def run(body, outs, ins, scratch, micros=1.0, limit=16, out_space=pltpu.VMEM):
    return pl.pallas_call(
        body,
        out_shape=outs,
        in_specs=[pl.BlockSpec(memory_space=pltpu.VMEM)] * len(ins),
        out_specs=[pl.BlockSpec(memory_space=out_space)] * len(outs),
        scratch_shapes=scratch,
        cost_estimate=pl.CostEstimate(
            flops=int(micros * 1.15e9), bytes_accessed=1024, transcendentals=0
        ),
        compiler_params=pltpu.CompilerParams(vmem_limit_bytes=limit * 1024 * 1024),
    )(*ins)


def arrival(bands):
    slots, bit = [0], bands // 2
    while bit:
        slots += [slot ^ bit for slot in slots]
        bit //= 2
    return slots


def here():
    return lax.axis_index("band"), lax.axis_index("sect")


def slots_at(at_ref, readers, sects, rows, cols):
    band, sect = here()
    count = at_ref.shape[1]
    bits = (cols * sects - 1).bit_length()
    both = jnp.left_shift(at_ref[0:1, :], bits) + at_ref[1:2, :]
    lane = lane_index((1, count))
    found = []
    for reader in readers:
        mine = lane == reader * sects + sect
        code = jnp.sum(jnp.where(mine, both, 0).astype(FULL)).astype(jnp.int32)
        row, col = jnp.right_shift(code, bits), jnp.bitwise_and(code, (1 << bits) - 1)
        found.append((row - band * rows, col - sect * cols))
    return found


def slot_anchors(at_ref, slots, sects, rows, cols):
    band, _ = here()
    return slots_at(at_ref, [jnp.bitwise_xor(band, j) for j in slots], sects, rows, cols)


def like(shape, dtype=HALF):
    return jax.ShapeDtypeStruct(shape, dtype)


def lane_index(shape):
    return lax.broadcasted_iota(jnp.int32, shape, len(shape) - 1)


def turn_rows(state_ref, flat):
    channels = state_ref.shape[0]
    flat[:channels] = state_ref[...]
    flat[channels:] = jnp.zeros((flat.shape[0] - channels,) + flat.shape[1:], HALF)
    return jnp.swapaxes(flat[...], 0, 1)


def pack(state):
    channels, rows, cols = state.shape
    padded = -(-channels // 8) * 8
    deep = -(-padded // 16) * 16
    span = -(-rows * REACH // LANES)

    def body(state_ref, right_ref, left_ref, rows_ref, flat):
        turned = turn_rows(state_ref, flat)
        rows_ref[...] = turned
        lane = lane_index((deep, LANES))
        tiles = [None] * span
        rim = jnp.zeros((deep, LANES), HALF)
        for r in range(rows):
            row = turned[r]
            at, off = divmod(r * REACH, LANES)
            moved = row if off == 0 else pltpu.roll(row, off, 1)
            if tiles[at] is None:
                tiles[at] = moved
            else:
                tiles[at] = jnp.where(lane >= off, moved, tiles[at])
            if off + REACH > LANES:
                tiles[at + 1] = moved
            moved = pltpu.roll(row, (2 * r + 2) % LANES, 1)
            rim = jnp.where((lane >= 2 * r) & (lane < 2 * r + 2), moved, rim)
        for at in range(span):
            right_ref[:, at * LANES : (at + 1) * LANES] = tiles[at][:padded]
        left_ref[...] = rim[:padded]

    return run(
        body,
        [like((padded, span * LANES)), like((padded, LANES)), like((rows, deep, cols))],
        [state],
        [pltpu.VMEM((deep, rows, cols), HALF)],
        micros=1.0,
    )


def prep(anchor, weights, biases, noise, bands, sects, rows, cols):
    steps, channels, cells = noise.shape
    count = len(weights)
    tile_rows = LANES // SIDE
    lines = len(biases)

    def body(at_ref, *refs):
        ins, lines_in, noise_ref = refs[:count], refs[count : count + lines], refs[count + lines]
        outs = refs[count + lines + 1 :]
        lines_out, noise_out = outs[count : count + lines], outs[count + lines]
        place_ref = outs[count + lines + 1]
        for k, (w_ref, o_ref) in enumerate(zip(ins, outs)):
            _, down, across = w_ref.shape
            o_ref[...] = jnp.zeros(o_ref.shape, HALF)
            for v in range(2):
                for a in range(3):
                    for b in range(3):
                        tap = (3 * (a + v) + b) * LANES
                        row, col = (v * LANES, tap) if k % 2 else (tap, v * LANES)
                        o_ref[row : row + down, col : col + across] = w_ref[3 * a + b]
        for line_ref, o_ref in zip(lines_in, lines_out):
            used = line_ref.shape[1]
            o_ref[...] = jnp.zeros(o_ref.shape, FULL)
            o_ref[:, :used] = line_ref[...]
            o_ref[:, LANES : LANES + used] = line_ref[...]
        for k in range(steps):
            for t in range(cells // LANES):
                block = noise_ref[k, :, t * LANES : (t + 1) * LANES].astype(FULL)
                block = jnp.concatenate(
                    [block, jnp.zeros((LANES - channels, LANES), FULL)], axis=0
                ).T.astype(HALF)
                for m in range(tile_rows):
                    r = t * tile_rows + m
                    noise_out[
                        k, r // 2 * SIDE : (r // 2 + 1) * SIDE, r % 2 * LANES : (r % 2 + 1) * LANES
                    ] = block[m * SIDE : (m + 1) * SIDE]
        cell = lax.broadcasted_iota(jnp.int32, (LANES, 2 * LANES), 0)
        target = lane_index((LANES, 2 * LANES))
        anchors = slot_anchors(at_ref, arrival(bands), sects, rows, cols)
        for j, (row0, col0) in enumerate(anchors):
            across = jnp.bitwise_and(cell, SIDE - 1) + col0
            for m in range(tile_rows):
                turn = jnp.bitwise_and(m - row0, tile_rows - 1)
                there = jnp.where(across < cols, across, across - cols + LANES + m * SIDE)
                hit = (target == there) & (cell >= turn * SIDE) & (cell < (turn + 1) * SIDE)
                place_ref[m, j * LANES : (j + 1) * LANES] = jnp.where(hit, 1.0, 0.0).astype(HALF)

    sizes = [(12 * LANES, 2 * LANES), (2 * LANES, 12 * LANES)]
    made = [like(sizes[k % 2]) for k in range(count)]
    made += [like((line.shape[0], 2 * LANES), FULL) for line in biases]
    made += [like((steps, cells // 2, 2 * LANES))]
    made += [like((tile_rows, bands * LANES, 2 * LANES))]
    out = run(body, made, [anchor, *weights, *biases, noise], [], micros=1.5)
    return out[:count], out[count : count + lines], *out[count + lines :]


def picks(anchor, bands, sects, rows, cols):
    width = cols + LANES

    def body(at_ref, pick_ref):
        source = lax.broadcasted_iota(jnp.int32, (width, LANES), 0)
        inner = lane_index((width, LANES))
        for _ in range(1, PER_TILE):
            inner = jnp.where(inner >= WIDE, inner - WIDE, inner)
        anchors = slot_anchors(at_ref, range(bands), sects, rows, cols)
        for j, (row0, col0) in enumerate(anchors):
            want = jnp.bitwise_and(inner + (col0 - 2), width - 1)
            pick_ref[:, j * LANES : (j + 1) * LANES] = jnp.where(source == want, 1.0, 0.0).astype(HALF)

    return run(body, [like((width, bands * LANES))], [anchor], [], micros=0.4)[0]


def add_parts(kept, got):
    def body(kept_ref, got_ref, out_ref):
        out_ref[...] = kept_ref[...] + got_ref[...]

    return run(body, [like(kept.shape)], [kept, got], [], micros=0.3)[0]


def window_tile(picked, t, row0, rows, padded, lanes):
    zone = lane_index((padded, LANES))
    total = jnp.zeros((padded, LANES), FULL)
    for m in range(PER_TILE):
        r = row0 + t * PER_TILE + m
        low = jnp.where((r >= 0) & (r < rows), WIDE * m, 2 * LANES)
        keep = (zone >= low) & (zone < WIDE * (m + 1))
        value = picked[jnp.clip(r, 0, rows - 1), :padded, lanes]
        total = jnp.where(keep, value, total)
    return total.astype(HALF)


def batches(bands):
    size = 4 if bands % 4 == 0 else bands
    return [range(first, first + size) for first in range(0, bands, size)], size


def select_rows(source, pick, picked):
    rows, deep, _ = source.shape
    chunk = rows // 2

    def select(c, carry):
        view = source[pl.ds(c * chunk, chunk)].reshape(chunk * deep, LANES)
        picked[pl.ds(c * chunk, chunk)] = jnp.dot(
            view, pick, preferred_element_type=FULL
        ).reshape(chunk, deep, pick.shape[1])
        return carry

    lax.fori_loop(0, rows // chunk, select, 0)


def extract_own(anchor, turned, pick, padded, bands, sects):
    rows, deep, cols = turned.shape
    groups, size = batches(bands)

    def body(at_ref, rows_ref, pick_ref, out_ref, picked):
        anchors = slot_anchors(at_ref, range(bands), sects, rows, cols)
        for group in groups:
            select_rows(rows_ref, pick_ref[:cols, group[0] * LANES : (group[-1] + 1) * LANES], picked)
            for j in group:
                row0 = anchors[j][0] - 2
                inside = (row0 > -WIDE) & (row0 < rows)

                @pl.when(inside)
                def _(j=j, row0=row0, at=(j - group[0]) * LANES):
                    for t in range(TILES):
                        out_ref[j, :, t * LANES : (t + 1) * LANES] = window_tile(
                            picked, t, row0, rows, padded, slice(at, at + LANES)
                        )

                @pl.when(jnp.logical_not(inside))
                def _(j=j):
                    out_ref[j] = jnp.zeros((padded, TILES * LANES), HALF)

    return run(
        body,
        [like((bands, padded, TILES * LANES))],
        [anchor, turned, pick],
        [pltpu.VMEM((rows, deep, size * LANES), FULL)],
        micros=1.5
    )[0]


def extract_rim(anchor, parts, turned, right, left, pick, bands, sects):
    rows, deep, cols = turned.shape
    padded = right.shape[0]

    def body(at_ref, part_ref, rows_ref, right_ref, left_ref, pick_ref,
             own_ref, low_ref, odd_ref, high_ref, near_ref, cross_ref, ext, picked):
        lane = lane_index((padded, LANES))
        none = jnp.zeros((padded, LANES), HALF)
        rim = left_ref[...]

        def expand(r):
            at, off = divmod(r * REACH, LANES)
            piece = right_ref[:, at * LANES : (at + 1) * LANES]
            if off:
                piece = pltpu.roll(piece, LANES - off, 1)
            if off + REACH > LANES:
                after = right_ref[:, (at + 1) * LANES : (at + 2) * LANES]
                piece = jnp.where(lane < LANES - off, piece, pltpu.roll(after, LANES - off, 1))
            turn = pltpu.roll(rim, (LANES - 2 - 2 * r) % LANES, 1)
            ext[r, :padded] = jnp.where(
                lane < REACH, piece, jnp.where(lane >= LANES - 2, turn, none)
            )

        ext[:, padded:] = jnp.zeros((rows, deep - padded, LANES), HALF)
        outer = (0, 1, rows - 2, rows - 1)
        for r in outer:
            expand(r)
        even = jnp.bitwise_and(here()[0], 1) == 0
        for k in range(2):
            top, low = k, rows - 2 + k
            near_ref[k, :, :cols] = jnp.where(even, rows_ref[low], rows_ref[top])
            near_ref[k, :, cols:] = jnp.where(even, ext[low], ext[top])
            cross_ref[k, :, :cols] = jnp.where(even, rows_ref[top], rows_ref[low])
            cross_ref[k, :, cols:] = jnp.where(even, ext[top], ext[low])

        def target(j):
            if j < 2:
                return (own_ref, odd_ref)[j], 0
            return (low_ref, high_ref)[j % 2], j // 2 - 1

        crossing = []
        anchors = slot_anchors(at_ref, range(bands), sects, rows, cols)
        for j, (row0, col0) in enumerate(anchors):
            row0 = row0 - 2
            inside = (row0 > -WIDE) & (row0 < rows)
            over = inside & ((col0 < 2) | (col0 > cols - REACH))
            crossing.append((row0, over))
            out_ref, at = target(j)
            out_ref[at] = part_ref[j]
        some = crossing[0][1]
        for _, over in crossing[1:]:
            some = some | over

        @pl.when(some)
        def _():
            for r in range(rows):
                if r not in outer:
                    expand(r)

        for j in range(bands):
            out_ref, at = target(j)
            row0, over = crossing[j]

            @pl.when(over)
            def _(j=j, out_ref=out_ref, at=at, row0=row0):
                select_rows(ext, pick_ref[cols:, j * LANES : (j + 1) * LANES], picked)
                for t in range(TILES):
                    out_ref[at, :, t * LANES : (t + 1) * LANES] += window_tile(
                        picked, t, row0, rows, padded, slice(0, LANES)
                    )

    one = like((1, padded, TILES * LANES))
    rest = like((max(bands // 2 - 1, 1), padded, TILES * LANES))
    edge = like((2, deep, cols + LANES))
    return run(
        body,
        [one, rest, one, rest, edge, edge],
        [anchor, parts, turned, right, left, pick],
        [pltpu.VMEM((rows, deep, LANES), HALF), pltpu.VMEM((rows, deep, LANES), FULL)],
        micros=1.5
    )


def product(view, weight):
    turned = weight.shape[0] == 2 * LANES
    return lax.dot_general(
        view, weight, (((1,), (1 if turned else 0,)), ((), ())), preferred_element_type=FULL
    )


def gather_pairs(shifted, first, count):
    view = jnp.concatenate(
        [shifted[b, pl.ds(first + u, count), v] for u in (0, 1) for v in (0, 1) for b in (0, 1, 2)],
        axis=-1,
    )
    return view.reshape(count * view.shape[1], view.shape[2])


def silu(value):
    return value / (1.0 + jnp.exp(-value))


def patch_step(anchor, addends, noise, weights, biases, step_bias, sects, limits):
    padded = addends[0].shape[1]
    steps = noise.shape[0]
    half = SIDE // 2
    loose = 48

    def body(*refs):
        at_ref, parts = refs[0], refs[1 : 1 + len(addends)]
        band, sect = here()
        mine = lane_index(at_ref.shape) == band * sects + sect
        at = jnp.sum(jnp.where(mine, at_ref[...], 0).astype(FULL), axis=1, keepdims=True)
        row0, col0 = at.astype(jnp.int32)[0:1][None], at.astype(jnp.int32)[1:2][None]
        (noise_ref, w_in, w_out, d_in, d_out, b_in, b_out, b_step, b_den, out_ref,
         flat, state_sh, hid, hid_sh, pad, pad_sh, corr, state) = refs[1 + len(addends) :]
        for t in range(TILES):
            lanes = slice(t * LANES, (t + 1) * LANES)
            tile = parts[0][0, :, lanes].astype(FULL)
            for part in parts[1:]:
                tile = tile + part[0, :, lanes].astype(FULL)
            tile = jnp.concatenate([tile, jnp.zeros((LANES - padded, LANES), FULL)], axis=0)
            flat[lanes, :] = tile.T
        for i in range(WIDE):
            t, m = divmod(i, PER_TILE)
            off = t * LANES + m * WIDE
            for b in range(3):
                state_sh[b, i // 2, i % 2] = flat[off + b : off + b + loose, :].astype(HALF)
        pairs = half + 1
        value = product(gather_pairs(state_sh, 0, pairs), w_in[...])
        value = silu(value + b_in[...]).reshape(pairs, loose, 2 * LANES)
        pair = lax.broadcasted_iota(jnp.int32, value.shape, 0)
        col = lax.broadcasted_iota(jnp.int32, value.shape, 1)
        odd = (lane_index(value.shape) >= LANES).astype(jnp.int32)
        grid_row = row0 - 1 + 2 * pair + odd
        grid_col = col0 - 1 + col
        keep = (
            (grid_row >= 0) & (grid_row < limits[0])
            & (grid_col >= 0) & (grid_col < limits[1]) & (col < SIDE + 2)
        )
        value = jnp.where(keep, value, 0.0)
        hid[:, 0] = value[:, :, :LANES]
        hid[:, 1] = value[:, :, LANES:]
        for b in range(3):
            hid_sh[b] = hid[:, :, b : b + SIDE, :].astype(HALF)
        value = product(gather_pairs(hid_sh, 0, half), w_out[...])
        center = jnp.concatenate(
            [state_sh[2, 1 : 1 + half, v, :SIDE, :] for v in (0, 1)], axis=-1
        ).astype(FULL).reshape(half * SIDE, 2 * LANES)
        mean = (center + value + b_out[...]).astype(HALF).astype(FULL)
        state[...] = mean + noise_ref[0].astype(FULL)
        pad[...] = jnp.zeros(pad.shape, FULL)
        deal = half // CHUNKS
        trips = jnp.where(band >= 0, CHUNKS, 0)

        def fill(source, first, count):
            shaped = source.reshape(count, SIDE, 2 * LANES)
            pad[pl.ds(first, count), 1, 8 : 8 + SIDE] = shaped[:, :, :LANES]
            pad[pl.ds(first + 1, count), 0, 8 : 8 + SIDE] = shaped[:, :, LANES:]

        def shift():
            for b in range(3):
                pad_sh[b] = pad[:, :, 7 + b : 7 + b + SIDE, :].astype(HALF)

        for step in range(steps):
            fill(state[...], 0, half)
            shift()

            def first(c, carry, step=step):
                value = product(gather_pairs(pad_sh, c * deal, deal), d_in[...])
                fill(silu(value + b_step[step : step + 1]), c * deal, deal)
                return carry

            lax.fori_loop(0, trips, first, 0)
            shift()

            def second(c, carry, step=step):
                value = product(gather_pairs(pad_sh, c * deal, deal), d_out[...])
                cells = pl.ds(pl.multiple_of(c * deal * SIDE, deal * SIDE), deal * SIDE)
                value = state[cells] - 0.5 * (value + b_den[...])
                if step + 1 < steps:
                    value = value + 0.5 * noise_ref[step + 1, cells].astype(FULL)
                state[cells] = value
                return carry

            lax.fori_loop(0, trips, second, 0)
        change = (state[...] - mean).reshape(half, SIDE, 2 * LANES)
        corr[:, 0] = change[:, :, :LANES]
        corr[:, 1] = change[:, :, LANES:]
        cells = corr[...].reshape(SIDE * SIDE, LANES)
        for t in range(SIDE * SIDE // LANES):
            lanes = slice(t * LANES, (t + 1) * LANES)
            out_ref[:, lanes] = cells[lanes].T[:padded].astype(HALF)

    return run(
        body,
        [like((padded, SIDE * SIDE))],
        [anchor, *addends, noise, *weights, *biases[:2], step_bias, biases[2]],
        [
            pltpu.VMEM((TILES * LANES, LANES), FULL),
            pltpu.VMEM((3, WIDE // 2, 2, loose, LANES), HALF),
            pltpu.VMEM((half + 1, 2, loose, LANES), FULL),
            pltpu.VMEM((3, half + 1, 2, SIDE, LANES), HALF),
            pltpu.VMEM((half + 1, 2, loose, LANES), FULL),
            pltpu.VMEM((3, half + 1, 2, SIDE, LANES), HALF),
            pltpu.VMEM((half, 2, SIDE, LANES), FULL),
            pltpu.VMEM((half * SIDE, 2 * LANES), FULL),
        ],
        micros=8.0
    )[0]


def spread(turned, right, left):
    rows, _, cols = turned.shape
    span = right.shape[1]
    loose = cols + 16

    def body(rows_ref, right_ref, left_ref, out_ref, after, before, line):
        def upright(value):
            value = value.astype(FULL)
            return jnp.concatenate(
                [value, jnp.zeros((LANES - value.shape[0], value.shape[1]), FULL)], axis=0
            ).T

        for t in range(span // LANES):
            lanes = slice(t * LANES, (t + 1) * LANES)
            after[lanes] = upright(right_ref[:, lanes])
        before[...] = upright(left_ref[...])
        line[...] = jnp.zeros(line.shape, FULL)

        def spread_rows(i, carry):
            for v in range(2):
                r = 2 * i + v
                line[v, 8 : 8 + cols] = upright(rows_ref[r])
                line[v, 8 + cols : 10 + cols] = after[pl.ds(r * REACH, 2)]
                line[v, 6:8] = before[pl.ds(2 * r, 2)]
                for b in range(3):
                    out_ref[b, i, v] = line[v, 6 + b : 6 + b + loose, :].astype(HALF)
            return carry

        lax.fori_loop(0, rows // 2, spread_rows, 0)

    return run(
        body,
        [like((3, rows // 2, 2, loose, LANES))],
        [turned, right, left],
        [
            pltpu.VMEM((span, LANES), FULL),
            pltpu.VMEM((LANES, LANES), FULL),
            pltpu.VMEM((2, loose + 8, LANES), FULL),
        ],
        micros=2.5
    )[0]


def grid_mean(shifted, near, cross, lower, padded, weights, biases, limits):
    rows = 2 * shifted.shape[1]
    _, deep, width = near.shape
    cols = width - LANES
    loose = cols + 16
    made = rows // 2
    pairs_in, pairs_out = made // 4 + 1, made // 4
    hidden_pairs = made // 2 + 1
    if hidden_pairs % pairs_in:
        hidden_pairs += pairs_in - hidden_pairs % pairs_in
    state_pairs = hidden_pairs + 1
    base = rows - made - 2 if lower else -2

    def body(shifted_ref, near_ref, cross_ref, w_in, w_out, b_in, b_out, out_ref,
             line, state_sh, hid, hid_sh):
        band, sect = here()
        row0 = band * rows + base + 1
        col0 = sect * cols - 1

        for pair in range(made // 2 + 2, state_pairs):
            for b in range(3):
                state_sh[b, pair] = jnp.zeros((2, loose, LANES), HALF)
        edge = made // 2 + 1 if lower else 0
        skip = 0 if lower else 1
        given = made // 2 + 1
        at = (rows - made) // 2 - 1 if lower else 0
        for b in range(3):
            state_sh[b, skip : skip + given] = shifted_ref[b, at : at + given]
        pair = jnp.bitwise_and(band, 1) == (0 if lower else 1)
        for v in range(2):
            rim = jnp.where(pair, near_ref[v], cross_ref[v])
            value = jnp.concatenate(
                [rim.astype(FULL), jnp.zeros((LANES - deep, width), FULL)], axis=0
            ).T
            line[v, 8 : 8 + cols] = value[:cols]
            line[v, 8 + cols :] = value[cols : cols + 16]
            line[v, :8] = value[width - 8 :]
            for b in range(3):
                state_sh[b, edge, v] = line[v, 6 + b : 6 + b + loose, :].astype(HALF)

        def first(chunk, carry):
            start = chunk * pairs_in
            value = product(gather_pairs(state_sh, start, pairs_in), w_in[...])
            value = silu(value + b_in[...]).reshape(pairs_in, loose, 2 * LANES)
            pair = lax.broadcasted_iota(jnp.int32, value.shape, 0)
            col = lax.broadcasted_iota(jnp.int32, value.shape, 1)
            odd = (lane_index(value.shape) >= LANES).astype(jnp.int32)
            grid_row = row0 + 2 * (start + pair) + odd
            grid_col = col0 + col
            keep = (
                (grid_row >= 0) & (grid_row < limits[0])
                & (grid_col >= 0) & (grid_col < limits[1])
            )
            value = jnp.where(keep, value, 0.0)
            hid[:, 0] = value[:, :, :LANES]
            hid[:, 1] = value[:, :, LANES:]
            for b in range(3):
                hid_sh[b, pl.ds(start, pairs_in)] = hid[:, :, b : b + cols, :].astype(HALF)
            return carry

        lax.fori_loop(0, hidden_pairs // pairs_in, first, 0)

        def second(chunk, carry):
            start = chunk * pairs_out
            value = product(gather_pairs(hid_sh, start, pairs_out), w_out[...]) + b_out[...]
            value = value.reshape(pairs_out, cols, 2 * LANES)
            for k in range(pairs_out):
                for v in range(2):
                    center = state_sh[2, start + k + 1, v, :cols, :].astype(FULL)
                    mean = center + value[k, :, v * LANES : (v + 1) * LANES]
                    out_ref[2 * (start + k) + v] = mean.T[:padded].astype(HALF)
            return carry

        lax.fori_loop(0, made // 2 // pairs_out, second, 0)

    return run(
        body,
        [like((made, padded, cols))],
        [shifted, near, cross, *weights, *biases],
        [
            pltpu.VMEM((2, loose + 8, LANES), FULL),
            pltpu.VMEM((3, state_pairs, 2, loose, LANES), HALF),
            pltpu.VMEM((pairs_in, 2, loose, LANES), FULL),
            pltpu.VMEM((3, hidden_pairs, 2, cols, LANES), HALF),
        ],
        micros=3.5,
    )[0]


def fill_view(view, at_ref, pieces, sources, sects, rows, cols):
    padded = pieces[0].shape[-2]
    tile_rows = view.shape[0]
    none = jnp.zeros((padded, LANES), HALF)
    anchors = slot_anchors(at_ref, sources, sects, rows, cols)
    for at, (piece, (row0, _)) in enumerate(zip(pieces, anchors)):
        lanes = slice(at * LANES, (at + 1) * LANES)
        for r in range(rows):
            i = r - row0
            tile = jnp.clip(
                jnp.right_shift(i, tile_rows.bit_length() - 1), 0, SIDE // tile_rows - 1
            )
            value = piece[:, pl.ds(pl.multiple_of(tile * LANES, LANES), LANES)]
            inside = (i >= 0) & (i < SIDE)
            view[r % tile_rows, r // tile_rows, :padded, lanes] = jnp.where(inside, value, none)
    view[:, :, padded:, :] = jnp.zeros(
        view.shape[:2] + (view.shape[2] - padded, view.shape[3]), HALF
    )


def view_shape(pieces, rows):
    tile_rows = LANES // SIDE
    deep = -(-pieces[0].shape[-2] // 16) * 16
    return (tile_rows, rows // tile_rows, deep, len(pieces) * LANES)


def gather_view(anchor, pieces, sources, sects, rows, cols):
    def body(at_ref, *refs):
        fill_view(refs[-1], at_ref, refs[:-1], sources, sects, rows, cols)

    shape = view_shape(pieces, rows)
    return run(body, [like(shape)], [anchor, *pieces], [], micros=0.8)[0]


def canvas(anchor, early, pieces, sources, place, sects, rows, cols):
    padded = pieces[0].shape[-2]
    deep = -(-padded // 16) * 16
    total = anchor.shape[1]
    slots = len(pieces)
    tile_rows = LANES // SIDE
    groups = rows // tile_rows

    def body(at_ref, *refs):
        band, sect = here()
        early_ref, place_ref, spill_ref, out_ref, inverse_ref, view = refs[slots:]
        fill_view(view, at_ref, refs[:slots], sources, sects, rows, cols)
        spilled = None
        for m in range(tile_rows):
            both = jnp.concatenate([early_ref[m], view[m]], axis=-1)
            value = jnp.dot(
                both.reshape(groups * deep, both.shape[-1]), place_ref[m],
                preferred_element_type=FULL,
            ).reshape(groups, deep, 2 * LANES)
            for k in range(groups):
                out_ref[k * tile_rows + m] = value[k, :padded, :LANES]
            part = value[:, :padded, LANES:]
            spilled = part if spilled is None else spilled + part
        for k in range(groups):
            spill_ref[:, k * LANES : (k + 1) * LANES] = spilled[k].astype(HALF)
        tall, wide = (rows, total), (total, cols)
        down = lax.broadcasted_iota(jnp.int32, tall, 0) + band * rows - at_ref[0:1, :]
        across = lane_index(wide) + sect * cols - at_ref[1:2, :].astype(FULL).T.astype(jnp.int32)
        down = jnp.where((down >= 0) & (down < SIDE), 1.0, 0.0)
        across = jnp.where((across >= 0) & (across < SIDE), 1.0, 0.0)
        count = jnp.dot(down.astype(HALF), across.astype(HALF), preferred_element_type=FULL)
        inverse_ref[...] = 1.0 / jnp.maximum(count, 1.0)

    return run(
        body,
        [
            like((padded, rows * SIDE)),
            like((rows, padded, cols), FULL),
            like((rows, cols), FULL),
        ],
        [anchor, *pieces, early, place],
        [pltpu.VMEM(view_shape(pieces, rows), HALF)],
        micros=1.5
    )


def finish(means, summed, arrived, inverse, channels):
    rows, padded, cols = summed.shape
    deep = -(-padded // 16) * 16
    half = means[0].shape[0]
    chunk = 8

    def body(top_ref, low_ref, sum_ref, spill_ref, inverse_ref, out_ref, flat, ready, sems):
        lane = lane_index((padded, LANES))
        none = jnp.zeros((padded, LANES), HALF)
        flat[:, padded:] = jnp.zeros((chunk, deep - padded, cols), HALF)
        copies = []
        for first in range(0, rows, chunk):
            for r in range(first, first + chunk):
                at, low = divmod(r * SIDE, LANES)
                extra = spill_ref[:, at * LANES : (at + 1) * LANES]
                if low:
                    extra = pltpu.roll(extra, LANES - low, 1)
                extra = jnp.where(lane < SIDE, extra, none).astype(FULL)
                mean = top_ref[r] if r < half else low_ref[r - half]
                value = mean.astype(FULL) + (sum_ref[r] + extra) * inverse_ref[r : r + 1]
                flat[r - first, :padded] = value.astype(HALF)
            k = first // chunk
            ready[k] = jnp.swapaxes(flat[...], 0, 1)[:channels]
            copies.append(
                pltpu.make_async_copy(
                    ready.at[k], out_ref.at[:, pl.ds(first, chunk), :], sems.at[k]
                )
            )
            copies[-1].start()
        for copy in copies:
            copy.wait()

    return run(
        body,
        [like((channels, rows, cols))],
        [*means, summed, arrived, inverse],
        [
            pltpu.VMEM((chunk, deep, cols), HALF),
            pltpu.VMEM((rows // chunk, channels, chunk, cols), HALF),
            pltpu.SemaphoreType.DMA((rows // chunk,)),
        ],
        micros=2.0,
        out_space=pltpu.HBM,
    )[0]


def step(
    state_field,
    conv_in_weight,
    conv_in_bias,
    conv_out_weight,
    conv_out_bias,
    patch_anchor,
    patch_noise,
    denoise_in_weight,
    step_bias,
    denoise_out_weight,
    denoise_bias,
):
    bands = lax.axis_size("band")
    sects = lax.axis_size("sect")
    channels, rows, cols = state_field.shape
    limits = (rows * bands, cols * sects)

    anchor = patch_anchor.T

    right_rim, left_rim, turned = pack(state_field)
    right = shift_from(right_rim, "sect", -1)
    left = shift_from(left_rim, "sect", 1)

    made, lines, noise, place = prep(
        anchor,
        [
            conv_in_weight.transpose(0, 2, 1),
            conv_out_weight,
            denoise_in_weight.transpose(0, 2, 1),
            denoise_out_weight,
        ],
        [conv_in_bias[None, :], conv_out_bias[None, :], denoise_bias[None, :], step_bias],
        patch_noise[0],
        bands,
        sects,
        rows,
        cols,
    )
    biases, step_lines = lines[:3], lines[3]

    padded = right_rim.shape[0]
    pick = picks(anchor, bands, sects, rows, cols)
    parts = extract_own(anchor, turned, pick, padded, bands, sects)
    own, kept, own_sent, sent, edge_near, edge_cross = extract_rim(
        anchor, parts, turned, right, left, pick, bands, sects
    )
    addends = [own]
    if bands > 2:
        got = swap(sent, "band", 1)
        kept = add_parts(kept, got)
    bit = 2
    while bit < bands:
        got = swap(kept[0::2], "band", bit)
        addends.append(got)
        kept = kept[1::2] + got[1:]
        bit *= 2
    addends.append(swap(own_sent, "band", 1))
    rim_near = swap(edge_near, "band", 1)
    steps = [(i, i + 1) for i in range(1, bands - 1, 2)]
    rim_cross = lax.ppermute(edge_cross, "band", steps + [(j, i) for i, j in steps])
    correction = patch_step(
        anchor, addends, noise, made, biases, step_lines, sects, limits
    )
    pieces = [correction]
    sources = arrival(bands)
    bit = bands // 2
    while bit:
        fresh = []
        for piece in pieces:
            fresh.append(swap(piece, "band", bit))
        pieces += fresh
        bit //= 2

    shifted = spread(turned, right, left)
    top_mean = grid_mean(shifted, rim_near, rim_cross, False, padded, made[:2], biases[:2], limits)
    low_mean = grid_mean(shifted, rim_near, rim_cross, True, padded, made[:2], biases[:2], limits)
    early = gather_view(anchor, pieces[:-1], sources[:-1], sects, rows, cols)
    spilled, summed, inverse = canvas(
        anchor, early, pieces[-1:], sources[-1:], place, sects, rows, cols
    )
    arrived = shift_from(spilled, "sect", 1)
    return finish([top_mean, low_mean], summed, arrived, inverse, channels)


def solution(mesh):
    placed = (
        P("groups", "band", "sect"),
        P(),
        P(),
        P(),
        P(),
        P("groups", None),
        P(("groups", "band", "sect"), None, None, None),
        P(),
        P(),
        P(),
        P(),
    )
    return jax.shard_map(
        step,
        mesh=mesh,
        in_specs=placed,
        out_specs=P("groups", "band", "sect"),
        check_vma=False,
    )
```

```python
import jax
import jax.numpy as jnp
from jax import lax
from jax.experimental import pallas as pl
from jax.experimental.pallas import tpu as pltpu
from jax.sharding import PartitionSpec as P


SIDE = 32
WIDE = SIDE + 4
LANES = 128
PER_PAIR = 2 * LANES // WIDE
TILES = -(-(WIDE // PER_PAIR * 2 * LANES + WIDE % PER_PAIR * WIDE) // LANES)
REACH = SIDE + 2
CHUNKS = 1
HALF = jnp.bfloat16
FULL = jnp.float32


def shift_from(block, axis, distance):
    count = lax.axis_size(axis)
    route = [(i - distance, i) for i in range(count) if 0 <= i - distance < count]
    return lax.ppermute(block, axis, route)


def swap(block, axis, bit):
    count = lax.axis_size(axis)
    return lax.ppermute(block, axis, [(i, i ^ bit) for i in range(count)])


def run(body, outs, ins, scratch, micros=1.0, limit=16, out_space=pltpu.VMEM):
    return pl.pallas_call(
        body,
        out_shape=outs,
        in_specs=[pl.BlockSpec(memory_space=pltpu.VMEM)] * len(ins),
        out_specs=[pl.BlockSpec(memory_space=out_space)] * len(outs),
        scratch_shapes=scratch,
        cost_estimate=pl.CostEstimate(
            flops=int(micros * 1.15e9), bytes_accessed=1024, transcendentals=0
        ),
        compiler_params=pltpu.CompilerParams(vmem_limit_bytes=limit * 1024 * 1024),
    )(*ins)


def arrival(bands):
    slots, bit = [0], bands // 2
    while bit:
        slots += [slot ^ bit for slot in slots]
        bit //= 2
    return slots


def here():
    return lax.axis_index("band"), lax.axis_index("sect")


def slots_at(at_ref, readers, sects, rows, cols):
    band, sect = here()
    count = at_ref.shape[1]
    bits = (cols * sects - 1).bit_length()
    both = jnp.left_shift(at_ref[0:1, :], bits) + at_ref[1:2, :]
    lane = lane_index((1, count))
    found = []
    for reader in readers:
        mine = lane == reader * sects + sect
        code = jnp.sum(jnp.where(mine, both, 0).astype(FULL)).astype(jnp.int32)
        row, col = jnp.right_shift(code, bits), jnp.bitwise_and(code, (1 << bits) - 1)
        found.append((row - band * rows, col - sect * cols))
    return found


def slot_anchors(at_ref, slots, sects, rows, cols):
    band, _ = here()
    return slots_at(at_ref, [jnp.bitwise_xor(band, j) for j in slots], sects, rows, cols)


def like(shape, dtype=HALF):
    return jax.ShapeDtypeStruct(shape, dtype)


def lane_index(shape):
    return lax.broadcasted_iota(jnp.int32, shape, len(shape) - 1)


def turn_rows(state_ref, flat):
    channels = state_ref.shape[0]
    flat[:channels] = state_ref[...]
    flat[channels:] = jnp.zeros((flat.shape[0] - channels,) + flat.shape[1:], HALF)
    return jnp.swapaxes(flat[...], 0, 1)


def pack(state):
    channels, rows, cols = state.shape
    padded = -(-channels // 8) * 8
    deep = -(-padded // 16) * 16
    span = -(-rows * REACH // LANES)

    def body(state_ref, right_ref, left_ref, rows_ref, flat):
        turned = turn_rows(state_ref, flat)
        rows_ref[...] = turned
        lane = lane_index((deep, LANES))
        tiles = [None] * span
        rim = jnp.zeros((deep, LANES), HALF)
        for r in range(rows):
            row = turned[r]
            at, off = divmod(r * REACH, LANES)
            moved = row if off == 0 else pltpu.roll(row, off, 1)
            if tiles[at] is None:
                tiles[at] = moved
            else:
                tiles[at] = jnp.where(lane >= off, moved, tiles[at])
            if off + REACH > LANES:
                tiles[at + 1] = moved
            moved = pltpu.roll(row, (2 * r + 2) % LANES, 1)
            rim = jnp.where((lane >= 2 * r) & (lane < 2 * r + 2), moved, rim)
        for at in range(span):
            right_ref[:, at * LANES : (at + 1) * LANES] = tiles[at][:padded]
        left_ref[...] = rim[:padded]

    return run(
        body,
        [like((padded, span * LANES)), like((padded, LANES)), like((rows, deep, cols))],
        [state],
        [pltpu.VMEM((deep, rows, cols), HALF)],
        micros=1.0,
    )


def prep(anchor, weights, biases, noise, bands, sects, rows, cols):
    steps, channels, cells = noise.shape
    count = len(weights)
    tile_rows = LANES // SIDE
    lines = len(biases)

    def body(at_ref, *refs):
        ins, lines_in, noise_ref = refs[:count], refs[count : count + lines], refs[count + lines]
        outs = refs[count + lines + 1 :]
        lines_out, noise_out = outs[count : count + lines], outs[count + lines]
        place_ref = outs[count + lines + 1]
        for k, (w_ref, o_ref) in enumerate(zip(ins, outs)):
            _, down, across = w_ref.shape
            o_ref[...] = jnp.zeros(o_ref.shape, HALF)
            for v in range(2):
                for a in range(3):
                    for b in range(3):
                        tap = (3 * (a + v) + b) * LANES
                        row, col = (v * LANES, tap) if k % 2 else (tap, v * LANES)
                        o_ref[row : row + down, col : col + across] = w_ref[3 * a + b]
        for line_ref, o_ref in zip(lines_in, lines_out):
            used = line_ref.shape[1]
            o_ref[...] = jnp.zeros(o_ref.shape, FULL)
            o_ref[:, :used] = line_ref[...]
            o_ref[:, LANES : LANES + used] = line_ref[...]
        for k in range(steps):
            for t in range(cells // LANES):
                block = noise_ref[k, :, t * LANES : (t + 1) * LANES].astype(FULL)
                block = jnp.concatenate(
                    [block, jnp.zeros((LANES - channels, LANES), FULL)], axis=0
                ).T.astype(HALF)
                for m in range(tile_rows):
                    r = t * tile_rows + m
                    noise_out[
                        k, r // 2 * SIDE : (r // 2 + 1) * SIDE, r % 2 * LANES : (r % 2 + 1) * LANES
                    ] = block[m * SIDE : (m + 1) * SIDE]
        cell = lax.broadcasted_iota(jnp.int32, (LANES, 2 * LANES), 0)
        target = lane_index((LANES, 2 * LANES))
        anchors = slot_anchors(at_ref, arrival(bands), sects, rows, cols)
        for j, (row0, col0) in enumerate(anchors):
            across = jnp.bitwise_and(cell, SIDE - 1) + col0
            for m in range(tile_rows):
                turn = jnp.bitwise_and(m - row0, tile_rows - 1)
                there = jnp.where(across < cols, across, across - cols + LANES + m * SIDE)
                hit = (target == there) & (cell >= turn * SIDE) & (cell < (turn + 1) * SIDE)
                place_ref[m, j * LANES : (j + 1) * LANES] = jnp.where(hit, 1.0, 0.0).astype(HALF)

    sizes = [(12 * LANES, 2 * LANES), (2 * LANES, 12 * LANES)]
    made = [like(sizes[k % 2]) for k in range(count)]
    made += [like((line.shape[0], 2 * LANES), FULL) for line in biases]
    made += [like((steps, cells // 2, 2 * LANES))]
    made += [like((tile_rows, bands * LANES, 2 * LANES))]
    out = run(body, made, [anchor, *weights, *biases, noise], [], micros=1.5)
    return out[:count], out[count : count + lines], *out[count + lines :]


def picks(anchor, bands, sects, rows, cols):
    width = cols + LANES

    def body(at_ref, pick_ref):
        source = lax.broadcasted_iota(jnp.int32, (width, LANES), 0)
        lane = lane_index((width, LANES))
        inners = []
        for half in range(2):
            inner = lane + half * LANES
            for _ in range(PER_PAIR):
                inner = jnp.where(inner >= WIDE, inner - WIDE, inner)
            inners.append(inner)
        anchors = slot_anchors(at_ref, range(bands), sects, rows, cols)
        for j, (row0, col0) in enumerate(anchors):
            for half, inner in enumerate(inners):
                want = jnp.bitwise_and(inner + (col0 - 2), width - 1)
                at = (2 * j + half) * LANES
                pick_ref[:, at : at + LANES] = jnp.where(source == want, 1.0, 0.0).astype(HALF)

    return run(body, [like((width, 2 * bands * LANES))], [anchor], [], micros=0.4)[0]


def add_parts(kept, got):
    def body(kept_ref, got_ref, out_ref):
        out_ref[...] = kept_ref[...] + got_ref[...]

    return run(body, [like(kept.shape)], [kept, got], [], micros=0.3)[0]


def window_tile(picked, t, row0, rows, padded, at):
    zone = lane_index((padded, LANES))
    total = jnp.zeros((padded, LANES), FULL)
    pair, half = divmod(t, 2)
    lanes = slice(at + half * LANES, at + (half + 1) * LANES)
    for k in range(PER_PAIR):
        i = pair * PER_PAIR + k
        low, high = k * WIDE - half * LANES, (k + 1) * WIDE - half * LANES
        if i >= WIDE or low >= LANES or high <= 0:
            continue
        r = row0 + i
        start = jnp.where((r >= 0) & (r < rows), low, 2 * LANES)
        keep = (zone >= start) & (zone < high)
        value = picked[jnp.clip(r, 0, rows - 1), :padded, lanes]
        total = jnp.where(keep, value, total)
    return total.astype(HALF)


def batches(bands):
    size = 2 if bands % 2 == 0 else bands
    return [range(first, first + size) for first in range(0, bands, size)], size


def select_rows(source, pick, picked):
    rows, deep, _ = source.shape
    chunk = rows // 2

    def select(c, carry):
        view = source[pl.ds(c * chunk, chunk)].reshape(chunk * deep, LANES)
        for at in range(0, pick.shape[1], LANES):
            picked[pl.ds(c * chunk, chunk), :, at : at + LANES] = jnp.dot(
                view, pick[:, at : at + LANES], preferred_element_type=FULL
            ).reshape(chunk, deep, LANES)
        return carry

    lax.fori_loop(0, rows // chunk, select, 0)


def extract_own(anchor, turned, pick, padded, bands, sects):
    rows, deep, cols = turned.shape
    groups, size = batches(bands)

    def body(at_ref, rows_ref, pick_ref, out_ref, picked):
        anchors = slot_anchors(at_ref, range(bands), sects, rows, cols)
        for group in groups:
            select_rows(
                rows_ref, pick_ref[:cols, 2 * group[0] * LANES : 2 * (group[-1] + 1) * LANES], picked
            )
            for j in group:
                row0 = anchors[j][0] - 2
                inside = (row0 > -WIDE) & (row0 < rows)

                @pl.when(inside)
                def _(j=j, row0=row0, at=2 * (j - group[0]) * LANES):
                    for t in range(TILES):
                        out_ref[j, :, t * LANES : (t + 1) * LANES] = window_tile(
                            picked, t, row0, rows, padded, at
                        )

                @pl.when(jnp.logical_not(inside))
                def _(j=j):
                    out_ref[j] = jnp.zeros((padded, TILES * LANES), HALF)

    return run(
        body,
        [like((bands, padded, TILES * LANES))],
        [anchor, turned, pick],
        [pltpu.VMEM((rows, deep, 2 * size * LANES), FULL)],
        micros=1.5
    )[0]


def extract_rim(anchor, parts, turned, right, left, pick, bands, sects):
    rows, deep, cols = turned.shape
    padded = right.shape[0]

    def body(at_ref, part_ref, rows_ref, right_ref, left_ref, pick_ref,
             own_ref, low_ref, odd_ref, high_ref, near_ref, cross_ref, ext, picked):
        lane = lane_index((padded, LANES))
        none = jnp.zeros((padded, LANES), HALF)
        rim = left_ref[...]

        def expand(r):
            at, off = divmod(r * REACH, LANES)
            piece = right_ref[:, at * LANES : (at + 1) * LANES]
            if off:
                piece = pltpu.roll(piece, LANES - off, 1)
            if off + REACH > LANES:
                after = right_ref[:, (at + 1) * LANES : (at + 2) * LANES]
                piece = jnp.where(lane < LANES - off, piece, pltpu.roll(after, LANES - off, 1))
            turn = pltpu.roll(rim, (LANES - 2 - 2 * r) % LANES, 1)
            ext[r, :padded] = jnp.where(
                lane < REACH, piece, jnp.where(lane >= LANES - 2, turn, none)
            )

        ext[:, padded:] = jnp.zeros((rows, deep - padded, LANES), HALF)
        outer = (0, 1, rows - 2, rows - 1)
        for r in outer:
            expand(r)
        even = jnp.bitwise_and(here()[0], 1) == 0
        for k in range(2):
            top, low = k, rows - 2 + k
            near_ref[k, :, :cols] = jnp.where(even, rows_ref[low], rows_ref[top])
            near_ref[k, :, cols:] = jnp.where(even, ext[low], ext[top])
            cross_ref[k, :, :cols] = jnp.where(even, rows_ref[top], rows_ref[low])
            cross_ref[k, :, cols:] = jnp.where(even, ext[top], ext[low])

        def target(j):
            if j < 2:
                return (own_ref, odd_ref)[j], 0
            return (low_ref, high_ref)[j % 2], j // 2 - 1

        crossing = []
        anchors = slot_anchors(at_ref, range(bands), sects, rows, cols)
        for j, (row0, col0) in enumerate(anchors):
            row0 = row0 - 2
            inside = (row0 > -WIDE) & (row0 < rows)
            over = inside & ((col0 < 2) | (col0 > cols - REACH))
            crossing.append((row0, over))
            out_ref, at = target(j)
            out_ref[at] = part_ref[j]
        some = crossing[0][1]
        for _, over in crossing[1:]:
            some = some | over

        @pl.when(some)
        def _():
            for r in range(rows):
                if r not in outer:
                    expand(r)

        for j in range(bands):
            out_ref, at = target(j)
            row0, over = crossing[j]

            @pl.when(over)
            def _(j=j, out_ref=out_ref, at=at, row0=row0):
                select_rows(ext, pick_ref[cols:, 2 * j * LANES : 2 * (j + 1) * LANES], picked)
                for t in range(TILES):
                    out_ref[at, :, t * LANES : (t + 1) * LANES] += window_tile(
                        picked, t, row0, rows, padded, 0
                    )

    one = like((1, padded, TILES * LANES))
    rest = like((max(bands // 2 - 1, 1), padded, TILES * LANES))
    edge = like((2, deep, cols + LANES))
    return run(
        body,
        [one, rest, one, rest, edge, edge],
        [anchor, parts, turned, right, left, pick],
        [pltpu.VMEM((rows, deep, LANES), HALF), pltpu.VMEM((rows, deep, 2 * LANES), FULL)],
        micros=1.5
    )


def product(view, weight):
    turned = weight.shape[0] == 2 * LANES
    return lax.dot_general(
        view, weight, (((1,), (1 if turned else 0,)), ((), ())), preferred_element_type=FULL
    )


def gather_pairs(shifted, first, count):
    view = jnp.concatenate(
        [shifted[b, pl.ds(first + u, count), v] for u in (0, 1) for v in (0, 1) for b in (0, 1, 2)],
        axis=-1,
    )
    return view.reshape(count * view.shape[1], view.shape[2])


def silu(value):
    return value / (1.0 + jnp.exp(-value))


def patch_step(anchor, addends, noise, weights, biases, step_bias, sects, limits):
    padded = addends[0].shape[1]
    steps = noise.shape[0]
    half = SIDE // 2
    loose = 48

    def body(*refs):
        at_ref, parts = refs[0], refs[1 : 1 + len(addends)]
        band, sect = here()
        mine = lane_index(at_ref.shape) == band * sects + sect
        at = jnp.sum(jnp.where(mine, at_ref[...], 0).astype(FULL), axis=1, keepdims=True)
        row0, col0 = at.astype(jnp.int32)[0:1][None], at.astype(jnp.int32)[1:2][None]
        (noise_ref, w_in, w_out, d_in, d_out, b_in, b_out, b_step, b_den, out_ref,
         flat, state_sh, hid, hid_sh, pad, pad_sh, corr, state) = refs[1 + len(addends) :]
        for t in range(TILES):
            lanes = slice(t * LANES, (t + 1) * LANES)
            tile = parts[0][0, :, lanes].astype(FULL)
            for part in parts[1:]:
                tile = tile + part[0, :, lanes].astype(FULL)
            tile = jnp.concatenate([tile, jnp.zeros((LANES - padded, LANES), FULL)], axis=0)
            flat[lanes, :] = tile.T
        for i in range(WIDE):
            pair, k = divmod(i, PER_PAIR)
            off = pair * 2 * LANES + k * WIDE
            for b in range(3):
                state_sh[b, i // 2, i % 2] = flat[off + b : off + b + loose, :].astype(HALF)
        pairs = half + 1
        value = product(gather_pairs(state_sh, 0, pairs), w_in[...])
        value = silu(value + b_in[...]).reshape(pairs, loose, 2 * LANES)
        pair = lax.broadcasted_iota(jnp.int32, value.shape, 0)
        col = lax.broadcasted_iota(jnp.int32, value.shape, 1)
        odd = (lane_index(value.shape) >= LANES).astype(jnp.int32)
        grid_row = row0 - 1 + 2 * pair + odd
        grid_col = col0 - 1 + col
        keep = (
            (grid_row >= 0) & (grid_row < limits[0])
            & (grid_col >= 0) & (grid_col < limits[1]) & (col < SIDE + 2)
        )
        value = jnp.where(keep, value, 0.0)
        hid[:, 0] = value[:, :, :LANES]
        hid[:, 1] = value[:, :, LANES:]
        for b in range(3):
            hid_sh[b] = hid[:, :, b : b + SIDE, :].astype(HALF)
        value = product(gather_pairs(hid_sh, 0, half), w_out[...])
        center = jnp.concatenate(
            [state_sh[2, 1 : 1 + half, v, :SIDE, :] for v in (0, 1)], axis=-1
        ).astype(FULL).reshape(half * SIDE, 2 * LANES)
        mean = (center + value + b_out[...]).astype(HALF).astype(FULL)
        state[...] = mean + noise_ref[0].astype(FULL)
        pad[...] = jnp.zeros(pad.shape, FULL)
        deal = half // CHUNKS
        trips = jnp.where(band >= 0, CHUNKS, 0)

        def fill(source, first, count):
            shaped = source.reshape(count, SIDE, 2 * LANES)
            pad[pl.ds(first, count), 1, 8 : 8 + SIDE] = shaped[:, :, :LANES]
            pad[pl.ds(first + 1, count), 0, 8 : 8 + SIDE] = shaped[:, :, LANES:]

        def shift():
            for b in range(3):
                pad_sh[b] = pad[:, :, 7 + b : 7 + b + SIDE, :].astype(HALF)

        for step in range(steps):
            fill(state[...], 0, half)
            shift()

            def first(c, carry, step=step):
                value = product(gather_pairs(pad_sh, c * deal, deal), d_in[...])
                fill(silu(value + b_step[step : step + 1]), c * deal, deal)
                return carry

            lax.fori_loop(0, trips, first, 0)
            shift()

            def second(c, carry, step=step):
                value = product(gather_pairs(pad_sh, c * deal, deal), d_out[...])
                cells = pl.ds(pl.multiple_of(c * deal * SIDE, deal * SIDE), deal * SIDE)
                value = state[cells] - 0.5 * (value + b_den[...])
                if step + 1 < steps:
                    value = value + 0.5 * noise_ref[step + 1, cells].astype(FULL)
                state[cells] = value
                return carry

            lax.fori_loop(0, trips, second, 0)
        change = (state[...] - mean).reshape(half, SIDE, 2 * LANES)
        corr[:, 0] = change[:, :, :LANES]
        corr[:, 1] = change[:, :, LANES:]
        cells = corr[...].reshape(SIDE * SIDE, LANES)
        for t in range(SIDE * SIDE // LANES):
            lanes = slice(t * LANES, (t + 1) * LANES)
            out_ref[:, lanes] = cells[lanes].T[:padded].astype(HALF)

    return run(
        body,
        [like((padded, SIDE * SIDE))],
        [anchor, *addends, noise, *weights, *biases[:2], step_bias, biases[2]],
        [
            pltpu.VMEM((TILES * LANES, LANES), FULL),
            pltpu.VMEM((3, WIDE // 2, 2, loose, LANES), HALF),
            pltpu.VMEM((half + 1, 2, loose, LANES), FULL),
            pltpu.VMEM((3, half + 1, 2, SIDE, LANES), HALF),
            pltpu.VMEM((half + 1, 2, loose, LANES), FULL),
            pltpu.VMEM((3, half + 1, 2, SIDE, LANES), HALF),
            pltpu.VMEM((half, 2, SIDE, LANES), FULL),
            pltpu.VMEM((half * SIDE, 2 * LANES), FULL),
        ],
        micros=8.0
    )[0]


def spread(turned, right, left):
    rows, _, cols = turned.shape
    span = right.shape[1]
    loose = cols + 16

    def body(rows_ref, right_ref, left_ref, out_ref, after, before, line):
        def upright(value):
            value = value.astype(FULL)
            return jnp.concatenate(
                [value, jnp.zeros((LANES - value.shape[0], value.shape[1]), FULL)], axis=0
            ).T

        for t in range(span // LANES):
            lanes = slice(t * LANES, (t + 1) * LANES)
            after[lanes] = upright(right_ref[:, lanes])
        before[...] = upright(left_ref[...])
        line[...] = jnp.zeros(line.shape, FULL)

        def spread_rows(i, carry):
            for v in range(2):
                r = 2 * i + v
                line[v, 8 : 8 + cols] = upright(rows_ref[r])
                line[v, 8 + cols : 10 + cols] = after[pl.ds(r * REACH, 2)]
                line[v, 6:8] = before[pl.ds(2 * r, 2)]
                for b in range(3):
                    out_ref[b, i, v] = line[v, 6 + b : 6 + b + loose, :].astype(HALF)
            return carry

        lax.fori_loop(0, rows // 2, spread_rows, 0)

    return run(
        body,
        [like((3, rows // 2, 2, loose, LANES))],
        [turned, right, left],
        [
            pltpu.VMEM((span, LANES), FULL),
            pltpu.VMEM((LANES, LANES), FULL),
            pltpu.VMEM((2, loose + 8, LANES), FULL),
        ],
        micros=2.5
    )[0]


def grid_mean(shifted, near, cross, lower, padded, weights, biases, limits):
    rows = 2 * shifted.shape[1]
    _, deep, width = near.shape
    cols = width - LANES
    loose = cols + 16
    made = rows // 2
    pairs_in, pairs_out = made // 4 + 1, made // 4
    hidden_pairs = made // 2 + 1
    if hidden_pairs % pairs_in:
        hidden_pairs += pairs_in - hidden_pairs % pairs_in
    state_pairs = hidden_pairs + 1
    base = rows - made - 2 if lower else -2

    def body(shifted_ref, near_ref, cross_ref, w_in, w_out, b_in, b_out, out_ref,
             line, state_sh, hid, hid_sh):
        band, sect = here()
        row0 = band * rows + base + 1
        col0 = sect * cols - 1

        for pair in range(made // 2 + 2, state_pairs):
            for b in range(3):
                state_sh[b, pair] = jnp.zeros((2, loose, LANES), HALF)
        edge = made // 2 + 1 if lower else 0
        skip = 0 if lower else 1
        given = made // 2 + 1
        at = (rows - made) // 2 - 1 if lower else 0
        for b in range(3):
            state_sh[b, skip : skip + given] = shifted_ref[b, at : at + given]
        pair = jnp.bitwise_and(band, 1) == (0 if lower else 1)
        beyond = band == (limits[0] // rows - 1 if lower else 0)
        none = jnp.zeros((deep, width), HALF)
        for v in range(2):
            rim = jnp.where(beyond, none, jnp.where(pair, near_ref[v], cross_ref[v]))
            value = jnp.concatenate(
                [rim.astype(FULL), jnp.zeros((LANES - deep, width), FULL)], axis=0
            ).T
            line[v, 8 : 8 + cols] = value[:cols]
            line[v, 8 + cols :] = value[cols : cols + 16]
            line[v, :8] = value[width - 8 :]
            for b in range(3):
                state_sh[b, edge, v] = line[v, 6 + b : 6 + b + loose, :].astype(HALF)

        def first(chunk, carry):
            start = chunk * pairs_in
            value = product(gather_pairs(state_sh, start, pairs_in), w_in[...])
            value = silu(value + b_in[...]).reshape(pairs_in, loose, 2 * LANES)
            pair = lax.broadcasted_iota(jnp.int32, value.shape, 0)
            col = lax.broadcasted_iota(jnp.int32, value.shape, 1)
            odd = (lane_index(value.shape) >= LANES).astype(jnp.int32)
            grid_row = row0 + 2 * (start + pair) + odd
            grid_col = col0 + col
            keep = (
                (grid_row >= 0) & (grid_row < limits[0])
                & (grid_col >= 0) & (grid_col < limits[1])
            )
            value = jnp.where(keep, value, 0.0)
            hid[:, 0] = value[:, :, :LANES]
            hid[:, 1] = value[:, :, LANES:]
            for b in range(3):
                hid_sh[b, pl.ds(start, pairs_in)] = hid[:, :, b : b + cols, :].astype(HALF)
            return carry

        lax.fori_loop(0, hidden_pairs // pairs_in, first, 0)

        def second(chunk, carry):
            start = chunk * pairs_out
            value = product(gather_pairs(hid_sh, start, pairs_out), w_out[...]) + b_out[...]
            value = value.reshape(pairs_out, cols, 2 * LANES)
            for k in range(pairs_out):
                for v in range(2):
                    center = state_sh[2, start + k + 1, v, :cols, :].astype(FULL)
                    mean = center + value[k, :, v * LANES : (v + 1) * LANES]
                    out_ref[2 * (start + k) + v] = mean.T[:padded].astype(HALF)
            return carry

        lax.fori_loop(0, made // 2 // pairs_out, second, 0)

    return run(
        body,
        [like((made, padded, cols))],
        [shifted, near, cross, *weights, *biases],
        [
            pltpu.VMEM((2, loose + 8, LANES), FULL),
            pltpu.VMEM((3, state_pairs, 2, loose, LANES), HALF),
            pltpu.VMEM((pairs_in, 2, loose, LANES), FULL),
            pltpu.VMEM((3, hidden_pairs, 2, cols, LANES), HALF),
        ],
        micros=3.5,
    )[0]


def fill_view(view, at_ref, pieces, sources, sects, rows, cols):
    padded = pieces[0].shape[-2]
    tile_rows = view.shape[0]
    none = jnp.zeros((padded, LANES), HALF)
    anchors = slot_anchors(at_ref, sources, sects, rows, cols)
    for at, (piece, (row0, _)) in enumerate(zip(pieces, anchors)):
        lanes = slice(at * LANES, (at + 1) * LANES)
        for r in range(rows):
            i = r - row0
            tile = jnp.clip(
                jnp.right_shift(i, tile_rows.bit_length() - 1), 0, SIDE // tile_rows - 1
            )
            value = piece[:, pl.ds(pl.multiple_of(tile * LANES, LANES), LANES)]
            inside = (i >= 0) & (i < SIDE)
            view[r % tile_rows, r // tile_rows, :padded, lanes] = jnp.where(inside, value, none)
    view[:, :, padded:, :] = jnp.zeros(
        view.shape[:2] + (view.shape[2] - padded, view.shape[3]), HALF
    )


def view_shape(pieces, rows):
    tile_rows = LANES // SIDE
    deep = -(-pieces[0].shape[-2] // 16) * 16
    return (tile_rows, rows // tile_rows, deep, len(pieces) * LANES)


def gather_view(anchor, pieces, sources, sects, rows, cols):
    def body(at_ref, *refs):
        fill_view(refs[-1], at_ref, refs[:-1], sources, sects, rows, cols)

    shape = view_shape(pieces, rows)
    return run(body, [like(shape)], [anchor, *pieces], [], micros=0.8)[0]


def canvas(anchor, early, pieces, sources, place, sects, rows, cols):
    padded = pieces[0].shape[-2]
    deep = -(-padded // 16) * 16
    total = anchor.shape[1]
    slots = len(pieces)
    tile_rows = LANES // SIDE
    groups = rows // tile_rows

    def body(at_ref, *refs):
        band, sect = here()
        early_ref, place_ref, spill_ref, out_ref, inverse_ref, view = refs[slots:]
        fill_view(view, at_ref, refs[:slots], sources, sects, rows, cols)
        spilled = None
        for m in range(tile_rows):
            both = jnp.concatenate([early_ref[m], view[m]], axis=-1)
            value = jnp.dot(
                both.reshape(groups * deep, both.shape[-1]), place_ref[m],
                preferred_element_type=FULL,
            ).reshape(groups, deep, 2 * LANES)
            for k in range(groups):
                out_ref[k * tile_rows + m] = value[k, :padded, :LANES]
            part = value[:, :padded, LANES:]
            spilled = part if spilled is None else spilled + part
        for k in range(groups):
            spill_ref[:, k * LANES : (k + 1) * LANES] = spilled[k].astype(HALF)
        tall, wide = (rows, total), (total, cols)
        down = lax.broadcasted_iota(jnp.int32, tall, 0) + band * rows - at_ref[0:1, :]
        across = lane_index(wide) + sect * cols - at_ref[1:2, :].astype(FULL).T.astype(jnp.int32)
        down = jnp.where((down >= 0) & (down < SIDE), 1.0, 0.0)
        across = jnp.where((across >= 0) & (across < SIDE), 1.0, 0.0)
        count = jnp.dot(down.astype(HALF), across.astype(HALF), preferred_element_type=FULL)
        inverse_ref[...] = 1.0 / jnp.maximum(count, 1.0)

    return run(
        body,
        [
            like((padded, rows * SIDE)),
            like((rows, padded, cols), FULL),
            like((rows, cols), FULL),
        ],
        [anchor, *pieces, early, place],
        [pltpu.VMEM(view_shape(pieces, rows), HALF)],
        micros=1.5
    )


def finish(means, summed, arrived, inverse, channels):
    rows, padded, cols = summed.shape
    deep = -(-padded // 16) * 16
    half = means[0].shape[0]
    chunk = 8

    def body(top_ref, low_ref, sum_ref, spill_ref, inverse_ref, out_ref, flat, ready, sems):
        lane = lane_index((padded, LANES))
        none = jnp.zeros((padded, LANES), HALF)
        flat[:, padded:] = jnp.zeros((chunk, deep - padded, cols), HALF)
        copies = []
        for first in range(0, rows, chunk):
            for r in range(first, first + chunk):
                at, low = divmod(r * SIDE, LANES)
                extra = spill_ref[:, at * LANES : (at + 1) * LANES]
                if low:
                    extra = pltpu.roll(extra, LANES - low, 1)
                extra = jnp.where(lane < SIDE, extra, none).astype(FULL)
                mean = top_ref[r] if r < half else low_ref[r - half]
                value = mean.astype(FULL) + (sum_ref[r] + extra) * inverse_ref[r : r + 1]
                flat[r - first, :padded] = value.astype(HALF)
            k = first // chunk
            ready[k] = jnp.swapaxes(flat[...], 0, 1)[:channels]
            copies.append(
                pltpu.make_async_copy(
                    ready.at[k], out_ref.at[:, pl.ds(first, chunk), :], sems.at[k]
                )
            )
            copies[-1].start()
        for copy in copies:
            copy.wait()

    return run(
        body,
        [like((channels, rows, cols))],
        [*means, summed, arrived, inverse],
        [
            pltpu.VMEM((chunk, deep, cols), HALF),
            pltpu.VMEM((rows // chunk, channels, chunk, cols), HALF),
            pltpu.SemaphoreType.DMA((rows // chunk,)),
        ],
        micros=2.0,
        out_space=pltpu.HBM,
    )[0]


def step(
    state_field,
    conv_in_weight,
    conv_in_bias,
    conv_out_weight,
    conv_out_bias,
    patch_anchor,
    patch_noise,
    denoise_in_weight,
    step_bias,
    denoise_out_weight,
    denoise_bias,
):
    bands = lax.axis_size("band")
    sects = lax.axis_size("sect")
    channels, rows, cols = state_field.shape
    limits = (rows * bands, cols * sects)

    anchor = patch_anchor.T

    right_rim, left_rim, turned = pack(state_field)
    right = shift_from(right_rim, "sect", -1)
    left = shift_from(left_rim, "sect", 1)

    made, lines, noise, place = prep(
        anchor,
        [
            conv_in_weight.transpose(0, 2, 1),
            conv_out_weight,
            denoise_in_weight.transpose(0, 2, 1),
            denoise_out_weight,
        ],
        [conv_in_bias[None, :], conv_out_bias[None, :], denoise_bias[None, :], step_bias],
        patch_noise[0],
        bands,
        sects,
        rows,
        cols,
    )
    biases, step_lines = lines[:3], lines[3]

    padded = right_rim.shape[0]
    pick = picks(anchor, bands, sects, rows, cols)
    parts = extract_own(anchor, turned, pick, padded, bands, sects)
    own, kept, own_sent, sent, edge_near, edge_cross = extract_rim(
        anchor, parts, turned, right, left, pick, bands, sects
    )
    addends = [own]
    if bands > 2:
        got = swap(sent, "band", 1)
        kept = add_parts(kept, got)
    bit = 2
    while bit < bands:
        got = swap(kept[0::2], "band", bit)
        addends.append(got)
        kept = kept[1::2] + got[1:]
        bit *= 2
    addends.append(swap(own_sent, "band", 1))
    rim_near = swap(edge_near, "band", 1)
    steps = [(i, i + 1) for i in range(1, bands - 1, 2)]
    alone = [(i, i) for i in range(bands) if all(i not in step for step in steps)]
    rim_cross = lax.ppermute(edge_cross, "band", steps + [(j, i) for i, j in steps] + alone)
    correction = patch_step(
        anchor, addends, noise, made, biases, step_lines, sects, limits
    )
    pieces = [correction]
    sources = arrival(bands)
    bit = bands // 2
    while bit:
        fresh = []
        for piece in pieces:
            fresh.append(swap(piece, "band", bit))
        pieces += fresh
        bit //= 2

    shifted = spread(turned, right, left)
    top_mean = grid_mean(shifted, rim_near, rim_cross, False, padded, made[:2], biases[:2], limits)
    low_mean = grid_mean(shifted, rim_near, rim_cross, True, padded, made[:2], biases[:2], limits)
    early = gather_view(anchor, pieces[:-1], sources[:-1], sects, rows, cols)
    spilled, summed, inverse = canvas(
        anchor, early, pieces[-1:], sources[-1:], place, sects, rows, cols
    )
    arrived = shift_from(spilled, "sect", 1)
    return finish([top_mean, low_mean], summed, arrived, inverse, channels)


def solution(mesh):
    placed = (
        P("groups", "band", "sect"),
        P(),
        P(),
        P(),
        P(),
        P("groups", None),
        P(("groups", "band", "sect"), None, None, None),
        P(),
        P(),
        P(),
        P(),
    )
    return jax.shard_map(
        step,
        mesh=mesh,
        in_specs=placed,
        out_specs=P("groups", "band", "sect"),
        check_vma=False,
    )
```

```python
import jax
import jax.numpy as jnp
from jax import lax
from jax.experimental import pallas as pl
from jax.experimental.pallas import tpu as pltpu
from jax.sharding import PartitionSpec as P


SIDE = 32
WIDE = SIDE + 4
LANES = 128
PER_PAIR = 2 * LANES // WIDE
TILES = -(-(WIDE // PER_PAIR * 2 * LANES + WIDE % PER_PAIR * WIDE) // LANES)
REACH = SIDE + 2
CHUNKS = 1
HALF = jnp.bfloat16
FULL = jnp.float32


def shift_from(block, axis, distance):
    count = lax.axis_size(axis)
    route = [(i - distance, i) for i in range(count) if 0 <= i - distance < count]
    return lax.ppermute(block, axis, route)


def swap(block, axis, bit):
    count = lax.axis_size(axis)
    return lax.ppermute(block, axis, [(i, i ^ bit) for i in range(count)])


def run(body, outs, ins, scratch, micros=1.0, limit=16, out_space=pltpu.VMEM):
    return pl.pallas_call(
        body,
        out_shape=outs,
        in_specs=[pl.BlockSpec(memory_space=pltpu.VMEM)] * len(ins),
        out_specs=[pl.BlockSpec(memory_space=out_space)] * len(outs),
        scratch_shapes=scratch,
        cost_estimate=pl.CostEstimate(
            flops=int(micros * 1.15e9), bytes_accessed=1024, transcendentals=0
        ),
        compiler_params=pltpu.CompilerParams(vmem_limit_bytes=limit * 1024 * 1024),
    )(*ins)


def arrival(bands):
    slots, bit = [0], bands // 2
    while bit:
        slots += [slot ^ bit for slot in slots]
        bit //= 2
    return slots


def here():
    return lax.axis_index("band"), lax.axis_index("sect")


def slots_at(at_ref, readers, sects, rows, cols):
    band, sect = here()
    count = at_ref.shape[1]
    bits = (cols * sects - 1).bit_length()
    both = jnp.left_shift(at_ref[0:1, :], bits) + at_ref[1:2, :]
    lane = lane_index((1, count))
    found = []
    for reader in readers:
        mine = lane == reader * sects + sect
        code = jnp.sum(jnp.where(mine, both, 0).astype(FULL)).astype(jnp.int32)
        row, col = jnp.right_shift(code, bits), jnp.bitwise_and(code, (1 << bits) - 1)
        found.append((row - band * rows, col - sect * cols))
    return found


def slot_anchors(at_ref, slots, sects, rows, cols):
    band, _ = here()
    return slots_at(at_ref, [jnp.bitwise_xor(band, j) for j in slots], sects, rows, cols)


def like(shape, dtype=HALF):
    return jax.ShapeDtypeStruct(shape, dtype)


def lane_index(shape):
    return lax.broadcasted_iota(jnp.int32, shape, len(shape) - 1)


def turn_rows(state_ref, flat):
    channels = state_ref.shape[0]
    flat[:channels] = state_ref[...]
    flat[channels:] = jnp.zeros((flat.shape[0] - channels,) + flat.shape[1:], HALF)
    return jnp.swapaxes(flat[...], 0, 1)


def pack(state):
    channels, rows, cols = state.shape
    padded = -(-channels // 8) * 8
    deep = -(-padded // 16) * 16
    span = -(-rows * REACH // LANES)

    def body(state_ref, right_ref, left_ref, rows_ref, flat):
        turned = turn_rows(state_ref, flat)
        rows_ref[...] = turned
        lane = lane_index((deep, LANES))
        tiles = [None] * span
        rim = jnp.zeros((deep, LANES), HALF)
        for r in range(rows):
            row = turned[r]
            at, off = divmod(r * REACH, LANES)
            moved = row if off == 0 else pltpu.roll(row, off, 1)
            if tiles[at] is None:
                tiles[at] = moved
            else:
                tiles[at] = jnp.where(lane >= off, moved, tiles[at])
            if off + REACH > LANES:
                tiles[at + 1] = moved
            moved = pltpu.roll(row, (2 * r + 2) % LANES, 1)
            rim = jnp.where((lane >= 2 * r) & (lane < 2 * r + 2), moved, rim)
        for at in range(span):
            right_ref[:, at * LANES : (at + 1) * LANES] = tiles[at][:padded]
        left_ref[...] = rim[:padded]

    return run(
        body,
        [like((padded, span * LANES)), like((padded, LANES)), like((rows, deep, cols))],
        [state],
        [pltpu.VMEM((deep, rows, cols), HALF)],
        micros=1.0,
    )


def prep(anchor, weights, biases, noise, bands, sects, rows, cols):
    steps, channels, cells = noise.shape
    count = len(weights)
    tile_rows = LANES // SIDE
    lines = len(biases)

    def body(at_ref, *refs):
        ins, lines_in, noise_ref = refs[:count], refs[count : count + lines], refs[count + lines]
        outs = refs[count + lines + 1 :]
        lines_out, noise_out = outs[count : count + lines], outs[count + lines]
        place_ref = outs[count + lines + 1]
        for k, (w_ref, o_ref) in enumerate(zip(ins, outs)):
            _, down, across = w_ref.shape
            o_ref[...] = jnp.zeros(o_ref.shape, HALF)
            for v in range(2):
                for a in range(3):
                    for b in range(3):
                        tap = (3 * (a + v) + b) * LANES
                        row, col = (v * LANES, tap) if k % 2 else (tap, v * LANES)
                        o_ref[row : row + down, col : col + across] = w_ref[3 * a + b]
        for line_ref, o_ref in zip(lines_in, lines_out):
            used = line_ref.shape[1]
            o_ref[...] = jnp.zeros(o_ref.shape, FULL)
            o_ref[:, :used] = line_ref[...]
            o_ref[:, LANES : LANES + used] = line_ref[...]
        for k in range(steps):
            for t in range(cells // LANES):
                block = noise_ref[k, :, t * LANES : (t + 1) * LANES].astype(FULL)
                block = jnp.concatenate(
                    [block, jnp.zeros((LANES - channels, LANES), FULL)], axis=0
                ).T.astype(HALF)
                for m in range(tile_rows):
                    r = t * tile_rows + m
                    noise_out[
                        k, r // 2 * SIDE : (r // 2 + 1) * SIDE, r % 2 * LANES : (r % 2 + 1) * LANES
                    ] = block[m * SIDE : (m + 1) * SIDE]
        cell = lax.broadcasted_iota(jnp.int32, (LANES, 2 * LANES), 0)
        target = lane_index((LANES, 2 * LANES))
        anchors = slot_anchors(at_ref, arrival(bands), sects, rows, cols)
        for j, (row0, col0) in enumerate(anchors):
            across = jnp.bitwise_and(cell, SIDE - 1) + col0
            for m in range(tile_rows):
                turn = jnp.bitwise_and(m - row0, tile_rows - 1)
                there = jnp.where(across < cols, across, across - cols + LANES + m * SIDE)
                hit = (target == there) & (cell >= turn * SIDE) & (cell < (turn + 1) * SIDE)
                place_ref[m, j * LANES : (j + 1) * LANES] = jnp.where(hit, 1.0, 0.0).astype(HALF)

    sizes = [(12 * LANES, 2 * LANES), (2 * LANES, 12 * LANES)]
    made = [like(sizes[k % 2]) for k in range(count)]
    made += [like((line.shape[0], 2 * LANES), FULL) for line in biases]
    made += [like((steps, cells // 2, 2 * LANES))]
    made += [like((tile_rows, bands * LANES, 2 * LANES))]
    out = run(body, made, [anchor, *weights, *biases, noise], [], micros=1.5)
    return out[:count], out[count : count + lines], *out[count + lines :]


def add_parts(kept, got):
    def body(kept_ref, got_ref, out_ref):
        out_ref[...] = kept_ref[...] + got_ref[...]

    return run(body, [like(kept.shape)], [kept, got], [], micros=0.3)[0]


def window_tile(source, t, row0, col0, low, high, rows, padded):
    lane = lane_index((1, LANES))
    total = jnp.zeros((padded, LANES), HALF)
    pair, half = divmod(t, 2)
    for k in range(PER_PAIR):
        i = pair * PER_PAIR + k
        zone = k * WIDE - half * LANES
        if i >= WIDE or zone >= LANES or zone + WIDE <= 0:
            continue
        r = row0 + i
        first = jnp.where((r >= 0) & (r < rows), zone + low, 2 * LANES)
        keep = jnp.where((lane >= first) & (lane < zone + high), 1.0, 0.0).astype(HALF)
        turn = jnp.bitwise_and(zone + 2 - col0, LANES - 1)
        value = pltpu.roll(source[jnp.clip(r, 0, rows - 1), :padded], turn, 1)
        total = total + value * keep
    return total


def extract_own(anchor, turned, padded, bands, sects):
    rows, _, cols = turned.shape

    def body(at_ref, rows_ref, out_ref):
        anchors = slot_anchors(at_ref, range(bands), sects, rows, cols)
        for j, (row0, col0) in enumerate(anchors):
            row0 = row0 - 2
            inside = (row0 > -WIDE) & (row0 < rows)
            low, high = jnp.maximum(2 - col0, 0), jnp.minimum(cols + 2 - col0, WIDE)

            @pl.when(inside)
            def _(j=j, row0=row0, col0=col0, low=low, high=high):
                for t in range(TILES):
                    out_ref[j, :, t * LANES : (t + 1) * LANES] = window_tile(
                        rows_ref, t, row0, col0, low, high, rows, padded
                    )

            @pl.when(jnp.logical_not(inside))
            def _(j=j):
                out_ref[j] = jnp.zeros((padded, TILES * LANES), HALF)

    return run(body, [like((bands, padded, TILES * LANES))], [anchor, turned], [], micros=1.5)[0]


def extract_rim(anchor, parts, turned, right, left, bands, sects):
    rows, deep, cols = turned.shape
    padded = right.shape[0]

    def body(at_ref, part_ref, rows_ref, right_ref, left_ref,
             own_ref, low_ref, odd_ref, high_ref, near_ref, cross_ref, ext):
        lane = lane_index((padded, LANES))
        none = jnp.zeros((padded, LANES), HALF)
        rim = left_ref[...]

        def expand(r):
            at, off = divmod(r * REACH, LANES)
            piece = right_ref[:, at * LANES : (at + 1) * LANES]
            if off:
                piece = pltpu.roll(piece, LANES - off, 1)
            if off + REACH > LANES:
                after = right_ref[:, (at + 1) * LANES : (at + 2) * LANES]
                piece = jnp.where(lane < LANES - off, piece, pltpu.roll(after, LANES - off, 1))
            turn = pltpu.roll(rim, (LANES - 2 - 2 * r) % LANES, 1)
            ext[r, :padded] = jnp.where(
                lane < REACH, piece, jnp.where(lane >= LANES - 2, turn, none)
            )

        ext[:, padded:] = jnp.zeros((rows, deep - padded, LANES), HALF)
        outer = (0, 1, rows - 2, rows - 1)
        for r in outer:
            expand(r)
        even = jnp.bitwise_and(here()[0], 1) == 0
        for k in range(2):
            top, low = k, rows - 2 + k
            near_ref[k, :, :cols] = jnp.where(even, rows_ref[low], rows_ref[top])
            near_ref[k, :, cols:] = jnp.where(even, ext[low], ext[top])
            cross_ref[k, :, :cols] = jnp.where(even, rows_ref[top], rows_ref[low])
            cross_ref[k, :, cols:] = jnp.where(even, ext[top], ext[low])

        def target(j):
            if j < 2:
                return (own_ref, odd_ref)[j], 0
            return (low_ref, high_ref)[j % 2], j // 2 - 1

        crossing = []
        anchors = slot_anchors(at_ref, range(bands), sects, rows, cols)
        for j, (row0, col0) in enumerate(anchors):
            row0 = row0 - 2
            inside = (row0 > -WIDE) & (row0 < rows)
            over = inside & ((col0 < 2) | (col0 > cols - REACH))
            low = jnp.where(col0 < 2, 0, cols + 2 - col0)
            high = jnp.where(col0 < 2, 2 - col0, WIDE)
            crossing.append((over, row0, col0, low, high))
            out_ref, at = target(j)
            out_ref[at] = part_ref[j]
        some = crossing[0][0]
        for over, *_ in crossing[1:]:
            some = some | over

        @pl.when(some)
        def _():
            for r in range(rows):
                if r not in outer:
                    expand(r)

        for j, (over, *where) in enumerate(crossing):
            out_ref, at = target(j)

            @pl.when(over)
            def _(out_ref=out_ref, at=at, where=where):
                for t in range(TILES):
                    out_ref[at, :, t * LANES : (t + 1) * LANES] += window_tile(
                        ext, t, *where, rows, padded
                    )

    one = like((1, padded, TILES * LANES))
    rest = like((max(bands // 2 - 1, 1), padded, TILES * LANES))
    edge = like((2, deep, cols + LANES))
    return run(
        body,
        [one, rest, one, rest, edge, edge],
        [anchor, parts, turned, right, left],
        [pltpu.VMEM((rows, deep, LANES), HALF)],
        micros=1.5
    )


def product(view, weight):
    turned = weight.shape[0] == 2 * LANES
    return lax.dot_general(
        view, weight, (((1,), (1 if turned else 0,)), ((), ())), preferred_element_type=FULL
    )


def gather_pairs(shifted, first, count):
    view = jnp.concatenate(
        [shifted[b, pl.ds(first + u, count), v] for u in (0, 1) for v in (0, 1) for b in (0, 1, 2)],
        axis=-1,
    )
    return view.reshape(count * view.shape[1], view.shape[2])


def silu(value):
    return value / (1.0 + jnp.exp(-value))


def patch_step(anchor, addends, noise, weights, biases, step_bias, sects, limits):
    padded = addends[0].shape[1]
    steps = noise.shape[0]
    half = SIDE // 2
    loose = 48

    def body(*refs):
        at_ref, parts = refs[0], refs[1 : 1 + len(addends)]
        band, sect = here()
        mine = lane_index(at_ref.shape) == band * sects + sect
        at = jnp.sum(jnp.where(mine, at_ref[...], 0).astype(FULL), axis=1, keepdims=True)
        row0, col0 = at.astype(jnp.int32)[0:1][None], at.astype(jnp.int32)[1:2][None]
        (noise_ref, w_in, w_out, d_in, d_out, b_in, b_out, b_step, b_den, out_ref,
         flat, state_sh, hid, hid_sh, pad, pad_sh, corr, state) = refs[1 + len(addends) :]
        for t in range(TILES):
            lanes = slice(t * LANES, (t + 1) * LANES)
            tile = parts[0][0, :, lanes].astype(FULL)
            for part in parts[1:]:
                tile = tile + part[0, :, lanes].astype(FULL)
            tile = jnp.concatenate([tile, jnp.zeros((LANES - padded, LANES), FULL)], axis=0)
            flat[lanes, :] = tile.T
        for i in range(WIDE):
            pair, k = divmod(i, PER_PAIR)
            off = pair * 2 * LANES + k * WIDE
            for b in range(3):
                state_sh[b, i // 2, i % 2] = flat[off + b : off + b + loose, :].astype(HALF)
        pairs = half + 1
        value = product(gather_pairs(state_sh, 0, pairs), w_in[...])
        value = silu(value + b_in[...]).reshape(pairs, loose, 2 * LANES)
        pair = lax.broadcasted_iota(jnp.int32, value.shape, 0)
        col = lax.broadcasted_iota(jnp.int32, value.shape, 1)
        odd = (lane_index(value.shape) >= LANES).astype(jnp.int32)
        grid_row = row0 - 1 + 2 * pair + odd
        grid_col = col0 - 1 + col
        keep = (
            (grid_row >= 0) & (grid_row < limits[0])
            & (grid_col >= 0) & (grid_col < limits[1]) & (col < SIDE + 2)
        )
        value = jnp.where(keep, value, 0.0)
        hid[:, 0] = value[:, :, :LANES]
        hid[:, 1] = value[:, :, LANES:]
        for b in range(3):
            hid_sh[b] = hid[:, :, b : b + SIDE, :].astype(HALF)
        value = product(gather_pairs(hid_sh, 0, half), w_out[...])
        center = jnp.concatenate(
            [state_sh[2, 1 : 1 + half, v, :SIDE, :] for v in (0, 1)], axis=-1
        ).astype(FULL).reshape(half * SIDE, 2 * LANES)
        mean = (center + value + b_out[...]).astype(HALF).astype(FULL)
        state[...] = mean + noise_ref[0].astype(FULL)
        pad[...] = jnp.zeros(pad.shape, FULL)
        deal = half // CHUNKS
        trips = jnp.where(band >= 0, CHUNKS, 0)

        def fill(source, first, count):
            shaped = source.reshape(count, SIDE, 2 * LANES)
            pad[pl.ds(first, count), 1, 8 : 8 + SIDE] = shaped[:, :, :LANES]
            pad[pl.ds(first + 1, count), 0, 8 : 8 + SIDE] = shaped[:, :, LANES:]

        def shift():
            for b in range(3):
                pad_sh[b] = pad[:, :, 7 + b : 7 + b + SIDE, :].astype(HALF)

        for step in range(steps):
            fill(state[...], 0, half)
            shift()

            def first(c, carry, step=step):
                value = product(gather_pairs(pad_sh, c * deal, deal), d_in[...])
                fill(silu(value + b_step[step : step + 1]), c * deal, deal)
                return carry

            lax.fori_loop(0, trips, first, 0)
            shift()

            def second(c, carry, step=step):
                value = product(gather_pairs(pad_sh, c * deal, deal), d_out[...])
                cells = pl.ds(pl.multiple_of(c * deal * SIDE, deal * SIDE), deal * SIDE)
                value = state[cells] - 0.5 * (value + b_den[...])
                if step + 1 < steps:
                    value = value + 0.5 * noise_ref[step + 1, cells].astype(FULL)
                state[cells] = value
                return carry

            lax.fori_loop(0, trips, second, 0)
        change = (state[...] - mean).reshape(half, SIDE, 2 * LANES)
        corr[:, 0] = change[:, :, :LANES]
        corr[:, 1] = change[:, :, LANES:]
        cells = corr[...].reshape(SIDE * SIDE, LANES)
        for t in range(SIDE * SIDE // LANES):
            lanes = slice(t * LANES, (t + 1) * LANES)
            out_ref[:, lanes] = cells[lanes].T[:padded].astype(HALF)

    return run(
        body,
        [like((padded, SIDE * SIDE))],
        [anchor, *addends, noise, *weights, *biases[:2], step_bias, biases[2]],
        [
            pltpu.VMEM((TILES * LANES, LANES), FULL),
            pltpu.VMEM((3, WIDE // 2, 2, loose, LANES), HALF),
            pltpu.VMEM((half + 1, 2, loose, LANES), FULL),
            pltpu.VMEM((3, half + 1, 2, SIDE, LANES), HALF),
            pltpu.VMEM((half + 1, 2, loose, LANES), FULL),
            pltpu.VMEM((3, half + 1, 2, SIDE, LANES), HALF),
            pltpu.VMEM((half, 2, SIDE, LANES), FULL),
            pltpu.VMEM((half * SIDE, 2 * LANES), FULL),
        ],
        micros=8.0
    )[0]


def spread(turned, right, left):
    rows, _, cols = turned.shape
    span = right.shape[1]
    loose = cols + 16

    def body(rows_ref, right_ref, left_ref, out_ref, after, before, line):
        def upright(value):
            value = value.astype(FULL)
            return jnp.concatenate(
                [value, jnp.zeros((LANES - value.shape[0], value.shape[1]), FULL)], axis=0
            ).T

        for t in range(span // LANES):
            lanes = slice(t * LANES, (t + 1) * LANES)
            after[lanes] = upright(right_ref[:, lanes])
        before[...] = upright(left_ref[...])
        line[...] = jnp.zeros(line.shape, FULL)

        def spread_rows(i, carry):
            for v in range(2):
                r = 2 * i + v
                line[v, 8 : 8 + cols] = upright(rows_ref[r])
                line[v, 8 + cols : 10 + cols] = after[pl.ds(r * REACH, 2)]
                line[v, 6:8] = before[pl.ds(2 * r, 2)]
                for b in range(3):
                    out_ref[b, i, v] = line[v, 6 + b : 6 + b + loose, :].astype(HALF)
            return carry

        lax.fori_loop(0, rows // 2, spread_rows, 0)

    return run(
        body,
        [like((3, rows // 2, 2, loose, LANES))],
        [turned, right, left],
        [
            pltpu.VMEM((span, LANES), FULL),
            pltpu.VMEM((LANES, LANES), FULL),
            pltpu.VMEM((2, loose + 8, LANES), FULL),
        ],
        micros=2.5
    )[0]


def grid_mean(shifted, near, cross, lower, padded, weights, biases, limits):
    rows = 2 * shifted.shape[1]
    _, deep, width = near.shape
    cols = width - LANES
    loose = cols + 16
    made = rows // 2
    pairs_in, pairs_out = made // 4 + 1, made // 4
    hidden_pairs = made // 2 + 1
    if hidden_pairs % pairs_in:
        hidden_pairs += pairs_in - hidden_pairs % pairs_in
    state_pairs = hidden_pairs + 1
    base = rows - made - 2 if lower else -2

    def body(shifted_ref, near_ref, cross_ref, w_in, w_out, b_in, b_out, out_ref,
             line, state_sh, hid, hid_sh):
        band, sect = here()
        row0 = band * rows + base + 1
        col0 = sect * cols - 1

        for pair in range(made // 2 + 2, state_pairs):
            for b in range(3):
                state_sh[b, pair] = jnp.zeros((2, loose, LANES), HALF)
        edge = made // 2 + 1 if lower else 0
        skip = 0 if lower else 1
        given = made // 2 + 1
        at = (rows - made) // 2 - 1 if lower else 0
        for b in range(3):
            state_sh[b, skip : skip + given] = shifted_ref[b, at : at + given]
        pair = jnp.bitwise_and(band, 1) == (0 if lower else 1)
        beyond = band == (limits[0] // rows - 1 if lower else 0)
        none = jnp.zeros((deep, width), HALF)
        for v in range(2):
            rim = jnp.where(beyond, none, jnp.where(pair, near_ref[v], cross_ref[v]))
            value = jnp.concatenate(
                [rim.astype(FULL), jnp.zeros((LANES - deep, width), FULL)], axis=0
            ).T
            line[v, 8 : 8 + cols] = value[:cols]
            line[v, 8 + cols :] = value[cols : cols + 16]
            line[v, :8] = value[width - 8 :]
            for b in range(3):
                state_sh[b, edge, v] = line[v, 6 + b : 6 + b + loose, :].astype(HALF)

        def first(chunk, carry):
            start = chunk * pairs_in
            value = product(gather_pairs(state_sh, start, pairs_in), w_in[...])
            value = silu(value + b_in[...]).reshape(pairs_in, loose, 2 * LANES)
            pair = lax.broadcasted_iota(jnp.int32, value.shape, 0)
            col = lax.broadcasted_iota(jnp.int32, value.shape, 1)
            odd = (lane_index(value.shape) >= LANES).astype(jnp.int32)
            grid_row = row0 + 2 * (start + pair) + odd
            grid_col = col0 + col
            keep = (
                (grid_row >= 0) & (grid_row < limits[0])
                & (grid_col >= 0) & (grid_col < limits[1])
            )
            value = jnp.where(keep, value, 0.0)
            hid[:, 0] = value[:, :, :LANES]
            hid[:, 1] = value[:, :, LANES:]
            for b in range(3):
                hid_sh[b, pl.ds(start, pairs_in)] = hid[:, :, b : b + cols, :].astype(HALF)
            return carry

        lax.fori_loop(0, hidden_pairs // pairs_in, first, 0)

        def second(chunk, carry):
            start = chunk * pairs_out
            value = product(gather_pairs(hid_sh, start, pairs_out), w_out[...]) + b_out[...]
            value = value.reshape(pairs_out, cols, 2 * LANES)
            for k in range(pairs_out):
                for v in range(2):
                    center = state_sh[2, start + k + 1, v, :cols, :].astype(FULL)
                    mean = center + value[k, :, v * LANES : (v + 1) * LANES]
                    out_ref[2 * (start + k) + v] = mean.T[:padded].astype(HALF)
            return carry

        lax.fori_loop(0, made // 2 // pairs_out, second, 0)

    return run(
        body,
        [like((made, padded, cols))],
        [shifted, near, cross, *weights, *biases],
        [
            pltpu.VMEM((2, loose + 8, LANES), FULL),
            pltpu.VMEM((3, state_pairs, 2, loose, LANES), HALF),
            pltpu.VMEM((pairs_in, 2, loose, LANES), FULL),
            pltpu.VMEM((3, hidden_pairs, 2, cols, LANES), HALF),
        ],
        micros=3.5,
    )[0]


def fill_view(view, at_ref, pieces, sources, sects, rows, cols):
    padded = pieces[0].shape[-2]
    tile_rows = view.shape[0]
    none = jnp.zeros((padded, LANES), HALF)
    anchors = slot_anchors(at_ref, sources, sects, rows, cols)
    for at, (piece, (row0, _)) in enumerate(zip(pieces, anchors)):
        lanes = slice(at * LANES, (at + 1) * LANES)
        for r in range(rows):
            i = r - row0
            tile = jnp.clip(
                jnp.right_shift(i, tile_rows.bit_length() - 1), 0, SIDE // tile_rows - 1
            )
            value = piece[:, pl.ds(pl.multiple_of(tile * LANES, LANES), LANES)]
            inside = (i >= 0) & (i < SIDE)
            view[r % tile_rows, r // tile_rows, :padded, lanes] = jnp.where(inside, value, none)
    view[:, :, padded:, :] = jnp.zeros(
        view.shape[:2] + (view.shape[2] - padded, view.shape[3]), HALF
    )


def view_shape(pieces, rows):
    tile_rows = LANES // SIDE
    deep = -(-pieces[0].shape[-2] // 16) * 16
    return (tile_rows, rows // tile_rows, deep, len(pieces) * LANES)


def gather_view(anchor, pieces, sources, sects, rows, cols):
    def body(at_ref, *refs):
        fill_view(refs[-1], at_ref, refs[:-1], sources, sects, rows, cols)

    shape = view_shape(pieces, rows)
    return run(body, [like(shape)], [anchor, *pieces], [], micros=0.8)[0]


def canvas(anchor, early, pieces, sources, place, sects, rows, cols):
    padded = pieces[0].shape[-2]
    deep = -(-padded // 16) * 16
    total = anchor.shape[1]
    slots = len(pieces)
    tile_rows = LANES // SIDE
    groups = rows // tile_rows

    def body(at_ref, *refs):
        band, sect = here()
        early_ref, place_ref, spill_ref, out_ref, inverse_ref, view = refs[slots:]
        fill_view(view, at_ref, refs[:slots], sources, sects, rows, cols)
        spilled = None
        for m in range(tile_rows):
            both = jnp.concatenate([early_ref[m], view[m]], axis=-1)
            value = jnp.dot(
                both.reshape(groups * deep, both.shape[-1]), place_ref[m],
                preferred_element_type=FULL,
            ).reshape(groups, deep, 2 * LANES)
            for k in range(groups):
                out_ref[k * tile_rows + m] = value[k, :padded, :LANES]
            part = value[:, :padded, LANES:]
            spilled = part if spilled is None else spilled + part
        for k in range(groups):
            spill_ref[:, k * LANES : (k + 1) * LANES] = spilled[k].astype(HALF)
        tall, wide = (rows, total), (total, cols)
        down = lax.broadcasted_iota(jnp.int32, tall, 0) + band * rows - at_ref[0:1, :]
        across = lane_index(wide) + sect * cols - at_ref[1:2, :].astype(FULL).T.astype(jnp.int32)
        down = jnp.where((down >= 0) & (down < SIDE), 1.0, 0.0)
        across = jnp.where((across >= 0) & (across < SIDE), 1.0, 0.0)
        count = jnp.dot(down.astype(HALF), across.astype(HALF), preferred_element_type=FULL)
        inverse_ref[...] = 1.0 / jnp.maximum(count, 1.0)

    return run(
        body,
        [
            like((padded, rows * SIDE)),
            like((rows, padded, cols), FULL),
            like((rows, cols), FULL),
        ],
        [anchor, *pieces, early, place],
        [pltpu.VMEM(view_shape(pieces, rows), HALF)],
        micros=1.5
    )


def finish(means, summed, arrived, inverse, channels):
    rows, padded, cols = summed.shape
    deep = -(-padded // 16) * 16
    half = means[0].shape[0]
    chunk = 8

    def body(top_ref, low_ref, sum_ref, spill_ref, inverse_ref, out_ref, flat, ready, sems):
        lane = lane_index((padded, LANES))
        none = jnp.zeros((padded, LANES), HALF)
        flat[:, padded:] = jnp.zeros((chunk, deep - padded, cols), HALF)
        copies = []
        for first in range(0, rows, chunk):
            for r in range(first, first + chunk):
                at, low = divmod(r * SIDE, LANES)
                extra = spill_ref[:, at * LANES : (at + 1) * LANES]
                if low:
                    extra = pltpu.roll(extra, LANES - low, 1)
                extra = jnp.where(lane < SIDE, extra, none).astype(FULL)
                mean = top_ref[r] if r < half else low_ref[r - half]
                value = mean.astype(FULL) + (sum_ref[r] + extra) * inverse_ref[r : r + 1]
                flat[r - first, :padded] = value.astype(HALF)
            k = first // chunk
            ready[k] = jnp.swapaxes(flat[...], 0, 1)[:channels]
            copies.append(
                pltpu.make_async_copy(
                    ready.at[k], out_ref.at[:, pl.ds(first, chunk), :], sems.at[k]
                )
            )
            copies[-1].start()
        for copy in copies:
            copy.wait()

    return run(
        body,
        [like((channels, rows, cols))],
        [*means, summed, arrived, inverse],
        [
            pltpu.VMEM((chunk, deep, cols), HALF),
            pltpu.VMEM((rows // chunk, channels, chunk, cols), HALF),
            pltpu.SemaphoreType.DMA((rows // chunk,)),
        ],
        micros=2.0,
        out_space=pltpu.HBM,
    )[0]


def step(
    state_field,
    conv_in_weight,
    conv_in_bias,
    conv_out_weight,
    conv_out_bias,
    patch_anchor,
    patch_noise,
    denoise_in_weight,
    step_bias,
    denoise_out_weight,
    denoise_bias,
):
    bands = lax.axis_size("band")
    sects = lax.axis_size("sect")
    channels, rows, cols = state_field.shape
    limits = (rows * bands, cols * sects)

    anchor = patch_anchor.T

    right_rim, left_rim, turned = pack(state_field)
    right = shift_from(right_rim, "sect", -1)
    left = shift_from(left_rim, "sect", 1)

    made, lines, noise, place = prep(
        anchor,
        [
            conv_in_weight.transpose(0, 2, 1),
            conv_out_weight,
            denoise_in_weight.transpose(0, 2, 1),
            denoise_out_weight,
        ],
        [conv_in_bias[None, :], conv_out_bias[None, :], denoise_bias[None, :], step_bias],
        patch_noise[0],
        bands,
        sects,
        rows,
        cols,
    )
    biases, step_lines = lines[:3], lines[3]

    padded = right_rim.shape[0]
    parts = extract_own(anchor, turned, padded, bands, sects)
    own, kept, own_sent, sent, edge_near, edge_cross = extract_rim(
        anchor, parts, turned, right, left, bands, sects
    )
    addends = [own]
    if bands > 2:
        got = swap(sent, "band", 1)
        kept = add_parts(kept, got)
    bit = 2
    while bit < bands:
        got = swap(kept[0::2], "band", bit)
        addends.append(got)
        kept = kept[1::2] + got[1:]
        bit *= 2
    addends.append(swap(own_sent, "band", 1))
    rim_near = swap(edge_near, "band", 1)
    steps = [(i, i + 1) for i in range(1, bands - 1, 2)]
    alone = [(i, i) for i in range(bands) if all(i not in step for step in steps)]
    rim_cross = lax.ppermute(edge_cross, "band", steps + [(j, i) for i, j in steps] + alone)
    correction = patch_step(
        anchor, addends, noise, made, biases, step_lines, sects, limits
    )
    pieces = [correction]
    sources = arrival(bands)
    bit = bands // 2
    while bit:
        fresh = []
        for piece in pieces:
            fresh.append(swap(piece, "band", bit))
        pieces += fresh
        bit //= 2

    shifted = spread(turned, right, left)
    top_mean = grid_mean(shifted, rim_near, rim_cross, False, padded, made[:2], biases[:2], limits)
    low_mean = grid_mean(shifted, rim_near, rim_cross, True, padded, made[:2], biases[:2], limits)
    early = gather_view(anchor, pieces[:-1], sources[:-1], sects, rows, cols)
    spilled, summed, inverse = canvas(
        anchor, early, pieces[-1:], sources[-1:], place, sects, rows, cols
    )
    arrived = shift_from(spilled, "sect", 1)
    return finish([top_mean, low_mean], summed, arrived, inverse, channels)


def solution(mesh):
    placed = (
        P("groups", "band", "sect"),
        P(),
        P(),
        P(),
        P(),
        P("groups", None),
        P(("groups", "band", "sect"), None, None, None),
        P(),
        P(),
        P(),
        P(),
    )
    return jax.shard_map(
        step,
        mesh=mesh,
        in_specs=placed,
        out_specs=P("groups", "band", "sect"),
        check_vma=False,
    )
```

```python
import jax
import jax.numpy as jnp
from jax import lax
from jax.experimental import pallas as pl
from jax.experimental.pallas import tpu as pltpu
from jax.sharding import PartitionSpec as P


SIDE = 32
WIDE = SIDE + 4
LANES = 128
PER_PAIR = 2 * LANES // WIDE
TILES = -(-(WIDE // PER_PAIR * 2 * LANES + WIDE % PER_PAIR * WIDE) // LANES)
REACH = SIDE + 2
CHUNKS = 1
HALF = jnp.bfloat16
FULL = jnp.float32


def shift_from(block, axis, distance):
    count = lax.axis_size(axis)
    route = [(i - distance, i) for i in range(count) if 0 <= i - distance < count]
    return lax.ppermute(block, axis, route)


def swap(block, axis, bit):
    count = lax.axis_size(axis)
    return lax.ppermute(block, axis, [(i, i ^ bit) for i in range(count)])


def run(body, outs, ins, scratch, micros=1.0, limit=16, out_space=pltpu.VMEM):
    return pl.pallas_call(
        body,
        out_shape=outs,
        in_specs=[pl.BlockSpec(memory_space=pltpu.VMEM)] * len(ins),
        out_specs=[pl.BlockSpec(memory_space=out_space)] * len(outs),
        scratch_shapes=scratch,
        cost_estimate=pl.CostEstimate(
            flops=int(micros * 1.15e9), bytes_accessed=1024, transcendentals=0
        ),
        compiler_params=pltpu.CompilerParams(vmem_limit_bytes=limit * 1024 * 1024),
    )(*ins)


def arrival(bands):
    slots, bit = [0], bands // 2
    while bit:
        slots += [slot ^ bit for slot in slots]
        bit //= 2
    return slots


def here():
    return lax.axis_index("band"), lax.axis_index("sect")


def slots_at(at_ref, readers, sects, rows, cols):
    band, sect = here()
    count = at_ref.shape[1]
    bits = (cols * sects - 1).bit_length()
    both = jnp.left_shift(at_ref[0:1, :], bits) + at_ref[1:2, :]
    lane = lane_index((1, count))
    found = []
    for reader in readers:
        mine = lane == reader * sects + sect
        code = jnp.sum(jnp.where(mine, both, 0).astype(FULL)).astype(jnp.int32)
        row, col = jnp.right_shift(code, bits), jnp.bitwise_and(code, (1 << bits) - 1)
        found.append((row - band * rows, col - sect * cols))
    return found


def slot_anchors(at_ref, slots, sects, rows, cols):
    band, _ = here()
    return slots_at(at_ref, [jnp.bitwise_xor(band, j) for j in slots], sects, rows, cols)


def like(shape, dtype=HALF):
    return jax.ShapeDtypeStruct(shape, dtype)


def lane_index(shape):
    return lax.broadcasted_iota(jnp.int32, shape, len(shape) - 1)


def turn_rows(state_ref, flat):
    channels = state_ref.shape[0]
    flat[:channels] = state_ref[...]
    flat[channels:] = jnp.zeros((flat.shape[0] - channels,) + flat.shape[1:], HALF)
    return jnp.swapaxes(flat[...], 0, 1)


def pack(state):
    channels, rows, cols = state.shape
    padded = -(-channels // 8) * 8
    deep = -(-padded // 16) * 16
    span = -(-rows * REACH // LANES)

    def body(state_ref, right_ref, left_ref, rows_ref, flat):
        turned = turn_rows(state_ref, flat)
        rows_ref[...] = turned
        lane = lane_index((deep, LANES))
        tiles = [None] * span
        rim = jnp.zeros((deep, LANES), HALF)
        for r in range(rows):
            row = turned[r]
            at, off = divmod(r * REACH, LANES)
            moved = row if off == 0 else pltpu.roll(row, off, 1)
            if tiles[at] is None:
                tiles[at] = moved
            else:
                tiles[at] = jnp.where(lane >= off, moved, tiles[at])
            if off + REACH > LANES:
                tiles[at + 1] = moved
            moved = pltpu.roll(row, (2 * r + 2) % LANES, 1)
            rim = jnp.where((lane >= 2 * r) & (lane < 2 * r + 2), moved, rim)
        for at in range(span):
            right_ref[:, at * LANES : (at + 1) * LANES] = tiles[at][:padded]
        left_ref[...] = rim[:padded]

    return run(
        body,
        [like((padded, span * LANES)), like((padded, LANES)), like((rows, deep, cols))],
        [state],
        [pltpu.VMEM((deep, rows, cols), HALF)],
        micros=1.0,
    )


def prep(anchor, weights, biases, noise, bands, sects, rows, cols):
    steps, channels, cells = noise.shape
    count = len(weights)
    tile_rows = LANES // SIDE
    lines = len(biases)

    def body(at_ref, *refs):
        ins, lines_in, noise_ref = refs[:count], refs[count : count + lines], refs[count + lines]
        outs, square = refs[count + lines + 1 : -1], refs[-1]
        lines_out, noise_out = outs[count : count + lines], outs[count + lines]
        place_ref = outs[count + lines + 1]
        square[...] = jnp.zeros(square.shape, FULL)
        for k, (w_ref, o_ref) in enumerate(zip(ins, outs)):
            _, down, across = w_ref.shape
            o_ref[...] = jnp.zeros(o_ref.shape, HALF)
            for a in range(3):
                for b in range(3):
                    weight = w_ref[3 * a + b]
                    if k % 2 == 0:
                        square[:down, :across] = weight.astype(FULL)
                        weight = square[...].T.astype(HALF)
                    deep, wide = weight.shape
                    for v in range(2):
                        tap = (3 * (a + v) + b) * LANES
                        o_ref[v * LANES : v * LANES + deep, tap : tap + wide] = weight
        for line_ref, o_ref in zip(lines_in, lines_out):
            used = line_ref.shape[1]
            o_ref[...] = jnp.zeros(o_ref.shape, FULL)
            o_ref[:, :used] = line_ref[...]
            o_ref[:, LANES : LANES + used] = line_ref[...]
        for k in range(steps):
            for t in range(cells // LANES):
                block = noise_ref[k, :, t * LANES : (t + 1) * LANES].astype(FULL)
                block = jnp.concatenate(
                    [block, jnp.zeros((LANES - channels, LANES), FULL)], axis=0
                ).T.astype(HALF)
                for m in range(tile_rows):
                    r = t * tile_rows + m
                    noise_out[
                        k, r // 2 * SIDE : (r // 2 + 1) * SIDE, r % 2 * LANES : (r % 2 + 1) * LANES
                    ] = block[m * SIDE : (m + 1) * SIDE]
        cell = lax.broadcasted_iota(jnp.int32, (LANES, 2 * LANES), 0)
        target = lane_index((LANES, 2 * LANES))
        anchors = slot_anchors(at_ref, arrival(bands), sects, rows, cols)
        for j, (row0, col0) in enumerate(anchors):
            across = jnp.bitwise_and(cell, SIDE - 1) + col0
            for m in range(tile_rows):
                turn = jnp.bitwise_and(m - row0, tile_rows - 1)
                there = jnp.where(across < cols, across, across - cols + LANES + m * SIDE)
                hit = (target == there) & (cell >= turn * SIDE) & (cell < (turn + 1) * SIDE)
                place_ref[m, j * LANES : (j + 1) * LANES] = jnp.where(hit, 1.0, 0.0).astype(HALF)

    made = [like((2 * LANES, 12 * LANES))] * count
    made += [like((line.shape[0], 2 * LANES), FULL) for line in biases]
    made += [like((steps, cells // 2, 2 * LANES))]
    made += [like((tile_rows, bands * LANES, 2 * LANES))]
    scratch = [pltpu.VMEM((LANES, LANES), FULL)]
    out = run(body, made, [anchor, *weights, *biases, noise], scratch, micros=1.5)
    return out[:count], out[count : count + lines], *out[count + lines :]


def add_parts(kept, got):
    def body(kept_ref, got_ref, out_ref):
        out_ref[...] = kept_ref[...] + got_ref[...]

    return run(body, [like(kept.shape)], [kept, got], [], micros=0.3)[0]


def window_tile(source, t, row0, col0, low, high, rows, padded):
    lane = lane_index((1, LANES))
    total = jnp.zeros((padded, LANES), HALF)
    pair, half = divmod(t, 2)
    for k in range(PER_PAIR):
        i = pair * PER_PAIR + k
        zone = k * WIDE - half * LANES
        if i >= WIDE or zone >= LANES or zone + WIDE <= 0:
            continue
        r = row0 + i
        first = jnp.where((r >= 0) & (r < rows), zone + low, 2 * LANES)
        keep = jnp.where((lane >= first) & (lane < zone + high), 1.0, 0.0).astype(HALF)
        turn = jnp.bitwise_and(zone + 2 - col0, LANES - 1)
        value = pltpu.roll(source[jnp.clip(r, 0, rows - 1), :padded], turn, 1)
        total = total + value * keep
    return total


def extract_own(anchor, turned, padded, bands, sects):
    rows, _, cols = turned.shape

    def body(at_ref, rows_ref, out_ref):
        anchors = slot_anchors(at_ref, range(bands), sects, rows, cols)
        for j, (row0, col0) in enumerate(anchors):
            row0 = row0 - 2
            inside = (row0 > -WIDE) & (row0 < rows)
            low, high = jnp.maximum(2 - col0, 0), jnp.minimum(cols + 2 - col0, WIDE)

            @pl.when(inside)
            def _(j=j, row0=row0, col0=col0, low=low, high=high):
                for t in range(TILES):
                    out_ref[j, :, t * LANES : (t + 1) * LANES] = window_tile(
                        rows_ref, t, row0, col0, low, high, rows, padded
                    )

            @pl.when(jnp.logical_not(inside))
            def _(j=j):
                out_ref[j] = jnp.zeros((padded, TILES * LANES), HALF)

    return run(body, [like((bands, padded, TILES * LANES))], [anchor, turned], [], micros=1.5)[0]


def extract_rim(anchor, parts, turned, right, left, bands, sects):
    rows, deep, cols = turned.shape
    padded = right.shape[0]

    def body(at_ref, part_ref, rows_ref, right_ref, left_ref,
             own_ref, low_ref, odd_ref, high_ref, near_ref, cross_ref, ext):
        lane = lane_index((padded, LANES))
        none = jnp.zeros((padded, LANES), HALF)
        rim = left_ref[...]

        def expand(r):
            at, off = divmod(r * REACH, LANES)
            piece = right_ref[:, at * LANES : (at + 1) * LANES]
            if off:
                piece = pltpu.roll(piece, LANES - off, 1)
            if off + REACH > LANES:
                after = right_ref[:, (at + 1) * LANES : (at + 2) * LANES]
                piece = jnp.where(lane < LANES - off, piece, pltpu.roll(after, LANES - off, 1))
            turn = pltpu.roll(rim, (LANES - 2 - 2 * r) % LANES, 1)
            ext[r, :padded] = jnp.where(
                lane < REACH, piece, jnp.where(lane >= LANES - 2, turn, none)
            )

        ext[:, padded:] = jnp.zeros((rows, deep - padded, LANES), HALF)
        outer = (0, 1, rows - 2, rows - 1)
        for r in outer:
            expand(r)
        even = jnp.bitwise_and(here()[0], 1) == 0
        for k in range(2):
            top, low = k, rows - 2 + k
            near_ref[k, :, :cols] = jnp.where(even, rows_ref[low], rows_ref[top])
            near_ref[k, :, cols:] = jnp.where(even, ext[low], ext[top])
            cross_ref[k, :, :cols] = jnp.where(even, rows_ref[top], rows_ref[low])
            cross_ref[k, :, cols:] = jnp.where(even, ext[top], ext[low])

        def target(j):
            if j < 2:
                return (own_ref, odd_ref)[j], 0
            return (low_ref, high_ref)[j % 2], j // 2 - 1

        crossing = []
        anchors = slot_anchors(at_ref, range(bands), sects, rows, cols)
        for j, (row0, col0) in enumerate(anchors):
            row0 = row0 - 2
            inside = (row0 > -WIDE) & (row0 < rows)
            over = inside & ((col0 < 2) | (col0 > cols - REACH))
            low = jnp.where(col0 < 2, 0, cols + 2 - col0)
            high = jnp.where(col0 < 2, 2 - col0, WIDE)
            crossing.append((over, row0, col0, low, high))
            out_ref, at = target(j)
            out_ref[at] = part_ref[j]
        some = crossing[0][0]
        for over, *_ in crossing[1:]:
            some = some | over

        @pl.when(some)
        def _():
            for r in range(rows):
                if r not in outer:
                    expand(r)

        for j, (over, *where) in enumerate(crossing):
            out_ref, at = target(j)

            @pl.when(over)
            def _(out_ref=out_ref, at=at, where=where):
                for t in range(TILES):
                    out_ref[at, :, t * LANES : (t + 1) * LANES] += window_tile(
                        ext, t, *where, rows, padded
                    )

    one = like((1, padded, TILES * LANES))
    rest = like((max(bands // 2 - 1, 1), padded, TILES * LANES))
    edge = like((2, deep, cols + LANES))
    return run(
        body,
        [one, rest, one, rest, edge, edge],
        [anchor, parts, turned, right, left],
        [pltpu.VMEM((rows, deep, LANES), HALF)],
        micros=1.5
    )


def product(view, weight):
    return lax.dot_general(
        view, weight, (((1,), (1,)), ((), ())), preferred_element_type=FULL
    )


def gather_pairs(shifted, first, count):
    view = jnp.concatenate(
        [shifted[b, pl.ds(first + u, count), v] for u in (0, 1) for v in (0, 1) for b in (0, 1, 2)],
        axis=-1,
    )
    return view.reshape(count * view.shape[1], view.shape[2])


def silu(value):
    return value / (1.0 + jnp.exp(-value))


def patch_step(anchor, addends, noise, weights, biases, step_bias, sects, limits):
    padded = addends[0].shape[1]
    steps = noise.shape[0]
    half = SIDE // 2
    loose = 48

    def body(*refs):
        at_ref, parts = refs[0], refs[1 : 1 + len(addends)]
        band, sect = here()
        mine = lane_index(at_ref.shape) == band * sects + sect
        at = jnp.sum(jnp.where(mine, at_ref[...], 0).astype(FULL), axis=1, keepdims=True)
        row0, col0 = at.astype(jnp.int32)[0:1][None], at.astype(jnp.int32)[1:2][None]
        (noise_ref, w_in, w_out, d_in, d_out, b_in, b_out, b_step, b_den, out_ref,
         flat, state_sh, hid, hid_sh, pad, pad_sh, corr, state) = refs[1 + len(addends) :]
        for t in range(TILES):
            lanes = slice(t * LANES, (t + 1) * LANES)
            tile = parts[0][0, :, lanes].astype(FULL)
            for part in parts[1:]:
                tile = tile + part[0, :, lanes].astype(FULL)
            tile = jnp.concatenate([tile, jnp.zeros((LANES - padded, LANES), FULL)], axis=0)
            flat[lanes, :] = tile.T
        for i in range(WIDE):
            pair, k = divmod(i, PER_PAIR)
            off = pair * 2 * LANES + k * WIDE
            for b in range(3):
                state_sh[b, i // 2, i % 2] = flat[off + b : off + b + loose, :].astype(HALF)
        pairs = half + 1
        value = product(gather_pairs(state_sh, 0, pairs), w_in[...])
        value = silu(value + b_in[...]).reshape(pairs, loose, 2 * LANES)
        pair = lax.broadcasted_iota(jnp.int32, value.shape, 0)
        col = lax.broadcasted_iota(jnp.int32, value.shape, 1)
        odd = (lane_index(value.shape) >= LANES).astype(jnp.int32)
        grid_row = row0 - 1 + 2 * pair + odd
        grid_col = col0 - 1 + col
        keep = (
            (grid_row >= 0) & (grid_row < limits[0])
            & (grid_col >= 0) & (grid_col < limits[1]) & (col < SIDE + 2)
        )
        value = jnp.where(keep, value, 0.0)
        hid[:, 0] = value[:, :, :LANES]
        hid[:, 1] = value[:, :, LANES:]
        for b in range(3):
            hid_sh[b] = hid[:, :, b : b + SIDE, :].astype(HALF)
        value = product(gather_pairs(hid_sh, 0, half), w_out[...])
        center = jnp.concatenate(
            [state_sh[2, 1 : 1 + half, v, :SIDE, :] for v in (0, 1)], axis=-1
        ).astype(FULL).reshape(half * SIDE, 2 * LANES)
        mean = (center + value + b_out[...]).astype(HALF).astype(FULL)
        state[...] = mean + noise_ref[0].astype(FULL)
        pad[...] = jnp.zeros(pad.shape, FULL)
        deal = half // CHUNKS
        trips = jnp.where(band >= 0, CHUNKS, 0)

        def fill(source, first, count):
            shaped = source.reshape(count, SIDE, 2 * LANES)
            pad[pl.ds(first, count), 1, 8 : 8 + SIDE] = shaped[:, :, :LANES]
            pad[pl.ds(first + 1, count), 0, 8 : 8 + SIDE] = shaped[:, :, LANES:]

        def shift():
            for b in range(3):
                pad_sh[b] = pad[:, :, 7 + b : 7 + b + SIDE, :].astype(HALF)

        for step in range(steps):
            fill(state[...], 0, half)
            shift()

            def first(c, carry, step=step):
                value = product(gather_pairs(pad_sh, c * deal, deal), d_in[...])
                fill(silu(value + b_step[step : step + 1]), c * deal, deal)
                return carry

            lax.fori_loop(0, trips, first, 0)
            shift()

            def second(c, carry, step=step):
                value = product(gather_pairs(pad_sh, c * deal, deal), d_out[...])
                cells = pl.ds(pl.multiple_of(c * deal * SIDE, deal * SIDE), deal * SIDE)
                value = state[cells] - 0.5 * (value + b_den[...])
                if step + 1 < steps:
                    value = value + 0.5 * noise_ref[step + 1, cells].astype(FULL)
                state[cells] = value
                return carry

            lax.fori_loop(0, trips, second, 0)
        change = (state[...] - mean).reshape(half, SIDE, 2 * LANES)
        corr[:, 0] = change[:, :, :LANES]
        corr[:, 1] = change[:, :, LANES:]
        cells = corr[...].reshape(SIDE * SIDE, LANES)
        for t in range(SIDE * SIDE // LANES):
            lanes = slice(t * LANES, (t + 1) * LANES)
            out_ref[:, lanes] = cells[lanes].T[:padded].astype(HALF)

    return run(
        body,
        [like((padded, SIDE * SIDE))],
        [anchor, *addends, noise, *weights, *biases[:2], step_bias, biases[2]],
        [
            pltpu.VMEM((TILES * LANES, LANES), FULL),
            pltpu.VMEM((3, WIDE // 2, 2, loose, LANES), HALF),
            pltpu.VMEM((half + 1, 2, loose, LANES), FULL),
            pltpu.VMEM((3, half + 1, 2, SIDE, LANES), HALF),
            pltpu.VMEM((half + 1, 2, loose, LANES), FULL),
            pltpu.VMEM((3, half + 1, 2, SIDE, LANES), HALF),
            pltpu.VMEM((half, 2, SIDE, LANES), FULL),
            pltpu.VMEM((half * SIDE, 2 * LANES), FULL),
        ],
        micros=8.0
    )[0]


def spread(turned, right, left):
    rows, _, cols = turned.shape
    span = right.shape[1]
    loose = cols + 16

    def body(rows_ref, right_ref, left_ref, out_ref, after, before, line):
        def upright(value):
            value = value.astype(FULL)
            return jnp.concatenate(
                [value, jnp.zeros((LANES - value.shape[0], value.shape[1]), FULL)], axis=0
            ).T

        for t in range(span // LANES):
            lanes = slice(t * LANES, (t + 1) * LANES)
            after[lanes] = upright(right_ref[:, lanes])
        before[...] = upright(left_ref[...])
        line[...] = jnp.zeros(line.shape, FULL)

        def spread_rows(i, carry):
            for v in range(2):
                r = 2 * i + v
                line[v, 8 : 8 + cols] = upright(rows_ref[r])
                line[v, 8 + cols : 10 + cols] = after[pl.ds(r * REACH, 2)]
                line[v, 6:8] = before[pl.ds(2 * r, 2)]
                for b in range(3):
                    out_ref[b, i, v] = line[v, 6 + b : 6 + b + loose, :].astype(HALF)
            return carry

        lax.fori_loop(0, rows // 2, spread_rows, 0)

    return run(
        body,
        [like((3, rows // 2, 2, loose, LANES))],
        [turned, right, left],
        [
            pltpu.VMEM((span, LANES), FULL),
            pltpu.VMEM((LANES, LANES), FULL),
            pltpu.VMEM((2, loose + 8, LANES), FULL),
        ],
        micros=2.5
    )[0]


def grid_mean(shifted, near, cross, lower, padded, weights, biases, limits):
    rows = 2 * shifted.shape[1]
    _, deep, width = near.shape
    cols = width - LANES
    loose = cols + 16
    made = rows // 2
    pairs_in, pairs_out = 3, made // 4
    hidden_pairs = made // 2 + 1
    if hidden_pairs % pairs_in:
        hidden_pairs += pairs_in - hidden_pairs % pairs_in
    state_pairs = hidden_pairs + 1
    base = rows - made - 2 if lower else -2

    def body(shifted_ref, near_ref, cross_ref, w_in, w_out, b_in, b_out, out_ref,
             line, state_sh, hid, hid_sh):
        band, sect = here()
        row0 = band * rows + base + 1
        col0 = sect * cols - 1

        for pair in range(made // 2 + 2, state_pairs):
            for b in range(3):
                state_sh[b, pair] = jnp.zeros((2, loose, LANES), HALF)
        edge = made // 2 + 1 if lower else 0
        skip = 0 if lower else 1
        given = made // 2 + 1
        at = (rows - made) // 2 - 1 if lower else 0
        for b in range(3):
            state_sh[b, skip : skip + given] = shifted_ref[b, at : at + given]
        pair = jnp.bitwise_and(band, 1) == (0 if lower else 1)
        beyond = band == (limits[0] // rows - 1 if lower else 0)
        none = jnp.zeros((deep, width), HALF)
        for v in range(2):
            rim = jnp.where(beyond, none, jnp.where(pair, near_ref[v], cross_ref[v]))
            value = jnp.concatenate(
                [rim.astype(FULL), jnp.zeros((LANES - deep, width), FULL)], axis=0
            ).T
            line[v, 8 : 8 + cols] = value[:cols]
            line[v, 8 + cols :] = value[cols : cols + 16]
            line[v, :8] = value[width - 8 :]
            for b in range(3):
                state_sh[b, edge, v] = line[v, 6 + b : 6 + b + loose, :].astype(HALF)

        def first(chunk, carry):
            start = chunk * pairs_in
            value = product(gather_pairs(state_sh, start, pairs_in), w_in[...])
            value = silu(value + b_in[...]).reshape(pairs_in, loose, 2 * LANES)
            pair = lax.broadcasted_iota(jnp.int32, value.shape, 0)
            col = lax.broadcasted_iota(jnp.int32, value.shape, 1)
            odd = (lane_index(value.shape) >= LANES).astype(jnp.int32)
            grid_row = row0 + 2 * (start + pair) + odd
            grid_col = col0 + col
            keep = (
                (grid_row >= 0) & (grid_row < limits[0])
                & (grid_col >= 0) & (grid_col < limits[1])
            )
            value = jnp.where(keep, value, 0.0)
            hid[:, 0] = value[:, :, :LANES]
            hid[:, 1] = value[:, :, LANES:]
            for b in range(3):
                hid_sh[b, pl.ds(start, pairs_in)] = hid[:, :, b : b + cols, :].astype(HALF)
            return carry

        lax.fori_loop(0, hidden_pairs // pairs_in, first, 0)

        def second(chunk, carry):
            start = chunk * pairs_out
            value = product(gather_pairs(hid_sh, start, pairs_out), w_out[...]) + b_out[...]
            value = value.reshape(pairs_out, cols, 2 * LANES)
            for k in range(pairs_out):
                for v in range(2):
                    center = state_sh[2, start + k + 1, v, :cols, :].astype(FULL)
                    mean = center + value[k, :, v * LANES : (v + 1) * LANES]
                    out_ref[2 * (start + k) + v] = mean.T[:padded].astype(HALF)
            return carry

        lax.fori_loop(0, made // 2 // pairs_out, second, 0)

    return run(
        body,
        [like((made, padded, cols))],
        [shifted, near, cross, *weights, *biases],
        [
            pltpu.VMEM((2, loose + 8, LANES), FULL),
            pltpu.VMEM((3, state_pairs, 2, loose, LANES), HALF),
            pltpu.VMEM((pairs_in, 2, loose, LANES), FULL),
            pltpu.VMEM((3, hidden_pairs, 2, cols, LANES), HALF),
        ],
        micros=3.5,
    )[0]


def fill_view(view, at_ref, pieces, sources, sects, rows, cols):
    padded = pieces[0].shape[-2]
    tile_rows = view.shape[0]
    none = jnp.zeros((padded, LANES), HALF)
    anchors = slot_anchors(at_ref, sources, sects, rows, cols)
    for at, (piece, (row0, _)) in enumerate(zip(pieces, anchors)):
        lanes = slice(at * LANES, (at + 1) * LANES)
        for r in range(rows):
            i = r - row0
            tile = jnp.clip(
                jnp.right_shift(i, tile_rows.bit_length() - 1), 0, SIDE // tile_rows - 1
            )
            value = piece[:, pl.ds(pl.multiple_of(tile * LANES, LANES), LANES)]
            inside = (i >= 0) & (i < SIDE)
            view[r % tile_rows, r // tile_rows, :padded, lanes] = jnp.where(inside, value, none)
    view[:, :, padded:, :] = jnp.zeros(
        view.shape[:2] + (view.shape[2] - padded, view.shape[3]), HALF
    )


def view_shape(pieces, rows):
    tile_rows = LANES // SIDE
    deep = -(-pieces[0].shape[-2] // 16) * 16
    return (tile_rows, rows // tile_rows, deep, len(pieces) * LANES)


def gather_view(anchor, pieces, sources, sects, rows, cols):
    def body(at_ref, *refs):
        fill_view(refs[-1], at_ref, refs[:-1], sources, sects, rows, cols)

    shape = view_shape(pieces, rows)
    return run(body, [like(shape)], [anchor, *pieces], [], micros=0.8)[0]


def canvas(anchor, early, pieces, sources, place, sects, rows, cols):
    padded = pieces[0].shape[-2]
    deep = -(-padded // 16) * 16
    total = anchor.shape[1]
    slots = len(pieces)
    tile_rows = LANES // SIDE
    groups = rows // tile_rows

    def body(at_ref, *refs):
        band, sect = here()
        early_ref, place_ref, spill_ref, out_ref, inverse_ref, view = refs[slots:]
        fill_view(view, at_ref, refs[:slots], sources, sects, rows, cols)
        spilled = None
        for m in range(tile_rows):
            both = jnp.concatenate([early_ref[m], view[m]], axis=-1)
            value = jnp.dot(
                both.reshape(groups * deep, both.shape[-1]), place_ref[m],
                preferred_element_type=FULL,
            ).reshape(groups, deep, 2 * LANES)
            for k in range(groups):
                out_ref[k * tile_rows + m] = value[k, :padded, :LANES]
            part = value[:, :padded, LANES:]
            spilled = part if spilled is None else spilled + part
        for k in range(groups):
            spill_ref[:, k * LANES : (k + 1) * LANES] = spilled[k].astype(HALF)
        tall, wide = (rows, total), (total, cols)
        down = lax.broadcasted_iota(jnp.int32, tall, 0) + band * rows - at_ref[0:1, :]
        across = lane_index(wide) + sect * cols - at_ref[1:2, :].astype(FULL).T.astype(jnp.int32)
        down = jnp.where((down >= 0) & (down < SIDE), 1.0, 0.0)
        across = jnp.where((across >= 0) & (across < SIDE), 1.0, 0.0)
        count = jnp.dot(down.astype(HALF), across.astype(HALF), preferred_element_type=FULL)
        inverse_ref[...] = 1.0 / jnp.maximum(count, 1.0)

    return run(
        body,
        [
            like((padded, rows * SIDE)),
            like((rows, padded, cols), FULL),
            like((rows, cols), FULL),
        ],
        [anchor, *pieces, early, place],
        [pltpu.VMEM(view_shape(pieces, rows), HALF)],
        micros=1.5
    )


def finish(means, summed, arrived, inverse, channels):
    rows, padded, cols = summed.shape
    deep = -(-padded // 16) * 16
    half = means[0].shape[0]
    chunk = 8

    def body(top_ref, low_ref, sum_ref, spill_ref, inverse_ref, out_ref, flat, ready, sems):
        lane = lane_index((padded, LANES))
        none = jnp.zeros((padded, LANES), HALF)
        flat[:, padded:] = jnp.zeros((chunk, deep - padded, cols), HALF)
        copies = []
        for first in range(0, rows, chunk):
            for r in range(first, first + chunk):
                at, low = divmod(r * SIDE, LANES)
                extra = spill_ref[:, at * LANES : (at + 1) * LANES]
                if low:
                    extra = pltpu.roll(extra, LANES - low, 1)
                extra = jnp.where(lane < SIDE, extra, none).astype(FULL)
                mean = top_ref[r] if r < half else low_ref[r - half]
                value = mean.astype(FULL) + (sum_ref[r] + extra) * inverse_ref[r : r + 1]
                flat[r - first, :padded] = value.astype(HALF)
            k = first // chunk
            ready[k] = jnp.swapaxes(flat[...], 0, 1)[:channels]
            copies.append(
                pltpu.make_async_copy(
                    ready.at[k], out_ref.at[:, pl.ds(first, chunk), :], sems.at[k]
                )
            )
            copies[-1].start()
        for copy in copies:
            copy.wait()

    return run(
        body,
        [like((channels, rows, cols))],
        [*means, summed, arrived, inverse],
        [
            pltpu.VMEM((chunk, deep, cols), HALF),
            pltpu.VMEM((rows // chunk, channels, chunk, cols), HALF),
            pltpu.SemaphoreType.DMA((rows // chunk,)),
        ],
        micros=2.0,
        out_space=pltpu.HBM,
    )[0]


def step(
    state_field,
    conv_in_weight,
    conv_in_bias,
    conv_out_weight,
    conv_out_bias,
    patch_anchor,
    patch_noise,
    denoise_in_weight,
    step_bias,
    denoise_out_weight,
    denoise_bias,
):
    bands = lax.axis_size("band")
    sects = lax.axis_size("sect")
    channels, rows, cols = state_field.shape
    limits = (rows * bands, cols * sects)

    anchor = patch_anchor.T

    right_rim, left_rim, turned = pack(state_field)
    right = shift_from(right_rim, "sect", -1)
    left = shift_from(left_rim, "sect", 1)

    made, lines, noise, place = prep(
        anchor,
        [
            conv_in_weight.transpose(0, 2, 1),
            conv_out_weight,
            denoise_in_weight.transpose(0, 2, 1),
            denoise_out_weight,
        ],
        [conv_in_bias[None, :], conv_out_bias[None, :], denoise_bias[None, :], step_bias],
        patch_noise[0],
        bands,
        sects,
        rows,
        cols,
    )
    biases, step_lines = lines[:3], lines[3]

    padded = right_rim.shape[0]
    parts = extract_own(anchor, turned, padded, bands, sects)
    own, kept, own_sent, sent, edge_near, edge_cross = extract_rim(
        anchor, parts, turned, right, left, bands, sects
    )
    addends = [own]
    if bands > 2:
        got = swap(sent, "band", 1)
        kept = add_parts(kept, got)
    bit = 2
    while bit < bands:
        got = swap(kept[0::2], "band", bit)
        addends.append(got)
        kept = kept[1::2] + got[1:]
        bit *= 2
    addends.append(swap(own_sent, "band", 1))
    rim_near = swap(edge_near, "band", 1)
    steps = [(i, i + 1) for i in range(1, bands - 1, 2)]
    alone = [(i, i) for i in range(bands) if all(i not in step for step in steps)]
    rim_cross = lax.ppermute(edge_cross, "band", steps + [(j, i) for i, j in steps] + alone)
    correction = patch_step(
        anchor, addends, noise, made, biases, step_lines, sects, limits
    )
    pieces = [correction]
    sources = arrival(bands)
    bit = bands // 2
    while bit:
        fresh = []
        for piece in pieces:
            fresh.append(swap(piece, "band", bit))
        pieces += fresh
        bit //= 2

    shifted = spread(turned, right, left)
    top_mean = grid_mean(shifted, rim_near, rim_cross, False, padded, made[:2], biases[:2], limits)
    low_mean = grid_mean(shifted, rim_near, rim_cross, True, padded, made[:2], biases[:2], limits)
    early = gather_view(anchor, pieces[:-1], sources[:-1], sects, rows, cols)
    spilled, summed, inverse = canvas(
        anchor, early, pieces[-1:], sources[-1:], place, sects, rows, cols
    )
    arrived = shift_from(spilled, "sect", 1)
    return finish([top_mean, low_mean], summed, arrived, inverse, channels)


def solution(mesh):
    placed = (
        P("groups", "band", "sect"),
        P(),
        P(),
        P(),
        P(),
        P("groups", None),
        P(("groups", "band", "sect"), None, None, None),
        P(),
        P(),
        P(),
        P(),
    )
    return jax.shard_map(
        step,
        mesh=mesh,
        in_specs=placed,
        out_specs=P("groups", "band", "sect"),
        check_vma=False,
    )
```

```python
import jax
import jax.numpy as jnp
from jax import lax
from jax.experimental import pallas as pl
from jax.experimental.pallas import tpu as pltpu
from jax.sharding import PartitionSpec as P


SIDE = 32
WIDE = SIDE + 4
LANES = 128
PER_PAIR = 2 * LANES // WIDE
TILES = -(-(WIDE // PER_PAIR * 2 * LANES + WIDE % PER_PAIR * WIDE) // LANES)
REACH = SIDE + 2
CHUNKS = 1
HALF = jnp.bfloat16
FULL = jnp.float32


def shift_from(block, axis, distance):
    count = lax.axis_size(axis)
    route = [(i - distance, i) for i in range(count) if 0 <= i - distance < count]
    return lax.ppermute(block, axis, route)


def swap(block, axis, bit):
    count = lax.axis_size(axis)
    return lax.ppermute(block, axis, [(i, i ^ bit) for i in range(count)])


def run(body, outs, ins, scratch, micros=1.0, limit=16, out_space=pltpu.VMEM):
    return pl.pallas_call(
        body,
        out_shape=outs,
        in_specs=[pl.BlockSpec(memory_space=pltpu.VMEM)] * len(ins),
        out_specs=[pl.BlockSpec(memory_space=out_space)] * len(outs),
        scratch_shapes=scratch,
        cost_estimate=pl.CostEstimate(
            flops=int(micros * 1.15e9), bytes_accessed=1024, transcendentals=0
        ),
        compiler_params=pltpu.CompilerParams(vmem_limit_bytes=limit * 1024 * 1024),
    )(*ins)


def arrival(bands):
    slots, bit = [0], bands // 2
    while bit:
        slots += [slot ^ bit for slot in slots]
        bit //= 2
    return slots


def here():
    return lax.axis_index("band"), lax.axis_index("sect")


def slots_at(at_ref, readers, sects, rows, cols):
    band, sect = here()
    count = at_ref.shape[1]
    bits = (cols * sects - 1).bit_length()
    both = jnp.left_shift(at_ref[0:1, :], bits) + at_ref[1:2, :]
    lane = lane_index((1, count))
    found = []
    for reader in readers:
        mine = lane == reader * sects + sect
        code = jnp.sum(jnp.where(mine, both, 0).astype(FULL)).astype(jnp.int32)
        row, col = jnp.right_shift(code, bits), jnp.bitwise_and(code, (1 << bits) - 1)
        found.append((row - band * rows, col - sect * cols))
    return found


def slot_anchors(at_ref, slots, sects, rows, cols):
    band, _ = here()
    return slots_at(at_ref, [jnp.bitwise_xor(band, j) for j in slots], sects, rows, cols)


def like(shape, dtype=HALF):
    return jax.ShapeDtypeStruct(shape, dtype)


def lane_index(shape):
    return lax.broadcasted_iota(jnp.int32, shape, len(shape) - 1)


def turn_rows(state_ref, flat):
    channels = state_ref.shape[0]
    flat[:channels] = state_ref[...]
    flat[channels:] = jnp.zeros((flat.shape[0] - channels,) + flat.shape[1:], HALF)
    return jnp.swapaxes(flat[...], 0, 1)


def pack(state):
    channels, rows, cols = state.shape
    padded = -(-channels // 8) * 8
    deep = -(-padded // 16) * 16
    span = -(-rows * REACH // LANES)

    def body(state_ref, right_ref, rows_ref, flat):
        turned = turn_rows(state_ref, flat)
        rows_ref[...] = turned
        lane = lane_index((deep, LANES))
        tiles = [None] * span
        for r in range(rows):
            row = turned[r]
            at, off = divmod(r * REACH, LANES)
            moved = row if off == 0 else pltpu.roll(row, off, 1)
            if tiles[at] is None:
                tiles[at] = moved
            else:
                tiles[at] = jnp.where(lane >= off, moved, tiles[at])
            if off + REACH > LANES:
                tiles[at + 1] = moved
        for at in range(span):
            right_ref[:, at * LANES : (at + 1) * LANES] = tiles[at][:padded]

    return run(
        body,
        [like((padded, span * LANES)), like((rows, deep, cols))],
        [state],
        [pltpu.VMEM((deep, rows, cols), HALF)],
        micros=1.0,
    )


def pack_left(turned, padded):
    rows, deep, _ = turned.shape

    def body(rows_ref, left_ref):
        lane = lane_index((deep, LANES))
        rim = jnp.zeros((deep, LANES), HALF)
        for r in range(rows):
            moved = pltpu.roll(rows_ref[r], (2 * r + 2) % LANES, 1)
            rim = jnp.where((lane >= 2 * r) & (lane < 2 * r + 2), moved, rim)
        left_ref[...] = rim[:padded]

    return run(body, [like((padded, LANES))], [turned], [], micros=0.3)[0]


def prep(anchor, weights, biases, noise, bands, sects, rows, cols):
    steps, channels, cells = noise.shape
    count = len(weights)
    tile_rows = LANES // SIDE
    lines = len(biases)

    def body(at_ref, *refs):
        ins, lines_in, noise_ref = refs[:count], refs[count : count + lines], refs[count + lines]
        outs, square = refs[count + lines + 1 : -1], refs[-1]
        lines_out, noise_out = outs[count : count + lines], outs[count + lines]
        place_ref = outs[count + lines + 1]
        square[...] = jnp.zeros(square.shape, FULL)
        for k, (w_ref, o_ref) in enumerate(zip(ins, outs)):
            _, down, across = w_ref.shape
            o_ref[...] = jnp.zeros(o_ref.shape, HALF)
            for a in range(3):
                for b in range(3):
                    weight = w_ref[3 * a + b]
                    if k % 2 == 0:
                        square[:down, :across] = weight.astype(FULL)
                        weight = square[...].T.astype(HALF)
                    deep, wide = weight.shape
                    for v in range(2):
                        tap = (3 * (a + v) + b) * LANES
                        o_ref[v * LANES : v * LANES + deep, tap : tap + wide] = weight
        for line_ref, o_ref in zip(lines_in, lines_out):
            used = line_ref.shape[1]
            o_ref[...] = jnp.zeros(o_ref.shape, FULL)
            o_ref[:, :used] = line_ref[...]
            o_ref[:, LANES : LANES + used] = line_ref[...]
        for k in range(steps):
            for t in range(cells // LANES):
                block = noise_ref[k, :, t * LANES : (t + 1) * LANES].astype(FULL)
                block = jnp.concatenate(
                    [block, jnp.zeros((LANES - channels, LANES), FULL)], axis=0
                ).T.astype(HALF)
                for m in range(tile_rows):
                    r = t * tile_rows + m
                    noise_out[
                        k, r // 2 * SIDE : (r // 2 + 1) * SIDE, r % 2 * LANES : (r % 2 + 1) * LANES
                    ] = block[m * SIDE : (m + 1) * SIDE]
        cell = lax.broadcasted_iota(jnp.int32, (LANES, 2 * LANES), 0)
        target = lane_index((LANES, 2 * LANES))
        anchors = slot_anchors(at_ref, arrival(bands), sects, rows, cols)
        for j, (row0, col0) in enumerate(anchors):
            across = jnp.bitwise_and(cell, SIDE - 1) + col0
            for m in range(tile_rows):
                turn = jnp.bitwise_and(m - row0, tile_rows - 1)
                there = jnp.where(across < cols, across, across - cols + LANES + m * SIDE)
                hit = (target == there) & (cell >= turn * SIDE) & (cell < (turn + 1) * SIDE)
                place_ref[m, j * LANES : (j + 1) * LANES] = jnp.where(hit, 1.0, 0.0).astype(HALF)

    made = [like((2 * LANES, 12 * LANES))] * count
    made += [like((line.shape[0], 2 * LANES), FULL) for line in biases]
    made += [like((steps, cells // 2, 2 * LANES))]
    made += [like((tile_rows, bands * LANES, 2 * LANES))]
    scratch = [pltpu.VMEM((LANES, LANES), FULL)]
    out = run(body, made, [anchor, *weights, *biases, noise], scratch, micros=1.5)
    return out[:count], out[count : count + lines], *out[count + lines :]


def add_parts(kept, got):
    def body(kept_ref, got_ref, out_ref):
        out_ref[...] = kept_ref[...] + got_ref[...]

    return run(body, [like(kept.shape)], [kept, got], [], micros=0.3)[0]


def window_tile(source, t, row0, col0, low, high, rows, padded):
    lane = lane_index((1, LANES))
    total = jnp.zeros((padded, LANES), HALF)
    pair, half = divmod(t, 2)
    for k in range(PER_PAIR):
        i = pair * PER_PAIR + k
        zone = k * WIDE - half * LANES
        if i >= WIDE or zone >= LANES or zone + WIDE <= 0:
            continue
        r = row0 + i
        first = jnp.where((r >= 0) & (r < rows), zone + low, 2 * LANES)
        keep = jnp.where((lane >= first) & (lane < zone + high), 1.0, 0.0).astype(HALF)
        turn = jnp.bitwise_and(zone + 2 - col0, LANES - 1)
        value = pltpu.roll(source[jnp.clip(r, 0, rows - 1), :padded], turn, 1)
        total = total + value * keep
    return total


def extract_own(anchor, turned, padded, bands, sects):
    rows, _, cols = turned.shape

    def body(at_ref, rows_ref, out_ref):
        anchors = slot_anchors(at_ref, range(bands), sects, rows, cols)
        for j, (row0, col0) in enumerate(anchors):
            row0 = row0 - 2
            inside = (row0 > -WIDE) & (row0 < rows)
            low, high = jnp.maximum(2 - col0, 0), jnp.minimum(cols + 2 - col0, WIDE)

            @pl.when(inside)
            def _(j=j, row0=row0, col0=col0, low=low, high=high):
                for t in range(TILES):
                    out_ref[j, :, t * LANES : (t + 1) * LANES] = window_tile(
                        rows_ref, t, row0, col0, low, high, rows, padded
                    )

            @pl.when(jnp.logical_not(inside))
            def _(j=j):
                out_ref[j] = jnp.zeros((padded, TILES * LANES), HALF)

    return run(body, [like((bands, padded, TILES * LANES))], [anchor, turned], [], micros=1.5)[0]


def extract_rim(anchor, parts, turned, right, left, bands, sects):
    rows, deep, cols = turned.shape
    padded = right.shape[0]

    def body(at_ref, part_ref, rows_ref, right_ref, left_ref,
             own_ref, low_ref, odd_ref, high_ref, near_ref, cross_ref, ext):
        lane = lane_index((padded, LANES))
        none = jnp.zeros((padded, LANES), HALF)
        rim = left_ref[...]

        def expand(r):
            at, off = divmod(r * REACH, LANES)
            piece = right_ref[:, at * LANES : (at + 1) * LANES]
            if off:
                piece = pltpu.roll(piece, LANES - off, 1)
            if off + REACH > LANES:
                after = right_ref[:, (at + 1) * LANES : (at + 2) * LANES]
                piece = jnp.where(lane < LANES - off, piece, pltpu.roll(after, LANES - off, 1))
            turn = pltpu.roll(rim, (LANES - 2 - 2 * r) % LANES, 1)
            ext[r, :padded] = jnp.where(
                lane < REACH, piece, jnp.where(lane >= LANES - 2, turn, none)
            )

        ext[:, padded:] = jnp.zeros((rows, deep - padded, LANES), HALF)
        outer = (0, 1, rows - 2, rows - 1)
        for r in outer:
            expand(r)
        even = jnp.bitwise_and(here()[0], 1) == 0
        for k in range(2):
            top, low = k, rows - 2 + k
            near_ref[k, :, :cols] = jnp.where(even, rows_ref[low], rows_ref[top])
            near_ref[k, :, cols:] = jnp.where(even, ext[low], ext[top])
            cross_ref[k, :, :cols] = jnp.where(even, rows_ref[top], rows_ref[low])
            cross_ref[k, :, cols:] = jnp.where(even, ext[top], ext[low])

        def target(j):
            if j < 2:
                return (own_ref, odd_ref)[j], 0
            return (low_ref, high_ref)[j % 2], j // 2 - 1

        crossing = []
        anchors = slot_anchors(at_ref, range(bands), sects, rows, cols)
        for j, (row0, col0) in enumerate(anchors):
            row0 = row0 - 2
            inside = (row0 > -WIDE) & (row0 < rows)
            over = inside & ((col0 < 2) | (col0 > cols - REACH))
            low = jnp.where(col0 < 2, 0, cols + 2 - col0)
            high = jnp.where(col0 < 2, 2 - col0, WIDE)
            crossing.append((over, row0, col0, low, high))
            out_ref, at = target(j)
            out_ref[at] = part_ref[j]
        some = crossing[0][0]
        for over, *_ in crossing[1:]:
            some = some | over

        @pl.when(some)
        def _():
            for r in range(rows):
                if r not in outer:
                    expand(r)

        for j, (over, *where) in enumerate(crossing):
            out_ref, at = target(j)

            @pl.when(over)
            def _(out_ref=out_ref, at=at, where=where):
                for t in range(TILES):
                    out_ref[at, :, t * LANES : (t + 1) * LANES] += window_tile(
                        ext, t, *where, rows, padded
                    )

    one = like((1, padded, TILES * LANES))
    rest = like((max(bands // 2 - 1, 1), padded, TILES * LANES))
    edge = like((2, deep, cols + LANES))
    return run(
        body,
        [one, rest, one, rest, edge, edge],
        [anchor, parts, turned, right, left],
        [pltpu.VMEM((rows, deep, LANES), HALF)],
        micros=1.5
    )


def product(view, weight):
    return lax.dot_general(
        view, weight, (((1,), (1,)), ((), ())), preferred_element_type=FULL
    )


def gather_pairs(shifted, first, count):
    view = jnp.concatenate(
        [shifted[b, pl.ds(first + u, count), v] for u in (0, 1) for v in (0, 1) for b in (0, 1, 2)],
        axis=-1,
    )
    return view.reshape(count * view.shape[1], view.shape[2])


def silu(value):
    return value / (1.0 + jnp.exp(-value))


def patch_step(anchor, addends, noise, weights, biases, step_bias, sects, limits):
    padded = addends[0].shape[1]
    steps = noise.shape[0]
    half = SIDE // 2
    loose = 48

    def body(*refs):
        at_ref, parts = refs[0], refs[1 : 1 + len(addends)]
        band, sect = here()
        mine = lane_index(at_ref.shape) == band * sects + sect
        at = jnp.sum(jnp.where(mine, at_ref[...], 0).astype(FULL), axis=1, keepdims=True)
        row0, col0 = at.astype(jnp.int32)[0:1][None], at.astype(jnp.int32)[1:2][None]
        (noise_ref, w_in, w_out, d_in, d_out, b_in, b_out, b_step, b_den, out_ref,
         flat, state_sh, hid, hid_sh, pad, pad_sh, corr, state) = refs[1 + len(addends) :]
        for t in range(TILES):
            lanes = slice(t * LANES, (t + 1) * LANES)
            tile = parts[0][0, :, lanes].astype(FULL)
            for part in parts[1:]:
                tile = tile + part[0, :, lanes].astype(FULL)
            tile = jnp.concatenate([tile, jnp.zeros((LANES - padded, LANES), FULL)], axis=0)
            flat[lanes, :] = tile.T
        for i in range(WIDE):
            pair, k = divmod(i, PER_PAIR)
            off = pair * 2 * LANES + k * WIDE
            for b in range(3):
                state_sh[b, i // 2, i % 2] = flat[off + b : off + b + loose, :].astype(HALF)
        pairs = half + 1
        value = product(gather_pairs(state_sh, 0, pairs), w_in[...])
        value = silu(value + b_in[...]).reshape(pairs, loose, 2 * LANES)
        pair = lax.broadcasted_iota(jnp.int32, value.shape, 0)
        col = lax.broadcasted_iota(jnp.int32, value.shape, 1)
        odd = (lane_index(value.shape) >= LANES).astype(jnp.int32)
        grid_row = row0 - 1 + 2 * pair + odd
        grid_col = col0 - 1 + col
        keep = (
            (grid_row >= 0) & (grid_row < limits[0])
            & (grid_col >= 0) & (grid_col < limits[1]) & (col < SIDE + 2)
        )
        value = jnp.where(keep, value, 0.0)
        hid[:, 0] = value[:, :, :LANES]
        hid[:, 1] = value[:, :, LANES:]
        for b in range(3):
            hid_sh[b] = hid[:, :, b : b + SIDE, :].astype(HALF)
        value = product(gather_pairs(hid_sh, 0, half), w_out[...])
        center = jnp.concatenate(
            [state_sh[2, 1 : 1 + half, v, :SIDE, :] for v in (0, 1)], axis=-1
        ).astype(FULL).reshape(half * SIDE, 2 * LANES)
        mean = (center + value + b_out[...]).astype(HALF).astype(FULL)
        state[...] = mean + noise_ref[0].astype(FULL)
        pad[...] = jnp.zeros(pad.shape, FULL)
        deal = half // CHUNKS
        trips = jnp.where(band >= 0, CHUNKS, 0)

        def fill(source, first, count):
            shaped = source.reshape(count, SIDE, 2 * LANES)
            pad[pl.ds(first, count), 1, 8 : 8 + SIDE] = shaped[:, :, :LANES]
            pad[pl.ds(first + 1, count), 0, 8 : 8 + SIDE] = shaped[:, :, LANES:]

        def shift():
            for b in range(3):
                pad_sh[b] = pad[:, :, 7 + b : 7 + b + SIDE, :].astype(HALF)

        for step in range(steps):
            fill(state[...], 0, half)
            shift()

            def first(c, carry, step=step):
                value = product(gather_pairs(pad_sh, c * deal, deal), d_in[...])
                fill(silu(value + b_step[step : step + 1]), c * deal, deal)
                return carry

            lax.fori_loop(0, trips, first, 0)
            shift()

            def second(c, carry, step=step):
                value = product(gather_pairs(pad_sh, c * deal, deal), d_out[...])
                cells = pl.ds(pl.multiple_of(c * deal * SIDE, deal * SIDE), deal * SIDE)
                value = state[cells] - 0.5 * (value + b_den[...])
                if step + 1 < steps:
                    value = value + 0.5 * noise_ref[step + 1, cells].astype(FULL)
                state[cells] = value
                return carry

            lax.fori_loop(0, trips, second, 0)
        change = (state[...] - mean).reshape(half, SIDE, 2 * LANES)
        corr[:, 0] = change[:, :, :LANES]
        corr[:, 1] = change[:, :, LANES:]
        cells = corr[...].reshape(SIDE * SIDE, LANES)
        for t in range(SIDE * SIDE // LANES):
            lanes = slice(t * LANES, (t + 1) * LANES)
            out_ref[:, lanes] = cells[lanes].T[:padded].astype(HALF)

    return run(
        body,
        [like((padded, SIDE * SIDE))],
        [anchor, *addends, noise, *weights, *biases[:2], step_bias, biases[2]],
        [
            pltpu.VMEM((TILES * LANES, LANES), FULL),
            pltpu.VMEM((3, WIDE // 2, 2, loose, LANES), HALF),
            pltpu.VMEM((half + 1, 2, loose, LANES), FULL),
            pltpu.VMEM((3, half + 1, 2, SIDE, LANES), HALF),
            pltpu.VMEM((half + 1, 2, loose, LANES), FULL),
            pltpu.VMEM((3, half + 1, 2, SIDE, LANES), HALF),
            pltpu.VMEM((half, 2, SIDE, LANES), FULL),
            pltpu.VMEM((half * SIDE, 2 * LANES), FULL),
        ],
        micros=8.0
    )[0]


def spread(turned, right, left):
    rows, _, cols = turned.shape
    span = right.shape[1]
    loose = cols + 16

    def body(rows_ref, right_ref, left_ref, out_ref, after, before, line):
        def upright(value):
            value = value.astype(FULL)
            return jnp.concatenate(
                [value, jnp.zeros((LANES - value.shape[0], value.shape[1]), FULL)], axis=0
            ).T

        for t in range(span // LANES):
            lanes = slice(t * LANES, (t + 1) * LANES)
            after[lanes] = upright(right_ref[:, lanes])
        before[...] = upright(left_ref[...])
        line[...] = jnp.zeros(line.shape, FULL)

        def spread_rows(i, carry):
            for v in range(2):
                r = 2 * i + v
                line[v, 8 : 8 + cols] = upright(rows_ref[r])
                line[v, 8 + cols : 10 + cols] = after[pl.ds(r * REACH, 2)]
                line[v, 6:8] = before[pl.ds(2 * r, 2)]
                for b in range(3):
                    out_ref[b, i, v] = line[v, 6 + b : 6 + b + loose, :].astype(HALF)
            return carry

        lax.fori_loop(0, rows // 2, spread_rows, 0)

    return run(
        body,
        [like((3, rows // 2, 2, loose, LANES))],
        [turned, right, left],
        [
            pltpu.VMEM((span, LANES), FULL),
            pltpu.VMEM((LANES, LANES), FULL),
            pltpu.VMEM((2, loose + 8, LANES), FULL),
        ],
        micros=2.5
    )[0]


def grid_mean(shifted, near, cross, lower, padded, weights, biases, limits):
    rows = 2 * shifted.shape[1]
    _, deep, width = near.shape
    cols = width - LANES
    loose = cols + 16
    made = rows // 2
    pairs_in, pairs_out = made // 4 + 1, made // 4
    hidden_pairs = made // 2 + 1
    if hidden_pairs % pairs_in:
        hidden_pairs += pairs_in - hidden_pairs % pairs_in
    state_pairs = hidden_pairs + 1
    base = rows - made - 2 if lower else -2

    def body(shifted_ref, near_ref, cross_ref, w_in, w_out, b_in, b_out, out_ref,
             line, state_sh, hid, hid_sh):
        band, sect = here()
        row0 = band * rows + base + 1
        col0 = sect * cols - 1

        for pair in range(made // 2 + 2, state_pairs):
            for b in range(3):
                state_sh[b, pair] = jnp.zeros((2, loose, LANES), HALF)
        edge = made // 2 + 1 if lower else 0
        skip = 0 if lower else 1
        given = made // 2 + 1
        at = (rows - made) // 2 - 1 if lower else 0
        for b in range(3):
            state_sh[b, skip : skip + given] = shifted_ref[b, at : at + given]
        pair = jnp.bitwise_and(band, 1) == (0 if lower else 1)
        beyond = band == (limits[0] // rows - 1 if lower else 0)
        none = jnp.zeros((deep, width), HALF)
        for v in range(2):
            rim = jnp.where(beyond, none, jnp.where(pair, near_ref[v], cross_ref[v]))
            value = jnp.concatenate(
                [rim.astype(FULL), jnp.zeros((LANES - deep, width), FULL)], axis=0
            ).T
            line[v, 8 : 8 + cols] = value[:cols]
            line[v, 8 + cols :] = value[cols : cols + 16]
            line[v, :8] = value[width - 8 :]
            for b in range(3):
                state_sh[b, edge, v] = line[v, 6 + b : 6 + b + loose, :].astype(HALF)

        def first(chunk, carry):
            start = chunk * pairs_in
            value = product(gather_pairs(state_sh, start, pairs_in), w_in[...])
            value = silu(value + b_in[...]).reshape(pairs_in, loose, 2 * LANES)
            pair = lax.broadcasted_iota(jnp.int32, value.shape, 0)
            col = lax.broadcasted_iota(jnp.int32, value.shape, 1)
            odd = (lane_index(value.shape) >= LANES).astype(jnp.int32)
            grid_row = row0 + 2 * (start + pair) + odd
            grid_col = col0 + col
            keep = (
                (grid_row >= 0) & (grid_row < limits[0])
                & (grid_col >= 0) & (grid_col < limits[1])
            )
            value = jnp.where(keep, value, 0.0)
            hid[:, 0] = value[:, :, :LANES]
            hid[:, 1] = value[:, :, LANES:]
            for b in range(3):
                hid_sh[b, pl.ds(start, pairs_in)] = hid[:, :, b : b + cols, :].astype(HALF)
            return carry

        lax.fori_loop(0, hidden_pairs // pairs_in, first, 0)

        def second(chunk, carry):
            start = chunk * pairs_out
            value = product(gather_pairs(hid_sh, start, pairs_out), w_out[...]) + b_out[...]
            value = value.reshape(pairs_out, cols, 2 * LANES)
            for k in range(pairs_out):
                for v in range(2):
                    center = state_sh[2, start + k + 1, v, :cols, :].astype(FULL)
                    mean = center + value[k, :, v * LANES : (v + 1) * LANES]
                    out_ref[2 * (start + k) + v] = mean.T[:padded].astype(HALF)
            return carry

        lax.fori_loop(0, made // 2 // pairs_out, second, 0)

    return run(
        body,
        [like((made, padded, cols))],
        [shifted, near, cross, *weights, *biases],
        [
            pltpu.VMEM((2, loose + 8, LANES), FULL),
            pltpu.VMEM((3, state_pairs, 2, loose, LANES), HALF),
            pltpu.VMEM((pairs_in, 2, loose, LANES), FULL),
            pltpu.VMEM((3, hidden_pairs, 2, cols, LANES), HALF),
        ],
        micros=3.5,
    )[0]


def fill_view(view, at_ref, pieces, sources, sects, rows, cols):
    padded = pieces[0].shape[-2]
    tile_rows = view.shape[0]
    none = jnp.zeros((padded, LANES), HALF)
    anchors = slot_anchors(at_ref, sources, sects, rows, cols)
    for at, (piece, (row0, _)) in enumerate(zip(pieces, anchors)):
        lanes = slice(at * LANES, (at + 1) * LANES)
        for r in range(rows):
            i = r - row0
            tile = jnp.clip(
                jnp.right_shift(i, tile_rows.bit_length() - 1), 0, SIDE // tile_rows - 1
            )
            value = piece[:, pl.ds(pl.multiple_of(tile * LANES, LANES), LANES)]
            inside = (i >= 0) & (i < SIDE)
            view[r % tile_rows, r // tile_rows, :padded, lanes] = jnp.where(inside, value, none)
    view[:, :, padded:, :] = jnp.zeros(
        view.shape[:2] + (view.shape[2] - padded, view.shape[3]), HALF
    )


def view_shape(pieces, rows):
    tile_rows = LANES // SIDE
    deep = -(-pieces[0].shape[-2] // 16) * 16
    return (tile_rows, rows // tile_rows, deep, len(pieces) * LANES)


def gather_view(anchor, pieces, sources, sects, rows, cols):
    def body(at_ref, *refs):
        fill_view(refs[-1], at_ref, refs[:-1], sources, sects, rows, cols)

    shape = view_shape(pieces, rows)
    return run(body, [like(shape)], [anchor, *pieces], [], micros=0.8)[0]


def canvas(anchor, early, pieces, sources, place, sects, rows, cols):
    padded = pieces[0].shape[-2]
    deep = -(-padded // 16) * 16
    total = anchor.shape[1]
    slots = len(pieces)
    tile_rows = LANES // SIDE
    groups = rows // tile_rows

    def body(at_ref, *refs):
        band, sect = here()
        early_ref, place_ref, spill_ref, out_ref, inverse_ref, view = refs[slots:]
        fill_view(view, at_ref, refs[:slots], sources, sects, rows, cols)
        spilled = None
        for m in range(tile_rows):
            both = jnp.concatenate([early_ref[m], view[m]], axis=-1)
            value = jnp.dot(
                both.reshape(groups * deep, both.shape[-1]), place_ref[m],
                preferred_element_type=FULL,
            ).reshape(groups, deep, 2 * LANES)
            for k in range(groups):
                out_ref[k * tile_rows + m] = value[k, :padded, :LANES]
            part = value[:, :padded, LANES:]
            spilled = part if spilled is None else spilled + part
        for k in range(groups):
            spill_ref[:, k * LANES : (k + 1) * LANES] = spilled[k].astype(HALF)
        tall, wide = (rows, total), (total, cols)
        down = lax.broadcasted_iota(jnp.int32, tall, 0) + band * rows - at_ref[0:1, :]
        across = lane_index(wide) + sect * cols - at_ref[1:2, :].astype(FULL).T.astype(jnp.int32)
        down = jnp.where((down >= 0) & (down < SIDE), 1.0, 0.0)
        across = jnp.where((across >= 0) & (across < SIDE), 1.0, 0.0)
        count = jnp.dot(down.astype(HALF), across.astype(HALF), preferred_element_type=FULL)
        inverse_ref[...] = 1.0 / jnp.maximum(count, 1.0)

    return run(
        body,
        [
            like((padded, rows * SIDE)),
            like((rows, padded, cols), FULL),
            like((rows, cols), FULL),
        ],
        [anchor, *pieces, early, place],
        [pltpu.VMEM(view_shape(pieces, rows), HALF)],
        micros=1.5
    )


def finish(means, summed, arrived, inverse, channels):
    rows, padded, cols = summed.shape
    deep = -(-padded // 16) * 16
    half = means[0].shape[0]
    chunk = 8

    def body(top_ref, low_ref, sum_ref, spill_ref, inverse_ref, out_ref, flat, ready, sems):
        lane = lane_index((padded, LANES))
        none = jnp.zeros((padded, LANES), HALF)
        flat[:, padded:] = jnp.zeros((chunk, deep - padded, cols), HALF)
        copies = []
        for first in range(0, rows, chunk):
            for r in range(first, first + chunk):
                at, low = divmod(r * SIDE, LANES)
                extra = spill_ref[:, at * LANES : (at + 1) * LANES]
                if low:
                    extra = pltpu.roll(extra, LANES - low, 1)
                extra = jnp.where(lane < SIDE, extra, none).astype(FULL)
                mean = top_ref[r] if r < half else low_ref[r - half]
                value = mean.astype(FULL) + (sum_ref[r] + extra) * inverse_ref[r : r + 1]
                flat[r - first, :padded] = value.astype(HALF)
            k = first // chunk
            ready[k] = jnp.swapaxes(flat[...], 0, 1)[:channels]
            copies.append(
                pltpu.make_async_copy(
                    ready.at[k], out_ref.at[:, pl.ds(first, chunk), :], sems.at[k]
                )
            )
            copies[-1].start()
        for copy in copies:
            copy.wait()

    return run(
        body,
        [like((channels, rows, cols))],
        [*means, summed, arrived, inverse],
        [
            pltpu.VMEM((chunk, deep, cols), HALF),
            pltpu.VMEM((rows // chunk, channels, chunk, cols), HALF),
            pltpu.SemaphoreType.DMA((rows // chunk,)),
        ],
        micros=2.0,
        out_space=pltpu.HBM,
    )[0]


def step(
    state_field,
    conv_in_weight,
    conv_in_bias,
    conv_out_weight,
    conv_out_bias,
    patch_anchor,
    patch_noise,
    denoise_in_weight,
    step_bias,
    denoise_out_weight,
    denoise_bias,
):
    bands = lax.axis_size("band")
    sects = lax.axis_size("sect")
    channels, rows, cols = state_field.shape
    limits = (rows * bands, cols * sects)

    anchor = patch_anchor.T

    right_rim, turned = pack(state_field)
    padded = right_rim.shape[0]
    left_rim = pack_left(turned, padded)
    right = shift_from(right_rim, "sect", -1)
    left = shift_from(left_rim, "sect", 1)

    made, lines, noise, place = prep(
        anchor,
        [
            conv_in_weight.transpose(0, 2, 1),
            conv_out_weight,
            denoise_in_weight.transpose(0, 2, 1),
            denoise_out_weight,
        ],
        [conv_in_bias[None, :], conv_out_bias[None, :], denoise_bias[None, :], step_bias],
        patch_noise[0],
        bands,
        sects,
        rows,
        cols,
    )
    biases, step_lines = lines[:3], lines[3]

    padded = right_rim.shape[0]
    parts = extract_own(anchor, turned, padded, bands, sects)
    own, kept, own_sent, sent, edge_near, edge_cross = extract_rim(
        anchor, parts, turned, right, left, bands, sects
    )
    addends = [own]
    if bands > 2:
        got = swap(sent, "band", 1)
        kept = add_parts(kept, got)
    bit = 2
    while bit < bands:
        got = swap(kept[0::2], "band", bit)
        addends.append(got)
        kept = kept[1::2] + got[1:]
        bit *= 2
    addends.append(swap(own_sent, "band", 1))
    rim_near = swap(edge_near, "band", 1)
    steps = [(i, i + 1) for i in range(1, bands - 1, 2)]
    alone = [(i, i) for i in range(bands) if all(i not in step for step in steps)]
    rim_cross = lax.ppermute(edge_cross, "band", steps + [(j, i) for i, j in steps] + alone)
    correction = patch_step(
        anchor, addends, noise, made, biases, step_lines, sects, limits
    )
    pieces = [correction]
    sources = arrival(bands)
    bit = bands // 2
    while bit:
        fresh = []
        for piece in pieces:
            fresh.append(swap(piece, "band", bit))
        pieces += fresh
        bit //= 2

    shifted = spread(turned, right, left)
    top_mean = grid_mean(shifted, rim_near, rim_cross, False, padded, made[:2], biases[:2], limits)
    low_mean = grid_mean(shifted, rim_near, rim_cross, True, padded, made[:2], biases[:2], limits)
    early = gather_view(anchor, pieces[:-1], sources[:-1], sects, rows, cols)
    spilled, summed, inverse = canvas(
        anchor, early, pieces[-1:], sources[-1:], place, sects, rows, cols
    )
    arrived = shift_from(spilled, "sect", 1)
    return finish([top_mean, low_mean], summed, arrived, inverse, channels)


def solution(mesh):
    placed = (
        P("groups", "band", "sect"),
        P(),
        P(),
        P(),
        P(),
        P("groups", None),
        P(("groups", "band", "sect"), None, None, None),
        P(),
        P(),
        P(),
        P(),
    )
    return jax.shard_map(
        step,
        mesh=mesh,
        in_specs=placed,
        out_specs=P("groups", "band", "sect"),
        check_vma=False,
    )
```
